32 devices in a mesh: section: 4 (over y, x), coil: 2 (over core), space: 4 (over z).
Axes of the slice: x: 2, y: 2, z: 4, core: 2. Of those that a mesh axis runs over, the one named last changes fastest.
Arguments:
- image: float32 [4, 2, 2, 256, 256], P(None, None, 'coil', 'space'), may hold values from -6 to 6
- sens: bfloat16 [4, 2, 2, 256, 512], P('coil', None, None, 'space'), may hold values from -2 to 2
- adjoint: float32 [4, 2, 2, 256, 256], P(None, None, 'coil', 'space'), may hold values from -6 to 6
- mask_bits: int32 [2, 256, 9], replicated, may hold values from 0 to 1073741823, as said below
- step_size: float32 [4], P('section'), may hold values from 0.3 to 1
- conv1_w: bfloat16 [4, 32, 108], P('section'), may hold values from -0.625 to 0.625
- conv1_b: float32 [4, 32], P('section'), may hold values from -1 to 1
- conv2_w: bfloat16 [4, 32, 108], P('section'), may hold values from -0.125 to 0.125
Outputs:
- cascade_images: float32 [4, 4, 2, 2, 256, 256], P('section', None, None, 'coil', 'space')
The draws below stay inside these ranges and needn't reach their ends.
Inputs may be any that keep to these rules, and one draw needn't show every extreme that they name: `mask_bits`: bit b of word w in row (p, ky) is 1 where k-space point (ky, 30 w + b) is sampled in phase p; bits for points at or beyond 256 are 0.
All inputs are finite; a program needn't handle non-finite values.
Results may differ from the reference program's by a relative error of at most 0.01.
Values may be sent and summed in bfloat16 or wider, within the bound.
No kernel may reach another device: no remote copies, remote signals or barrier semaphores. Data moves between devices by JAX's collectives and lax.ppermute only.
A program may use at most 128 MiB of HBM per device.

```python
import math
import jax
import jax.numpy as jnp
from jax import lax

NY = 256
NZ = 256
CH = 32
PH = 2
SLABS = 2
MB = 2
COILS = 4
NZW = 9
CASC = 4
N_SECTION = 4


def draw_mask_bits(key, part):
    row_k = jnp.arange(NY, dtype=jnp.int32)
    column_k = jnp.arange(NZW * 30, dtype=jnp.int32)
    dist_y = jnp.minimum(row_k, NY - row_k) * 64 // (NY // 2)
    dist_z = jnp.minimum(column_k, jnp.maximum(NZ - column_k, 0)) * 64 // (NZ // 2)
    radius = jnp.maximum(dist_y[:, None], dist_z[None, :])
    thresh = 40 - radius * 32 // 64
    samples = jax.random.randint(key, (PH, NY, NZW * 30), 0, 64)
    sampled = (samples < thresh[None]) | (radius[None] < 8)
    sampled = sampled & (column_k[None, None, :] < NZ)
    weights = jnp.left_shift(jnp.ones((30,), jnp.int32), jnp.arange(30, dtype=jnp.int32))
    packed = jnp.sum(sampled.astype(jnp.int32).reshape(PH, NY, NZW, 30) * weights, axis=3)
    return packed.astype(jnp.int32)


def level_of(own_key, dims, shards, smallest, largest):
    factor_of = 1.0
    for axis_at, shards_of in shards:
        draws = jax.random.uniform(jax.random.fold_in(jax.random.fold_in(own_key, 6), axis_at), (shards_of,), jnp.float32, smallest / len(shards), largest / len(shards))
        factor_of = factor_of * jnp.repeat(jnp.exp(draws), dims[axis_at] // shards_of).reshape((-1,) + (1,) * (len(dims) - 1 - axis_at))
    return factor_of


def normal_values(own_key, extent, spread, most, cuts=(), held_as=jnp.bfloat16):
    gain = level_of(own_key, extent, cuts, -0.22, 0.18) if cuts else 1.0
    entries = jax.random.normal(own_key, extent, jnp.float32) * spread * gain
    return jnp.minimum(jnp.maximum(entries, -most), most).astype(held_as)


def setup_inputs(seed: int = 0) -> dict:
    keys = jax.random.split(jax.random.key(seed), 9)
    image = normal_values(keys[0], (2 * PH, SLABS, MB, NY, NZ), 1.0, 6.0, ((2, 2), (3, 4)), jnp.float32)
    sens = normal_values(keys[1], (COILS, SLABS, MB, NY, 2 * NZ), ((2 * COILS) ** -0.5), 2.0, ((0, 2), (3, 4)))
    adjoint = normal_values(keys[2], (2 * PH, SLABS, MB, NY, NZ), 1.0, 6.0, ((2, 2), (3, 4)), jnp.float32)
    mask_bits = draw_mask_bits(jax.random.fold_in(keys[8], 71), 0)
    step_size = jnp.clip(jnp.exp(math.log(1.0) - 1.2039728 * jax.random.uniform(keys[4], (CASC,), jnp.float32) ** level_of(keys[4], (CASC,), ((0, 4),), -0.2, 0.2)), 0.3, 1.0)
    conv1_w = normal_values(keys[5], (CASC, CH, 54 * PH), (54 * PH) ** -0.5, 0.625, ((0, 4),))
    conv1_b = jnp.clip(jax.random.uniform(keys[6], (CASC, CH), jnp.float32, -1.0, 1.0) * level_of(keys[6], (CASC, CH), ((0, 4),), -0.4, 0.0), -1.0, 1.0)
    conv2_w = normal_values(keys[7], (CASC, CH, 54 * PH), (0.7 * (27 * CH) ** -0.5), 0.125, ((0, 4),))
    return dict(image=image, sens=sens, adjoint=adjoint, mask_bits=mask_bits, step_size=step_size, conv1_w=conv1_w, conv1_b=conv1_b, conv2_w=conv2_w)


def dft_tables(length):
    index = jnp.arange(length, dtype=jnp.int32)
    product = index[:, None] * index[None, :] % length
    angle = product.astype(jnp.float32) * (2.0 * math.pi / length)
    scale = 1.0 / math.sqrt(length)
    return ((jnp.cos(angle) * scale).astype(jnp.bfloat16), (jnp.sin(angle) * scale).astype(jnp.bfloat16))

def unpack_mask(mask_bits, length_z):
    column = jnp.arange(length_z, dtype=jnp.int32)
    word_count = mask_bits.shape[2]
    select = (column[:, None] // 30 == jnp.arange(word_count, dtype=jnp.int32)[None, :]).astype(jnp.int32)
    chosen = lax.optimization_barrier(jnp.sum(mask_bits[:, :, None, :] * select[None, None], axis=3))
    return (jnp.right_shift(chosen, column % 30) & 1).astype(jnp.float32)

def mult_last(values, table):
    return jnp.einsum('...n,nk->...k', values.astype(jnp.float32), table.astype(jnp.float32), precision=lax.Precision.HIGHEST)

def mult_rows(values, table):
    return jnp.einsum('kn,...nz->...kz', table.astype(jnp.float32), values.astype(jnp.float32), precision=lax.Precision.HIGHEST)

def along_last(real_part, imag_part, cos_table, sin_table, direction):
    first = mult_last(real_part, cos_table) + direction * mult_last(imag_part, sin_table)
    second = mult_last(imag_part, cos_table) - direction * mult_last(real_part, sin_table)
    return (first, second)

def along_rows(real_part, imag_part, cos_table, sin_table, direction):
    first = mult_rows(real_part, cos_table) + direction * mult_rows(imag_part, sin_table)
    second = mult_rows(imag_part, cos_table) - direction * mult_rows(real_part, sin_table)
    return (first, second)

def to_half(values):
    return values.astype(jnp.bfloat16)

def correlate(source, kernel):
    return lax.conv_general_dilated(source, kernel, (1, 1, 1), 'SAME', dimension_numbers=('NCDHW', 'OIDHW', 'NCDHW'), precision=lax.Precision.HIGHEST)

def reference(image, sens, adjoint, mask_bits, step_size, conv1_w, conv1_b, conv2_w):
    sampled = unpack_mask(mask_bits, NZ)[:, None, None]
    cos_z, sin_z = dft_tables(NZ)
    cos_y, sin_y = dft_tables(NY)
    adjoint_c = adjoint.reshape(PH, 2, SLABS, MB, NY, NZ)
    current_x = image
    results = []
    for cascade in range(N_SECTION):
        current = current_x.reshape(PH, 2, SLABS, MB, NY, NZ)
        rounded = to_half(current).astype(jnp.float32)
        image_re = rounded[:, 0]
        image_im = rounded[:, 1]

        def coil_step(totals, coil_map):
            coil_maps = coil_map.reshape(SLABS, MB, NY, 2, NZ).astype(jnp.float32)
            map_re = coil_maps[:, :, :, 0]
            map_im = coil_maps[:, :, :, 1]
            coil_re = to_half(map_re * image_re - map_im * image_im)
            coil_im = to_half(map_re * image_im + map_im * image_re)
            fwd_re, fwd_im = along_last(coil_re, coil_im, cos_z, sin_z, 1.0)
            spec_re, spec_im = along_rows(to_half(fwd_re), to_half(fwd_im), cos_y, sin_y, 1.0)
            spec_re = to_half(spec_re * sampled)
            spec_im = to_half(spec_im * sampled)
            inv_re, inv_im = along_rows(spec_re, spec_im, cos_y, sin_y, -1.0)
            out_re, out_im = along_last(to_half(inv_re), to_half(inv_im), cos_z, sin_z, -1.0)
            back_re = to_half(out_re).astype(jnp.float32)
            back_im = to_half(out_im).astype(jnp.float32)
            total_re = totals[0] + map_re * back_re + map_im * back_im
            total_im = totals[1] + map_re * back_im - map_im * back_re
            return ((total_re, total_im), None)
        empty_acc = jnp.zeros((PH, SLABS, MB, NY, NZ), jnp.float32)
        (grad_re, grad_im), unused = lax.scan(coil_step, (empty_acc, empty_acc), sens)
        gradient = jnp.stack([grad_re, grad_im], axis=1) - adjoint_c
        updated = current - step_size[cascade] * gradient
        updated = updated.reshape(2 * PH, SLABS, MB, NY, NZ)
        lifted = to_half(updated).astype(jnp.float32).transpose(1, 0, 2, 3, 4)
        first_w = conv1_w[cascade].astype(jnp.float32).reshape(CH, 3, 3, 3, 2 * PH).transpose(0, 4, 1, 2, 3)
        hidden = correlate(lifted, first_w) + conv1_b[cascade][None, :, None, None, None]
        hidden = to_half(jnp.maximum(hidden, 0.0)).astype(jnp.float32)
        second_w = conv2_w[cascade].astype(jnp.float32).reshape(CH, 3, 3, 3, 2 * PH).transpose(4, 0, 1, 2, 3)
        refine = correlate(hidden, second_w).transpose(1, 0, 2, 3, 4)
        current_x = updated + refine
        results.append(current_x)
    return jnp.stack(results)
```

```python
import functools
import math

import jax
import jax.numpy as jnp
from jax import lax
from jax.experimental import pallas as pl
from jax.experimental.pallas import tpu as pltpu
from jax.sharding import Mesh
from jax.sharding import PartitionSpec as P

BF = jnp.bfloat16
F32 = jnp.float32
ROWS = 8
LANES = 128


def dft_tables(length):
    index = jnp.arange(length, dtype=jnp.int32)
    product = index[:, None] * index[None, :] % length
    angle = product.astype(F32) * (2.0 * math.pi / length)
    scale = 1.0 / math.sqrt(length)
    return (jnp.cos(angle) * scale).astype(BF), (jnp.sin(angle) * scale).astype(BF)


def block_tables(length):
    cos, sin = dft_tables(length)
    first = jnp.concatenate(
        [jnp.concatenate([cos, -sin], axis=1), jnp.concatenate([sin, cos], axis=1)], axis=0
    )
    second = jnp.concatenate(
        [jnp.concatenate([cos, sin], axis=1), jnp.concatenate([-sin, cos], axis=1)], axis=0
    )
    return first, second


def unpack_mask(mask_bits, length_z):
    column = jnp.arange(length_z, dtype=jnp.int32)
    word_count = mask_bits.shape[2]
    select = (column[:, None] // 30 == jnp.arange(word_count, dtype=jnp.int32)[None, :]).astype(
        jnp.int32
    )
    chosen = jnp.sum(mask_bits[:, :, None, :] * select[None, None], axis=3)
    return (jnp.right_shift(chosen, column % 30) & 1).astype(F32)


def dot(left, right):
    return jnp.dot(left, right, preferred_element_type=F32)


def shifted_lanes(values, step):
    length = values.shape[1]
    lane = lax.broadcasted_iota(jnp.int32, values.shape, 1)
    if step > 0:
        return jnp.where(lane == 0, 0.0, pltpu.roll(values, 1, 1))
    return jnp.where(lane == length - 1, 0.0, pltpu.roll(values, length - 1, 1))


def consistency_kernel(
    phases,
    neighbours,
    step_ref,
    base_ref,
    *refs,
):
    part_refs = refs[:neighbours]
    (
        sens_ref,
        adjoint_ref,
        mask_ref,
        first_z,
        second_z,
        first_y,
        second_y,
        x_ref,
        dc_ref,
        v_ref,
        total,
    ) = refs[neighbours:]
    channels, length_y, length_z = base_ref.shape
    for channel in range(channels):
        value = base_ref[channel].astype(F32)
        for part in part_refs:
            value = value + part[channel].astype(F32)
        x_ref[channel] = value
        total[channel] = -adjoint_ref[channel].astype(F32)

    def coil(index, carry):
        maps = sens_ref[index].astype(F32)
        map_re, map_im = maps[:, :length_z], maps[:, length_z:]
        for phase in range(phases):
            image_re = x_ref[2 * phase].astype(BF).astype(F32)
            image_im = x_ref[2 * phase + 1].astype(BF).astype(F32)
            coil_img = jnp.concatenate(
                [
                    (map_re * image_re - map_im * image_im).astype(BF),
                    (map_re * image_im + map_im * image_re).astype(BF),
                ],
                axis=1,
            )
            kz = dot(coil_img, first_z[...]).astype(BF)
            kz = jnp.concatenate([kz[:, :length_z], kz[:, length_z:]], axis=0)
            spectrum = dot(second_y[...], kz)
            keep = mask_ref[phase]
            spectrum = jnp.concatenate(
                [
                    (spectrum[:length_y] * keep).astype(BF),
                    (spectrum[length_y:] * keep).astype(BF),
                ],
                axis=0,
            )
            back_y = dot(first_y[...], spectrum).astype(BF)
            back_y = jnp.concatenate([back_y[:length_y], back_y[length_y:]], axis=1)
            back = dot(back_y, second_z[...])
            back_re, back_im = back[:, :length_z], back[:, length_z:]
            total[2 * phase] += map_re * back_re + map_im * back_im
            total[2 * phase + 1] += map_re * back_im - map_im * back_re
        return carry

    lax.fori_loop(0, sens_ref.shape[0], coil, 0)
    for channel in range(channels):
        value = x_ref[channel] - step_ref[0] * total[channel]
        dc_ref[channel] = value
        v_ref[channel] = value.astype(BF)


def refine_kernel(
    neighbours,
    width,
    v_ref,
    *refs,
):
    other_refs = refs[:neighbours]
    dc_ref, w1_ref, b1_ref, w2_ref, base_ref = refs[neighbours : neighbours + 5]
    send_refs = refs[neighbours + 5 : 2 * neighbours + 5]
    mixed, hidden = refs[2 * neighbours + 5 :]
    channels, length_y, length_z = v_ref.shape
    tiles, mixed_rows, lanes = mixed.shape
    per_row = mixed_rows // (length_y + 2)
    for tile in range(tiles):
        mixed[tile, 0:per_row, :] = jnp.zeros((per_row, lanes), F32)
        mixed[tile, (length_y + 1) * per_row :, :] = jnp.zeros((per_row, lanes), F32)
    hidden[0:width, :] = jnp.zeros((width, length_z), BF)
    hidden[(length_y + 1) * width :, :] = jnp.zeros((width, length_z), BF)
    sources = [v_ref, *other_refs]
    for at in range(per_row):
        plane, channel = divmod(at, channels)
        if plane < len(sources):
            value = sources[plane][channel].astype(F32)
        else:
            value = jnp.zeros((length_y, length_z), F32)
        for tile in range(tiles):
            mixed[tile, pl.ds(per_row + at, length_y, stride=per_row), :] = value[
                :, tile * lanes : (tile + 1) * lanes
            ]

    def first(block, carry):
        for half in range(2):
            at = block * 2 + half
            start = pl.multiple_of(at * (ROWS * per_row), ROWS * per_row)
            window = jnp.concatenate(
                [mixed[tile, pl.ds(start, (ROWS + 2) * per_row), :] for tile in range(tiles)],
                axis=1,
            )
            taps = jnp.concatenate(
                [
                    shifted_lanes(window, 1).astype(BF),
                    window.astype(BF),
                    shifted_lanes(window, -1).astype(BF),
                ],
                axis=0,
            )
            value = dot(w1_ref[...], taps) + b1_ref[...]
            store = pl.multiple_of((at * ROWS + 1) * width, width)
            hidden[pl.ds(store, ROWS * width), :] = jnp.maximum(value, 0.0).astype(BF)
        return carry

    lax.fori_loop(0, length_y // (2 * ROWS), first, 0)
    block_rows = channels * ROWS

    def second(block, carry):
        results = []
        for half in range(2):
            at = block * 2 + half
            start = pl.multiple_of(at * (ROWS * width), ROWS * width)
            parts = dot(w2_ref[...], hidden[pl.ds(start, (ROWS + 2) * width), :])
            third = parts.shape[0] // 3
            results.append(
                shifted_lanes(parts[:third], 1)
                + parts[third : 2 * third]
                + shifted_lanes(parts[2 * third :], -1)
            )
        rows = pl.ds(pl.multiple_of(block * (2 * ROWS), 2 * ROWS), 2 * ROWS)
        for plane in range(neighbours + 1):
            for channel in range(channels):
                lo = plane * block_rows + channel * ROWS
                value = jnp.concatenate([piece[lo : lo + ROWS] for piece in results], axis=0)
                if plane == 0:
                    base_ref[channel, rows, :] = dc_ref[channel, rows, :] + value
                else:
                    send_refs[plane - 1][channel, rows, :] = value.astype(BF)
        return carry

    lax.fori_loop(0, length_y // (2 * ROWS), second, 0)


def gathered_rows(value, axis, dim):
    count = lax.axis_size(axis)
    index = lax.axis_index(axis)
    size = value.shape[dim]
    shape = list(value.shape)
    shape[dim] = size * count
    whole = jnp.zeros(shape, value.dtype)
    for step in range(count):
        block = value
        if step:
            block = lax.ppermute(value, axis, [(i, (i + step) % count) for i in range(count)])
        whole = lax.dynamic_update_slice_in_dim(
            whole, block, (index - step) % count * size, dim
        )
    return whole


def banded(base, rows):
    taps = base.shape[-2]
    window = rows + taps - 1
    pads = [(0, 0)] * (base.ndim - 2)
    return jnp.stack(
        [jnp.pad(base, (*pads, (row, window - taps - row), (0, 0))) for row in range(rows)], axis=0
    )


def per_device(image, sens, adjoint, mask_bits, step_size, conv1_w, conv1_b, conv2_w):
    channels, slab_count, _, row_count, length_z = image.shape
    phases, length_y = mask_bits.shape[:2]
    planes = lax.axis_size("coil")
    coil_local = sens.shape[0]
    width = conv1_w.shape[1]
    groups = lax.axis_size("group")
    members = lax.axis_size("member")
    cascades = groups * members
    group = lax.axis_index("group")
    member = lax.axis_index("member")
    plane = lax.axis_index("coil")
    section = group * members + member
    first_z, second_z = block_tables(length_z)
    first_y, second_y = (first_z, second_z) if length_y == length_z else block_tables(length_y)
    sampled = unpack_mask(mask_bits, length_z)

    packed = jnp.concatenate(
        [
            conv1_w.reshape(1, -1).astype(F32),
            conv2_w.reshape(1, -1).astype(F32),
            conv1_b.reshape(1, -1),
            step_size.reshape(1, 1),
        ],
        axis=1,
    )
    packed = gathered_rows(gathered_rows(packed, "member", 0), "group", 0)
    taps = conv1_w.shape[2]
    count_w = width * taps
    all_w1 = packed[:, :count_w].reshape(cascades, width, 3, 3, 3, channels)
    all_w2 = packed[:, count_w : 2 * count_w].reshape(cascades, width, 3, 3, 3, channels)
    all_b1 = packed[:, 2 * count_w : 2 * count_w + width]
    steps = packed[:, 2 * count_w + width]

    if planes == 1:
        sides = []
    elif planes == 2:
        sides = [None]
    else:
        sides = [-1, 1]
    neighbours = len(sides)
    involved = neighbours + 1
    per_row = -(-(involved * channels) // 8) * 8

    def tap_of(side, sign):
        if side is None:
            return jnp.where(plane == 0, 1 + sign, 1 - sign)
        return 1 + sign * side

    def weights_of(cascade):
        w1 = all_w1[cascade]
        w2 = all_w2[cascade]
        taken1 = [w1[:, 1]]
        taken2 = [w2[:, 1]]
        for side in sides:
            taken1.append(lax.dynamic_index_in_dim(w1, tap_of(side, 1), 1, keepdims=False))
            taken2.append(lax.dynamic_index_in_dim(w2, tap_of(side, -1), 1, keepdims=False))
        for _ in range(per_row // channels - involved):
            taken1.append(jnp.zeros_like(taken1[0]))
        base1 = jnp.stack(taken1, axis=3)
        base1 = base1.transpose(0, 2, 1, 3, 4).reshape(width, 3, 3, per_row)
        big1 = banded(base1, ROWS)
        big1 = big1.reshape(ROWS * width, 3 * (ROWS + 2) * per_row).astype(BF)
        base2 = jnp.stack(taken2, axis=0)
        base2 = base2.transpose(3, 0, 4, 2, 1)
        big2 = banded(base2, ROWS).transpose(1, 2, 3, 0, 4, 5)
        big2 = big2.reshape(3 * involved * channels * ROWS, (ROWS + 2) * width).astype(BF)
        bias = jnp.tile(all_b1[cascade], ROWS)[:, None]
        return big1, bias, big2

    maps = lax.dynamic_index_in_dim(sens, group, 1, keepdims=False)
    maps = lax.all_to_all(maps, "coil", split_axis=1, concat_axis=0, tiled=True)
    maps = gathered_rows(maps[:, 0], "space", 1)
    own_image = lax.dynamic_index_in_dim(image, group, 1, keepdims=False)[:, 0].astype(BF)
    own_adjoint = lax.dynamic_index_in_dim(adjoint, group, 1, keepdims=False)[:, 0].astype(BF)
    base = gathered_rows(own_image, "space", 1)
    target = gathered_rows(own_adjoint, "space", 1)

    full = jax.ShapeDtypeStruct((channels, length_y, length_z), F32)
    half = jax.ShapeDtypeStruct((channels, length_y, length_z), BF)
    vmem = pl.BlockSpec(memory_space=pltpu.VMEM)
    smem = pl.BlockSpec(memory_space=pltpu.SMEM)
    params = pltpu.CompilerParams(vmem_limit_bytes=56 * 1024 * 1024)

    def consistency(cascade, base, parts):
        return pl.pallas_call(
            functools.partial(consistency_kernel, phases, len(parts)),
            out_shape=(full, full, half),
            in_specs=[smem] + [vmem] * (8 + len(parts)),
            out_specs=(vmem, vmem, vmem),
            scratch_shapes=[pltpu.VMEM((channels, length_y, length_z), F32)],
            compiler_params=params,
        )(
            steps[cascade : cascade + 1],
            base,
            *parts,
            maps,
            target,
            sampled,
            first_z,
            second_z,
            first_y,
            second_y,
        )

    def refine(cascade, value, others, updated):
        big1, bias, big2 = weights_of(cascade)
        return pl.pallas_call(
            functools.partial(refine_kernel, neighbours, width),
            out_shape=(full,) + (half,) * neighbours,
            in_specs=[vmem] * (5 + neighbours),
            out_specs=(vmem,) * (1 + neighbours),
            scratch_shapes=[
                pltpu.VMEM((length_z // LANES, (length_y + 2) * per_row, LANES), F32),
                pltpu.VMEM(((length_y + 2) * width, length_z), BF),
            ],
            compiler_params=params,
        )(value, *others, updated, big1, bias, big2)

    def exchanged(values):
        received = []
        for value, side in zip(values, sides):
            if side is None:
                pairs = [(0, 1), (1, 0)]
            else:
                pairs = [(i, i - side) for i in range(planes) if 0 <= i - side < planes]
            received.append(lax.ppermute(value, "coil", pairs))
        return received

    row_start = lax.axis_index("space") * row_count

    def own_rows(value):
        return lax.dynamic_slice_in_dim(value, row_start, row_count, 1)

    results = []
    parts = []
    for cascade in range(cascades):
        current, updated, value = consistency(cascade, base, parts)
        if cascade:
            results.append(own_rows(current))
        others = exchanged([value] * neighbours)
        base, *sends = refine(cascade, value, others, updated)
        turned = sends[::-1] if neighbours == 2 else sends
        parts = exchanged(turned)[::-1] if neighbours == 2 else exchanged(turned)
    last = own_rows(base)
    for part in parts:
        last = last + own_rows(part).astype(F32)
    results.append(last)

    def result_of(wanted):
        chosen = results[0]
        for cascade in range(1, cascades):
            chosen = jnp.where(wanted == cascade, results[cascade], chosen)
        return chosen

    output = jnp.zeros((channels, slab_count, row_count, length_z), F32)
    for step in range(groups):
        if step == 0:
            chosen = result_of(section)
        else:
            target_group = (group - step) % groups
            chosen = result_of(target_group * members + member).astype(BF)
            chosen = lax.ppermute(
                chosen, "group", [(i, (i - step) % groups) for i in range(groups)]
            ).astype(F32)
        output = lax.dynamic_update_slice_in_dim(
            output, chosen[:, None], (group + step) % groups, 1
        )
    return output[None, :, :, None]


def solution(mesh):
    sections, coils, spaces = mesh.devices.shape
    def run(image, *args):
        groups = image.shape[1]
        fine = Mesh(
            mesh.devices.reshape(groups, sections // groups, coils, spaces),
            ("group", "member", "coil", "space"),
        )
        section = ("group", "member")
        in_specs = (
            P(None, None, "coil", "space", None),
            P("coil", None, None, "space", None),
            P(None, None, "coil", "space", None),
            P(),
            P(section),
            P(section, None, None),
            P(section, None),
            P(section, None, None),
        )
        out_specs = P(section, None, None, "coil", "space", None)
        return jax.shard_map(
            per_device, mesh=fine, in_specs=in_specs, out_specs=out_specs, check_vma=False
        )(image, *args)

    return run
```

```python
import functools
import math

import jax
import jax.numpy as jnp
from jax import lax
from jax.experimental import pallas as pl
from jax.experimental.pallas import tpu as pltpu
from jax.sharding import Mesh
from jax.sharding import PartitionSpec as P

BF = jnp.bfloat16
F32 = jnp.float32
ROWS = 8
UNROLL = 4
LANES = 128


def half_tables(length):
    half = length // 2
    slot = jnp.arange(half, dtype=jnp.int32)
    index = jnp.arange(length, dtype=jnp.int32)
    product = slot[:, None] * index[None, :] % length
    angle = product.astype(F32) * (2.0 * math.pi / length)
    scale = 1.0 / math.sqrt(length)
    odd = (index % 2).astype(F32)[None, :] * scale
    even = scale - odd
    first = slot[:, None] == 0
    cos = jnp.where(first, even, jnp.cos(angle) * scale)
    sin = jnp.where(first, odd, jnp.sin(angle) * scale)
    return jnp.concatenate([cos, sin], axis=0).astype(BF)


def slot_order(length):
    half = length // 2
    slot = jnp.arange(length, dtype=jnp.int32)
    return jnp.where(slot <= half, slot, length + half - slot)


def unpack_mask(mask_bits, length_z):
    half = mask_bits.shape[1] // 2
    mask_bits = jnp.concatenate(
        [mask_bits[:, : half + 1], jnp.flip(mask_bits[:, half + 1 :], axis=1)], axis=1
    )
    column = slot_order(length_z)
    word_count = mask_bits.shape[2]
    chosen = jnp.zeros(mask_bits.shape[:2] + (length_z,), jnp.int32)
    for word in range(word_count):
        chosen = jnp.where(column // 30 == word, mask_bits[:, :, word : word + 1], chosen)
    return (jnp.right_shift(chosen, column % 30) & 1).astype(F32)


def dot(left, right):
    return jnp.dot(left, right, preferred_element_type=F32)


def shifted_lanes(values, step):
    length = values.shape[1]
    lane = lax.broadcasted_iota(jnp.int32, values.shape, 1)
    if step > 0:
        return jnp.where(lane == 0, 0.0, pltpu.roll(values, 1, 1))
    return jnp.where(lane == length - 1, 0.0, pltpu.roll(values, length - 1, 1))


def first_lane(on, other):
    lane = lax.broadcasted_iota(jnp.int32, on.shape, 1)
    return jnp.where(lane == 0, on, other)


def first_row(on, other):
    row = lax.broadcasted_iota(jnp.int32, (8, on.shape[1]), 0)
    return jnp.concatenate([jnp.where(row == 0, on[:8], other[:8]), other[8:]], axis=0)


def spread(cos_re, sin_re, cos_im, sin_im, pick):
    add_re = pick(sin_re, sin_im)
    add_im = pick(sin_im, -sin_re)
    return cos_re + add_re, cos_re - add_re, cos_im + add_im, cos_im - add_im


def folded(plus_re, minus_re, plus_im, minus_im, pick):
    sum_re, odd_re = plus_re + minus_re, plus_re - minus_re
    sum_im, odd_im = plus_im + minus_im, plus_im - minus_im
    return sum_re, pick(odd_re, -odd_im), sum_im, pick(odd_im, odd_re)


def joined(parts, axis):
    return jnp.concatenate([part.astype(BF) for part in parts], axis=axis)


def consistency_kernel(phases, width, cascade, neighbours, place_ref, base_ref, *refs):
    part_refs = refs[:neighbours]
    (
        maps_ref,
        adjoint_ref,
        mask_ref,
        pack_ref,
        table_z,
        table_zt,
        table_y,
        table_yt,
        rows_ref,
        dc_ref,
        v_ref,
        image,
        total,
    ) = refs[neighbours:]
    channels, length_y, length_z = base_ref.shape
    half_y, half_z = length_y // 2, length_z // 2
    for channel in range(channels):
        value = base_ref[channel].astype(F32)
        for part in part_refs:
            value = value + part[channel].astype(F32)
        image[channel] = value
        total[channel] = -adjoint_ref[channel].astype(F32)
    row_count = rows_ref.shape[1]
    start = pl.multiple_of(place_ref[0] * row_count, row_count)
    rows_ref[...] = image[:, pl.ds(start, row_count), :]

    def item(map_re, map_im, phase):
        image_re = image[2 * phase].astype(BF).astype(F32)
        image_im = image[2 * phase + 1].astype(BF).astype(F32)
        coil_img = joined(
            [map_re * image_re - map_im * image_im, map_re * image_im + map_im * image_re], 0
        )
        value = dot(coil_img, table_zt[...])
        kz = joined(
            spread(
                value[:length_y, :half_z],
                value[:length_y, half_z:],
                value[length_y:, :half_z],
                value[length_y:, half_z:],
                first_lane,
            ),
            1,
        )
        value = dot(table_y[...], kz)
        plus_re, minus_re, plus_im, minus_im = spread(
            value[:half_y, :length_z],
            value[half_y:, :length_z],
            value[:half_y, length_z:],
            value[half_y:, length_z:],
            first_row,
        )
        plus = mask_ref[phase, :half_y]
        minus = mask_ref[phase, half_y:]
        even_re, odd_re, even_im, odd_im = folded(
            plus_re * plus, minus_re * minus, plus_im * plus, minus_im * minus, first_row
        )
        spectrum = jnp.concatenate(
            [joined([even_re, even_im], 1), joined([odd_re, odd_im], 1)], axis=0
        )
        value = dot(table_yt[...], spectrum)
        even_re, odd_re, even_im, odd_im = folded(
            value[:, :half_z],
            value[:, half_z:length_z],
            value[:, length_z : length_z + half_z],
            value[:, length_z + half_z :],
            first_lane,
        )
        back = dot(
            jnp.concatenate([joined([even_re, odd_re], 1), joined([even_im, odd_im], 1)], axis=0),
            table_z[...],
        )
        back_re, back_im = back[:length_y], back[length_y:]
        total[2 * phase] += map_re * back_re + map_im * back_im
        total[2 * phase + 1] += map_re * back_im - map_im * back_re

    def coil(index, carry):
        maps = maps_ref[index].astype(F32)
        for phase in range(phases):
            item(maps[:, :length_z], maps[:, length_z:], phase)
        return carry

    lax.fori_loop(0, maps_ref.shape[0], coil, 0)
    step = pack_ref[cascade, 2 * width : 2 * width + 1, 1:2]
    for channel in range(channels):
        value = image[channel] - step * total[channel]
        dc_ref[channel] = value
        v_ref[channel] = value.astype(BF)


def refine_kernel(neighbours, width, cascade, v_ref, *refs):
    other_refs = refs[:neighbours]
    dc_ref, pack_ref, select1_ref, select2_ref, base_ref = refs[neighbours : neighbours + 5]
    send_refs = refs[neighbours + 5 : 2 * neighbours + 5]
    mixed, taps, hidden, weight1, weight2 = refs[2 * neighbours + 5 :]
    channels, length_y, length_z = v_ref.shape
    tiles, mixed_rows, lanes = mixed.shape
    padded = length_y + 2 * ROWS
    per_row = mixed_rows // padded
    count = select1_ref.shape[1]
    bias_at = weight1.shape[1] - 2 * ROWS

    small1 = pack_ref[cascade, :width, :count].astype(BF)
    small2 = pack_ref[cascade, width : 2 * width, :count].astype(BF)
    bias = pack_ref[cascade, 2 * width :, 0:1]
    terms = []
    for _ in range(3):
        terms.append(bias.astype(BF).astype(F32))
        bias = bias - terms[-1]
    for row in range(ROWS):
        value = dot(small1, select1_ref[row])
        column = lax.broadcasted_iota(jnp.int32, value.shape, 1)
        for at, term in enumerate(terms):
            value = jnp.where(column == bias_at + at, term, value)
        weight1[row * width : (row + 1) * width, :] = value.astype(BF)
    repeated = jnp.concatenate([small2] * (ROWS + 2), axis=0)
    shape = weight2.shape
    column = lax.broadcasted_iota(jnp.int32, shape, 1)
    lower = (lax.broadcasted_iota(jnp.int32, shape, 0) & (ROWS - 1)) * width
    value = jnp.zeros(shape, F32)
    for tap in range(3):
        placed = lax.dot_general(
            select2_ref[tap], repeated, (((1,), (1,)), ((), ())), preferred_element_type=F32
        )
        low = lower + tap * width
        value = jnp.where((column >= low) & (column < low + width), placed, value)
    weight2[...] = value.astype(BF)

    for tile in range(tiles):
        mixed[tile, 0:per_row, :] = jnp.zeros((per_row, lanes), F32)
        tail = (length_y + 1) * per_row
        mixed[tile, tail:, :] = jnp.zeros((mixed_rows - tail, lanes), F32)
    hidden[0:width, :] = jnp.zeros((width, length_z), BF)
    hidden[(length_y + 1) * width :, :] = jnp.zeros((width, length_z), BF)
    sources = [v_ref, *other_refs]
    for at in range(per_row):
        plane, channel = divmod(at, channels)
        if plane < len(sources):
            value = sources[plane][channel].astype(F32)
        else:
            value = jnp.zeros((length_y, length_z), F32)
        for tile in range(tiles):
            mixed[tile, pl.ds(per_row + at, length_y, stride=per_row), :] = value[
                :, tile * lanes : (tile + 1) * lanes
            ]

    group = 2 * ROWS

    def build(block, carry):
        start = pl.multiple_of(block * (group * per_row), group * per_row)
        window = jnp.concatenate(
            [mixed[tile, pl.ds(start, group * per_row), :] for tile in range(tiles)], axis=1
        )
        shape = (group, per_row, length_z)
        value = jnp.stack(
            [
                shifted_lanes(window, 1).reshape(shape),
                window.reshape(shape),
                shifted_lanes(window, -1).reshape(shape),
            ],
            axis=1,
        )
        store = pl.multiple_of(block * (group * 3 * per_row), group * 3 * per_row)
        taps[pl.ds(store, group * 3 * per_row), :] = value.reshape(-1, length_z).astype(BF)
        return carry

    lax.fori_loop(0, padded // group, build, 0)
    ones_row = lax.broadcasted_iota(jnp.int32, (2 * ROWS, length_z), 0)
    ones = jnp.where(ones_row < 3, 1.0, 0.0).astype(BF)

    def first(block, carry):
        for part in range(UNROLL):
            at = block * UNROLL + part
            start = pl.multiple_of(at * (ROWS * 3 * per_row), ROWS * 3 * per_row)
            window = jnp.concatenate(
                [taps[pl.ds(start, (ROWS + 2) * 3 * per_row), :], ones], axis=0
            )
            value = dot(weight1[...], window)
            store = pl.multiple_of((at * ROWS + 1) * width, width)
            hidden[pl.ds(store, ROWS * width), :] = jnp.maximum(value, 0.0).astype(BF)
        return carry

    lax.fori_loop(0, length_y // (UNROLL * ROWS), first, 0)
    block_rows = channels * ROWS

    def second(block, carry):
        results = []
        for part in range(UNROLL):
            at = block * UNROLL + part
            start = pl.multiple_of(at * (ROWS * width), ROWS * width)
            parts = dot(weight2[...], hidden[pl.ds(start, (ROWS + 2) * width), :])
            third = parts.shape[0] // 3
            results.append(
                shifted_lanes(parts[:third], 1)
                + parts[third : 2 * third]
                + shifted_lanes(parts[2 * third :], -1)
            )
        span = UNROLL * ROWS
        rows = pl.ds(pl.multiple_of(block * span, span), span)
        for plane in range(neighbours + 1):
            for channel in range(channels):
                lo = plane * block_rows + channel * ROWS
                value = jnp.concatenate([piece[lo : lo + ROWS] for piece in results], axis=0)
                if plane == 0:
                    base_ref[channel, rows, :] = dc_ref[channel, rows, :] + value
                else:
                    send_refs[plane - 1][channel, rows, :] = value.astype(BF)
        return carry

    lax.fori_loop(0, length_y // (UNROLL * ROWS), second, 0)


def gathered_rows(value, axis, dim):
    count = lax.axis_size(axis)
    index = lax.axis_index(axis)
    size = value.shape[dim]
    shape = list(value.shape)
    shape[dim] = size * count
    whole = jnp.zeros(shape, value.dtype)
    for step in range(count):
        block = value
        if step:
            block = lax.ppermute(value, axis, [(i, (i + step) % count) for i in range(count)])
        whole = lax.dynamic_update_slice_in_dim(
            whole, block, (index - step) % count * size, dim
        )
    return whole


def per_device(image, sens, adjoint, mask_bits, step_size, conv1_w, conv1_b, conv2_w):
    channels, slab_count, _, row_count, length_z = image.shape
    phases, length_y = mask_bits.shape[:2]
    planes = lax.axis_size("coil")
    coil_local = sens.shape[0]
    width = conv1_w.shape[1]
    groups = lax.axis_size("group")
    members = lax.axis_size("member")
    cascades = groups * members
    group = lax.axis_index("group")
    member = lax.axis_index("member")
    plane = lax.axis_index("coil")
    section = group * members + member
    table_z = half_tables(length_z)
    table_y = table_z if length_y == length_z else half_tables(length_y)
    tables = (table_z, table_z.T, table_y, table_y.T)
    sampled = unpack_mask(mask_bits, length_z)
    count = conv1_w.shape[2]
    extra = jnp.concatenate(
        [conv1_b.T, jnp.broadcast_to(step_size.reshape(1, 1), (width, 1))], axis=1
    )
    packed = jnp.concatenate(
        [
            jnp.pad(part, ((0, 0), (0, -(-count // LANES) * LANES - part.shape[1])))
            for part in (conv1_w[0].astype(F32), conv2_w[0].astype(F32), extra)
        ],
        axis=0,
    )[None]
    packed = gathered_rows(gathered_rows(packed, "member", 0), "group", 0)

    if planes == 1:
        sides = []
    elif planes == 2:
        sides = [None]
    else:
        sides = [-1, 1]
    neighbours = len(sides)
    involved = neighbours + 1
    per_row = -(-(involved * channels) // 8) * 8

    def tap_of(side, sign):
        if side is None:
            return jnp.where(plane == 0, 1 + sign, 1 - sign)
        return jnp.full((), 1 + sign * side, jnp.int32)

    one = jnp.ones((), jnp.int32)
    planes1 = [one] + [tap_of(side, 1) for side in sides]
    planes2 = [one] + [tap_of(side, -1) for side in sides]
    window = ROWS + 2
    used = window * 3 * per_row
    shape = (ROWS, count, used + 2 * ROWS)
    row = lax.broadcasted_iota(jnp.int32, shape, 0)
    tap = lax.broadcasted_iota(jnp.int32, shape, 1)
    column = lax.broadcasted_iota(jnp.int32, shape, 2)
    slot = column % per_row
    wanted = jnp.full(shape, -1, jnp.int32)
    for at, value in enumerate(planes1):
        wanted = jnp.where(slot // channels == at, value, wanted)
    select1 = (
        (column < used)
        & (tap // (9 * channels) == wanted)
        & (tap // (3 * channels) % 3 == column // (3 * per_row) - row)
        & (tap // channels % 3 == column // per_row % 3)
        & (tap % channels == slot % channels)
    ).astype(BF)
    shape = (3, 3 * involved * channels * ROWS, count)
    row = lax.broadcasted_iota(jnp.int32, shape, 1)
    tap = lax.broadcasted_iota(jnp.int32, shape, 2)
    at_plane = row // (channels * ROWS) % involved
    wanted = jnp.full(shape, -1, jnp.int32)
    for at, value in enumerate(planes2):
        wanted = jnp.where(at_plane == at, value, wanted)
    select2 = (
        (tap // (9 * channels) == wanted)
        & (tap // (3 * channels) % 3 == lax.broadcasted_iota(jnp.int32, shape, 0))
        & (tap // channels % 3 == row // (involved * channels * ROWS))
        & (tap % channels == row // ROWS % channels)
    ).astype(BF)

    maps = lax.dynamic_index_in_dim(sens, group, 1, keepdims=False)
    maps = lax.all_to_all(maps, "coil", split_axis=1, concat_axis=0, tiled=True)
    maps = gathered_rows(maps[:, 0], "space", 1)
    own_image = lax.dynamic_index_in_dim(image, group, 1, keepdims=False)[:, 0].astype(BF)
    own_adjoint = lax.dynamic_index_in_dim(adjoint, group, 1, keepdims=False)[:, 0].astype(BF)
    base = gathered_rows(own_image, "space", 1)
    target = gathered_rows(own_adjoint, "space", 1)

    full = jax.ShapeDtypeStruct((channels, length_y, length_z), F32)
    half = jax.ShapeDtypeStruct((channels, length_y, length_z), BF)
    vmem = pl.BlockSpec(memory_space=pltpu.VMEM)
    smem = pl.BlockSpec(memory_space=pltpu.SMEM)
    params = pltpu.CompilerParams(vmem_limit_bytes=56 * 1024 * 1024)

    place = lax.axis_index("space").reshape(1)
    rows_shape = jax.ShapeDtypeStruct((channels, row_count, length_z), F32)

    def consistency(cascade, base, parts):
        return pl.pallas_call(
            functools.partial(consistency_kernel, phases, width, cascade, len(parts)),
            out_shape=(rows_shape, full, half),
            in_specs=[smem] + [vmem] * (9 + len(parts)),
            out_specs=(vmem, vmem, vmem),
            scratch_shapes=[pltpu.VMEM((channels, length_y, length_z), F32)] * 2,
            compiler_params=params,
        )(place, base, *parts, maps, target, sampled, packed, *tables)

    def refine(cascade, value, others, updated):
        padded = length_y + 2 * ROWS
        return pl.pallas_call(
            functools.partial(refine_kernel, neighbours, width, cascade),
            out_shape=(full,) + (half,) * neighbours,
            in_specs=[vmem] * (5 + neighbours),
            out_specs=(vmem,) * (1 + neighbours),
            scratch_shapes=[
                pltpu.VMEM((length_z // LANES, padded * per_row, LANES), F32),
                pltpu.VMEM((padded * 3 * per_row, length_z), BF),
                pltpu.VMEM(((length_y + 2) * width, length_z), BF),
                pltpu.VMEM((ROWS * width, select1.shape[2]), BF),
                pltpu.VMEM((select2.shape[1], (ROWS + 2) * width), BF),
            ],
            compiler_params=params,
        )(value, *others, updated, packed, select1, select2)

    def exchanged(values):
        received = []
        for value, side in zip(values, sides):
            if side is None:
                pairs = [(0, 1), (1, 0)]
            else:
                pairs = [(i, i - side) for i in range(planes) if 0 <= i - side < planes]
            received.append(lax.ppermute(value, "coil", pairs))
        return received

    row_start = lax.axis_index("space") * row_count

    def own_rows(value):
        return lax.dynamic_slice_in_dim(value, row_start, row_count, 1)

    results = []
    parts = []
    for cascade in range(cascades):
        rows, updated, value = consistency(cascade, base, parts)
        if cascade:
            results.append(rows)
        others = exchanged([value] * neighbours)
        base, *sends = refine(cascade, value, others, updated)
        turned = sends[::-1] if neighbours == 2 else sends
        parts = exchanged(turned)[::-1] if neighbours == 2 else exchanged(turned)
    last = own_rows(base)
    for part in parts:
        last = last + own_rows(part).astype(F32)
    results.append(last)

    def result_of(wanted):
        chosen = results[0]
        for cascade in range(1, cascades):
            chosen = jnp.where(wanted == cascade, results[cascade], chosen)
        return chosen

    output = jnp.zeros((channels, slab_count, row_count, length_z), F32)
    for step in range(groups):
        if step == 0:
            chosen = result_of(section)
        else:
            target_group = (group - step) % groups
            chosen = result_of(target_group * members + member).astype(BF)
            chosen = lax.ppermute(
                chosen, "group", [(i, (i - step) % groups) for i in range(groups)]
            ).astype(F32)
        output = lax.dynamic_update_slice_in_dim(
            output, chosen[:, None], (group + step) % groups, 1
        )
    return output[None, :, :, None]


def solution(mesh):
    sections, coils, spaces = mesh.devices.shape
    def run(image, *args):
        groups = image.shape[1]
        fine = Mesh(
            mesh.devices.reshape(groups, sections // groups, coils, spaces),
            ("group", "member", "coil", "space"),
        )
        section = ("group", "member")
        in_specs = (
            P(None, None, "coil", "space", None),
            P("coil", None, None, "space", None),
            P(None, None, "coil", "space", None),
            P(),
            P(section),
            P(section, None, None),
            P(section, None),
            P(section, None, None),
        )
        out_specs = P(section, None, None, "coil", "space", None)
        return jax.shard_map(
            per_device, mesh=fine, in_specs=in_specs, out_specs=out_specs, check_vma=False
        )(image, *args)

    return run
```

```python
import functools

import jax
import jax.numpy as jnp
import numpy as np
from jax import lax
from jax.experimental import pallas as pl
from jax.experimental.pallas import tpu as pltpu
from jax.sharding import Mesh
from jax.sharding import PartitionSpec as P

BF = jnp.bfloat16
F32 = jnp.float32
ROWS = 8
UNROLL = 4
LANES = 128


def half_tables(length):
    half = length // 2
    index = np.arange(length)
    angle = np.arange(half)[:, None] * index[None, :] % length * (2.0 * np.pi / length)
    scale = 1.0 / np.sqrt(length)
    cos = np.cos(angle) * scale
    sin = np.sin(angle) * scale
    cos[0] = np.where(index % 2 == 0, scale, 0.0)
    sin[0] = np.where(index % 2 == 0, 0.0, scale)
    return np.concatenate([cos, sin], axis=0).astype(BF)


def slot_order(length):
    half = length // 2
    slot = np.arange(length)
    return np.where(slot <= half, slot, length + half - slot)


def tap_selectors(channels, per_row, offsets):
    count = 27 * channels
    involved = len(offsets)
    used = (ROWS + 2) * 3 * per_row
    columns = -(-(used + 3) // LANES) * LANES
    tap = np.arange(count)
    plane, tap_y, tap_z, channel = (
        tap // (9 * channels),
        tap // (3 * channels) % 3,
        tap // channels % 3,
        tap % channels,
    )
    column = np.arange(columns)
    slot = column % per_row
    offset = np.array(list(offsets) + [9] * (per_row // channels + 1))[slot // channels]
    first = (
        (column[None] < 9 * per_row)
        & (plane[:, None] == 1 + offset[None])
        & (tap_y[:, None] == column[None] // (3 * per_row))
        & (tap_z[:, None] == column[None] // per_row % 3)
        & (channel[:, None] == slot[None] % channels)
    )
    row = np.arange(3 * involved * channels * ROWS)
    offset = np.array(offsets)[row // (channels * ROWS) % involved]
    second = (
        (plane[None] == 1 - offset[:, None])
        & (tap_z[None] == row[:, None] // (involved * channels * ROWS))
        & (channel[None] == row[:, None] // ROWS % channels)
    )
    second = np.stack([second & (tap_y[None] == at) for at in range(3)])
    return first.astype(BF), second.astype(BF)


def dot(left, right):
    return jnp.dot(left, right, preferred_element_type=F32)


def shifted_lanes(values, step):
    length = values.shape[1]
    lane = lax.broadcasted_iota(jnp.int32, values.shape, 1)
    if step > 0:
        return jnp.where(lane == 0, 0.0, pltpu.roll(values, 1, 1))
    return jnp.where(lane == length - 1, 0.0, pltpu.roll(values, length - 1, 1))


def first_lane(on, other):
    lane = lax.broadcasted_iota(jnp.int32, on.shape, 1)
    return jnp.where(lane == 0, on, other)


def first_row(on, other):
    row = lax.broadcasted_iota(jnp.int32, (8, on.shape[1]), 0)
    return jnp.concatenate([jnp.where(row == 0, on[:8], other[:8]), other[8:]], axis=0)


def spread(cos_re, sin_re, cos_im, sin_im, pick):
    add_re = pick(sin_re, sin_im)
    add_im = pick(sin_im, -sin_re)
    return cos_re + add_re, cos_re - add_re, cos_im + add_im, cos_im - add_im


def folded(plus_re, minus_re, plus_im, minus_im, pick):
    sum_re, odd_re = plus_re + minus_re, plus_re - minus_re
    sum_im, odd_im = plus_im + minus_im, plus_im - minus_im
    return sum_re, pick(odd_re, -odd_im), sum_im, pick(odd_im, odd_re)


def joined(parts, axis):
    return jnp.concatenate([part.astype(BF) for part in parts], axis=axis)


def consistency_kernel(phases, width, cascade, neighbours, place_ref, base_ref, *refs):
    part_refs = refs[:neighbours]
    (
        maps_ref,
        adjoint_ref,
        mask_ref,
        pack_ref,
        table_z,
        table_zt,
        table_y,
        table_yt,
        rows_ref,
        dc_ref,
        v_ref,
        image,
        total,
    ) = refs[neighbours:]
    channels, length_y, length_z = base_ref.shape
    half_y, half_z = length_y // 2, length_z // 2
    for channel in range(channels):
        value = base_ref[channel].astype(F32)
        for part in part_refs:
            value = value + part[channel].astype(F32)
        image[channel] = value
        total[channel] = -adjoint_ref[channel].astype(F32)
    row_count = rows_ref.shape[1]
    start = pl.multiple_of(place_ref[0] * row_count, row_count)
    rows_ref[...] = image[:, pl.ds(start, row_count), :]

    def item(map_re, map_im, phase):
        image_re = image[2 * phase].astype(BF).astype(F32)
        image_im = image[2 * phase + 1].astype(BF).astype(F32)
        coil_img = joined(
            [map_re * image_re - map_im * image_im, map_re * image_im + map_im * image_re], 0
        )
        value = dot(coil_img, table_zt[...])
        kz = joined(
            spread(
                value[:length_y, :half_z],
                value[:length_y, half_z:],
                value[length_y:, :half_z],
                value[length_y:, half_z:],
                first_lane,
            ),
            1,
        )
        value = dot(table_y[...], kz)
        plus_re, minus_re, plus_im, minus_im = spread(
            value[:half_y, :length_z],
            value[half_y:, :length_z],
            value[:half_y, length_z:],
            value[half_y:, length_z:],
            first_row,
        )
        plus = mask_ref[phase, :half_y]
        minus = mask_ref[phase, half_y:]
        even_re, odd_re, even_im, odd_im = folded(
            plus_re * plus, minus_re * minus, plus_im * plus, minus_im * minus, first_row
        )
        spectrum = jnp.concatenate(
            [joined([even_re, even_im], 1), joined([odd_re, odd_im], 1)], axis=0
        )
        value = dot(table_yt[...], spectrum)
        even_re, odd_re, even_im, odd_im = folded(
            value[:, :half_z],
            value[:, half_z:length_z],
            value[:, length_z : length_z + half_z],
            value[:, length_z + half_z :],
            first_lane,
        )
        back = dot(
            jnp.concatenate([joined([even_re, odd_re], 1), joined([even_im, odd_im], 1)], axis=0),
            table_z[...],
        )
        back_re, back_im = back[:length_y], back[length_y:]
        total[2 * phase] += map_re * back_re + map_im * back_im
        total[2 * phase + 1] += map_re * back_im - map_im * back_re

    def coil(index, carry):
        map_re = maps_ref[2 * index].astype(F32)
        map_im = maps_ref[2 * index + 1].astype(F32)
        for phase in range(phases):
            item(map_re, map_im, phase)
        return carry

    lax.fori_loop(0, maps_ref.shape[0] // 2, coil, 0)
    step = pack_ref[cascade, 2 * width : 2 * width + 1, 1:2]
    for channel in range(channels):
        value = image[channel] - step * total[channel]
        dc_ref[channel] = value
        v_ref[channel] = value.astype(BF)


def refine_kernel(neighbours, width, cascade, place_ref, v_ref, *refs):
    other_refs = refs[:neighbours]
    dc_ref, weight1_ref, weight2_ref, base_ref = refs[neighbours : neighbours + 4]
    send_refs = refs[neighbours + 4 : 2 * neighbours + 4]
    mixed, taps, hidden = refs[2 * neighbours + 4 :]
    channels, length_y, length_z = v_ref.shape
    tiles, mixed_rows, lanes = mixed.shape
    padded = length_y + 2 * ROWS
    per_row = mixed_rows // padded
    total_blocks = length_y // ROWS
    out_rows = base_ref.shape[1]
    if out_rows == length_y:
        first_block, out_block, blocks = 0, 0, total_blocks
    else:
        wanted = out_rows // ROWS + 2
        blocks = min(total_blocks, -(-wanted // UNROLL) * UNROLL)
        out_block = place_ref[0] * (out_rows // ROWS)
        first_block = jnp.clip(out_block - 1, 0, total_blocks - blocks)

    for tile in range(tiles):
        mixed[tile, 0:per_row, :] = jnp.zeros((per_row, lanes), F32)
        tail = (length_y + 1) * per_row
        mixed[tile, tail:, :] = jnp.zeros((mixed_rows - tail, lanes), F32)
    hidden[0:width, :] = jnp.zeros((width, length_z), BF)
    hidden[(length_y + 1) * width :, :] = jnp.zeros((width, length_z), BF)
    sources = [v_ref, *other_refs]
    for at in range(per_row):
        plane, channel = divmod(at, channels)
        if plane < len(sources):
            value = sources[plane][channel].astype(F32)
        else:
            value = jnp.zeros((length_y, length_z), F32)
        for tile in range(tiles):
            mixed[tile, pl.ds(per_row + at, length_y, stride=per_row), :] = value[
                :, tile * lanes : (tile + 1) * lanes
            ]

    group = 2 * ROWS

    def build(block, carry):
        start = pl.multiple_of(block * (group * per_row), group * per_row)
        window = jnp.concatenate(
            [mixed[tile, pl.ds(start, group * per_row), :] for tile in range(tiles)], axis=1
        )
        shape = (group, per_row, length_z)
        value = jnp.stack(
            [
                shifted_lanes(window, 1).reshape(shape),
                window.reshape(shape),
                shifted_lanes(window, -1).reshape(shape),
            ],
            axis=1,
        )
        store = pl.multiple_of(block * (group * 3 * per_row), group * 3 * per_row)
        taps[pl.ds(store, group * 3 * per_row), :] = value.reshape(-1, length_z).astype(BF)
        return carry

    builds = min(padded // group, blocks * ROWS // group + 2)
    if builds == padded // group:
        build_at = 0
    else:
        build_at = jnp.minimum(first_block * ROWS // group, padded // group - builds)
    lax.fori_loop(build_at, build_at + builds, build, 0)
    spare = weight1_ref.shape[2] - (ROWS + 2) * 3 * per_row
    ones_row = lax.broadcasted_iota(jnp.int32, (spare, length_z), 0)
    ones = jnp.where(ones_row < 3, 1.0, 0.0).astype(BF)

    def first(block, carry):
        for part in range(UNROLL):
            at = first_block + block * UNROLL + part
            start = pl.multiple_of(at * (ROWS * 3 * per_row), ROWS * 3 * per_row)
            window = jnp.concatenate(
                [taps[pl.ds(start, (ROWS + 2) * 3 * per_row), :], ones], axis=0
            )
            value = dot(weight1_ref[cascade], window)
            store = pl.multiple_of((at * ROWS + 1) * width, width)
            hidden[pl.ds(store, ROWS * width), :] = jnp.maximum(value, 0.0).astype(BF)
        return carry

    lax.fori_loop(0, blocks // UNROLL, first, 0)
    block_rows = channels * ROWS
    unroll = min(UNROLL, out_rows // ROWS)
    span = unroll * ROWS

    def second(block, carry):
        results = []
        for part in range(unroll):
            at = out_block + block * unroll + part
            start = pl.multiple_of(at * (ROWS * width), ROWS * width)
            parts = dot(weight2_ref[cascade], hidden[pl.ds(start, (ROWS + 2) * width), :])
            third = parts.shape[0] // 3
            results.append(
                shifted_lanes(parts[:third], 1)
                + parts[third : 2 * third]
                + shifted_lanes(parts[2 * third :], -1)
            )
        rows = pl.ds(pl.multiple_of(block * span, span), span)
        from_rows = pl.ds(pl.multiple_of(out_block * ROWS + block * span, ROWS * 2), span)
        for plane in range(neighbours + 1):
            for channel in range(channels):
                lo = plane * block_rows + channel * ROWS
                value = jnp.concatenate([piece[lo : lo + ROWS] for piece in results], axis=0)
                if plane == 0:
                    base_ref[channel, rows, :] = dc_ref[channel, from_rows, :] + value
                else:
                    send_refs[plane - 1][channel, rows, :] = value.astype(BF)
        return carry

    lax.fori_loop(0, out_rows // span, second, 0)


def prepare_kernel(
    width,
    per_row,
    place_ref,
    pack_ref,
    bits_ref,
    columns_ref,
    order_ref,
    select1_ref,
    select2_ref,
    weight1_ref,
    weight2_ref,
    mask_ref,
):
    phases, length_y, length_z = mask_ref.shape
    for phase in range(phases):
        bits = bits_ref[phase]
        chosen = jnp.zeros((length_y, length_z), jnp.int32)
        for word in range(bits.shape[1]):
            chosen = jnp.where(columns_ref[0:1] == word, bits[:, word : word + 1], chosen)
        shift = jnp.broadcast_to(columns_ref[1:2], chosen.shape)
        taken = lax.shift_right_logical(chosen, shift) & 1
        mask_ref[phase] = dot(order_ref[...], taken.astype(F32).astype(BF))

    variant = place_ref[1] if select1_ref.shape[0] > 1 else 0
    count = select1_ref.shape[1]
    for cascade in range(pack_ref.shape[0]):
        small1 = pack_ref[cascade, :width, :count].astype(BF)
        small2 = pack_ref[cascade, width : 2 * width, :count].astype(BF)
        bias = pack_ref[cascade, 2 * width :, 0:1]
        terms = []
        for _ in range(3):
            terms.append(bias.astype(BF).astype(F32))
            bias = bias - terms[-1]
        base = dot(small1, select1_ref[variant])
        column = lax.broadcasted_iota(jnp.int32, base.shape, 1)
        step = per_row
        for row in range(ROWS):
            value = base if row == 0 else pltpu.roll(base, row * 3 * step, 1)
            for at, term in enumerate(terms):
                value = jnp.where(column == (ROWS + 2) * 3 * step + at, term, value)
            weight1_ref[cascade, row * width : (row + 1) * width, :] = value.astype(BF)
        repeated = jnp.concatenate([small2] * (ROWS + 2), axis=0)
        shape = weight2_ref.shape[1:]
        column = lax.broadcasted_iota(jnp.int32, shape, 1)
        lower = (lax.broadcasted_iota(jnp.int32, shape, 0) & (ROWS - 1)) * width
        value = jnp.zeros(shape, F32)
        for tap in range(3):
            placed = lax.dot_general(
                select2_ref[variant, tap],
                repeated,
                (((1,), (1,)), ((), ())),
                preferred_element_type=F32,
            )
            low = lower + tap * width
            value = jnp.where((column >= low) & (column < low + width), placed, value)
        weight2_ref[cascade] = value.astype(BF)


def assemble_kernel(members, spaces, place_ref, *refs):
    local_ref = refs[0]
    block_refs = refs[1 : 1 + (spaces - 1) * members]
    out_refs = refs[1 + (spaces - 1) * members :]
    rows = local_ref.shape[2]

    def put(owner, at, block):
        where = pl.ds(pl.multiple_of(at * rows, rows), rows)
        taken = 0
        for out_ref in out_refs:
            size = out_ref.shape[0] // members
            for index in range(size):
                out_ref[owner * size + index, where, :] = block[taken + index]
            taken += size

    for member in range(members):
        put(member, place_ref[0], local_ref[member])
    for step in range(1, spaces):
        at = lax.rem(place_ref[0] - step + spaces, spaces)
        for offset in range(members):
            owner = lax.rem(place_ref[2] + offset, members)
            put(owner, at, block_refs[(step - 1) * members + offset])


def ring(value, axis, step):
    count = lax.axis_size(axis)
    return lax.ppermute(value, axis, [(i, (i + step) % count) for i in range(count)])


def gathered(value, axis):
    count = lax.axis_size(axis)
    index = lax.axis_index(axis)
    whole = jnp.zeros((count,) + value.shape, value.dtype)
    for step in range(count):
        block = ring(value, axis, step) if step else value
        whole = lax.dynamic_update_index_in_dim(whole, block, (index - step) % count, 0)
    return whole


def per_device(image, sens, adjoint, mask_bits, step_size, conv1_w, conv1_b, conv2_w):
    channels, slab_count, _, row_count, length_z = image.shape
    phases, length_y = mask_bits.shape[:2]
    planes = lax.axis_size("coil")
    coil_local = sens.shape[0]
    width = conv1_w.shape[1]
    groups = lax.axis_size("group")
    members = lax.axis_size("member")
    cascades = groups * members
    group = lax.axis_index("group")
    member = lax.axis_index("member")
    plane = lax.axis_index("coil")
    section = group * members + member
    table_z = half_tables(length_z)
    table_y = half_tables(length_y)
    tables = tuple(jnp.asarray(value) for value in (table_z, table_z.T, table_y, table_y.T))
    count = conv1_w.shape[2]
    extra = jnp.concatenate(
        [conv1_b.T, jnp.broadcast_to(step_size.reshape(1, 1), (width, 1))], axis=1
    )
    packed = jnp.concatenate(
        [
            jnp.pad(part, ((0, 0), (0, -(-count // LANES) * LANES - part.shape[1])))
            for part in (conv1_w[0].astype(F32), conv2_w[0].astype(F32), extra)
        ],
        axis=0,
    )
    packed = gathered(gathered(packed, "member"), "group")
    packed = packed.reshape((cascades,) + packed.shape[2:])

    if planes == 1:
        sides, variants = [], [[0]]
    elif planes == 2:
        sides, variants = [None], [[0, 1], [0, -1]]
    else:
        sides, variants = [-1, 1], [[0, -1, 1]]
    neighbours = len(sides)
    involved = neighbours + 1
    per_row = -(-(involved * channels) // 8) * 8
    chosen = [tap_selectors(channels, per_row, offsets) for offsets in variants]
    select1, select2 = (jnp.asarray(np.stack(parts)) for parts in zip(*chosen))

    place = jnp.stack([lax.axis_index("space"), plane, member]).astype(jnp.int32)
    spaces = lax.axis_size("space")
    maps = lax.dynamic_index_in_dim(sens, group, 1, keepdims=False)
    maps = lax.all_to_all(maps, "coil", split_axis=1, concat_axis=0, tiled=True)[:, 0]
    coils = maps.shape[0]
    maps = maps.reshape(coils, row_count, 2, length_z).transpose(0, 2, 1, 3)
    own_image = lax.dynamic_index_in_dim(image, group, 1, keepdims=False)[:, 0].astype(BF)
    own_adjoint = lax.dynamic_index_in_dim(adjoint, group, 1, keepdims=False)[:, 0].astype(BF)
    shared = members if phases % members == 0 and coils % members == 0 else 1
    local = jnp.concatenate(
        [
            part.reshape(shared, -1, row_count, length_z)
            for part in (own_image, maps, own_adjoint)
        ],
        axis=1,
    )
    mine = lax.dynamic_index_in_dim(local, member % shared, 0, keepdims=False)
    blocks = []
    for step in range(1, spaces):
        block = ring(mine, "space", step)
        blocks.append(block)
        for offset in range(1, shared):
            blocks.append(ring(block, "member", -offset))

    full = jax.ShapeDtypeStruct((channels, length_y, length_z), F32)
    half = jax.ShapeDtypeStruct((channels, length_y, length_z), BF)
    vmem = pl.BlockSpec(memory_space=pltpu.VMEM)
    smem = pl.BlockSpec(memory_space=pltpu.SMEM)
    params = pltpu.CompilerParams(vmem_limit_bytes=32 * 1024 * 1024)
    base, maps, target = pl.pallas_call(
        functools.partial(assemble_kernel, shared, spaces),
        out_shape=(
            half,
            jax.ShapeDtypeStruct((2 * coils, length_y, length_z), BF),
            half,
        ),
        in_specs=[smem] + [vmem] * (1 + len(blocks)),
        out_specs=(vmem,) * 3,
        compiler_params=params,
    )(place, local, *blocks)
    order = np.eye(length_y)[slot_order(length_y)].astype(BF)
    column = slot_order(length_z)
    columns = np.stack([column // 30, column % 30]).astype(np.int32)
    weight1, weight2, sampled = pl.pallas_call(
        functools.partial(prepare_kernel, width, per_row),
        out_shape=(
            jax.ShapeDtypeStruct((cascades, ROWS * width, select1.shape[2]), BF),
            jax.ShapeDtypeStruct((cascades, select2.shape[2], (ROWS + 2) * width), BF),
            jax.ShapeDtypeStruct((phases, length_y, length_z), F32),
        ),
        in_specs=[smem] + [vmem] * 6,
        out_specs=(vmem,) * 3,
        compiler_params=params,
    )(place, packed, mask_bits, jnp.asarray(columns), jnp.asarray(order), select1, select2)

    rows_shape = jax.ShapeDtypeStruct((channels, row_count, length_z), F32)

    def consistency(cascade, base, parts):
        return pl.pallas_call(
            functools.partial(consistency_kernel, phases, width, cascade, len(parts)),
            out_shape=(rows_shape, full, half),
            in_specs=[smem] + [vmem] * (9 + len(parts)),
            out_specs=(vmem, vmem, vmem),
            scratch_shapes=[pltpu.VMEM((channels, length_y, length_z), F32)] * 2,
            compiler_params=params,
        )(place, base, *parts, maps, target, sampled, packed, *tables)

    def refine(cascade, value, others, updated):
        padded = length_y + 2 * ROWS
        height = row_count if cascade == cascades - 1 and row_count % (2 * ROWS) == 0 else length_y
        shape = (channels, height, length_z)
        return pl.pallas_call(
            functools.partial(refine_kernel, neighbours, width, cascade),
            out_shape=(jax.ShapeDtypeStruct(shape, F32),)
            + (jax.ShapeDtypeStruct(shape, BF),) * neighbours,
            in_specs=[smem] + [vmem] * (4 + neighbours),
            out_specs=(vmem,) * (1 + neighbours),
            scratch_shapes=[
                pltpu.VMEM((length_z // LANES, padded * per_row, LANES), F32),
                pltpu.VMEM((padded * 3 * per_row, length_z), BF),
                pltpu.VMEM(((length_y + 2) * width, length_z), BF),
            ],
            compiler_params=params,
        )(place, value, *others, updated, weight1, weight2)

    def exchanged(values):
        received = []
        for value, side in zip(values, sides):
            if side is None:
                pairs = [(0, 1), (1, 0)]
            else:
                pairs = [(i, i - side) for i in range(planes) if 0 <= i - side < planes]
            received.append(lax.ppermute(value, "coil", pairs))
        return received

    row_start = lax.axis_index("space") * row_count

    def own_rows(value):
        if value.shape[1] == row_count:
            return value
        return lax.dynamic_slice_in_dim(value, row_start, row_count, 1)

    results = []
    parts = []
    for cascade in range(cascades):
        rows, updated, value = consistency(cascade, base, parts)
        if cascade:
            results.append(rows)
        others = exchanged([value] * neighbours)
        base, *sends = refine(cascade, value, others, updated)
        turned = sends[::-1] if neighbours == 2 else sends
        parts = exchanged(turned)[::-1] if neighbours == 2 else exchanged(turned)
    last = own_rows(base)
    for part in parts:
        last = last + own_rows(part).astype(F32)
    results.append(last)

    def result_of(wanted):
        chosen = results[0]
        for cascade in range(1, cascades):
            chosen = jnp.where(wanted == cascade, results[cascade], chosen)
        return chosen

    output = jnp.zeros((channels, slab_count, row_count, length_z), F32)
    for step in range(groups):
        if step == 0:
            chosen = result_of(section)
        else:
            target_group = (group - step) % groups
            chosen = result_of(target_group * members + member).astype(BF)
            chosen = lax.ppermute(
                chosen, "group", [(i, (i - step) % groups) for i in range(groups)]
            ).astype(F32)
        output = lax.dynamic_update_slice_in_dim(
            output, chosen[:, None], (group + step) % groups, 1
        )
    return output[None, :, :, None]


def solution(mesh):
    sections, coils, spaces = mesh.devices.shape
    def run(image, *args):
        groups = image.shape[1]
        fine = Mesh(
            mesh.devices.reshape(groups, sections // groups, coils, spaces),
            ("group", "member", "coil", "space"),
        )
        section = ("group", "member")
        in_specs = (
            P(None, None, "coil", "space", None),
            P("coil", None, None, "space", None),
            P(None, None, "coil", "space", None),
            P(),
            P(section),
            P(section, None, None),
            P(section, None),
            P(section, None, None),
        )
        out_specs = P(section, None, None, "coil", "space", None)
        return jax.shard_map(
            per_device, mesh=fine, in_specs=in_specs, out_specs=out_specs, check_vma=False
        )(image, *args)

    return run
```

```python
import functools

import jax
import jax.numpy as jnp
import numpy as np
from jax import lax
from jax.experimental import pallas as pl
from jax.experimental.pallas import tpu as pltpu
from jax.sharding import Mesh
from jax.sharding import PartitionSpec as P

BF = jnp.bfloat16
F32 = jnp.float32
ROWS = 8
UNROLL = 4
LANES = 128


def half_tables(length):
    half = length // 2
    index = np.arange(length)
    angle = np.arange(half)[:, None] * index[None, :] % length * (2.0 * np.pi / length)
    scale = 1.0 / np.sqrt(length)
    cos = np.cos(angle) * scale
    sin = np.sin(angle) * scale
    cos[0] = np.where(index % 2 == 0, scale, 0.0)
    sin[0] = np.where(index % 2 == 0, 0.0, scale)
    return np.concatenate([cos, sin], axis=0).astype(BF)


def slot_order(length):
    half = length // 2
    slot = np.arange(length)
    return np.where(slot <= half, slot, length + half - slot)


def tap_selectors(channels, per_row, offsets):
    count = 27 * channels
    involved = len(offsets)
    used = (ROWS + 2) * 3 * per_row
    columns = -(-(used + 3) // LANES) * LANES
    tap = np.arange(count)
    plane, tap_y, tap_z, channel = (
        tap // (9 * channels),
        tap // (3 * channels) % 3,
        tap // channels % 3,
        tap % channels,
    )
    column = np.arange(columns)
    slot = column % per_row
    offset = np.array(list(offsets) + [9] * (per_row // channels + 1))[slot // channels]
    first = (
        (column[None] < 9 * per_row)
        & (plane[:, None] == 1 + offset[None])
        & (tap_y[:, None] == column[None] // (3 * per_row))
        & (tap_z[:, None] == column[None] // per_row % 3)
        & (channel[:, None] == slot[None] % channels)
    )
    row = np.arange(3 * involved * channels * ROWS)
    offset = np.array(offsets)[row // (channels * ROWS) % involved]
    second = (
        (plane[None] == 1 - offset[:, None])
        & (tap_z[None] == row[:, None] // (involved * channels * ROWS))
        & (channel[None] == row[:, None] // ROWS % channels)
    )
    second = np.stack([second & (tap_y[None] == at) for at in range(3)])
    return first.astype(BF), second.astype(BF)


def dot(left, right):
    return jnp.dot(left, right, preferred_element_type=F32)


def shifted_lanes(values, step):
    length = values.shape[1]
    lane = lax.broadcasted_iota(jnp.int32, values.shape, 1)
    if step > 0:
        return jnp.where(lane == 0, 0.0, pltpu.roll(values, 1, 1))
    return jnp.where(lane == length - 1, 0.0, pltpu.roll(values, length - 1, 1))


def first_lane(on, other):
    lane = lax.broadcasted_iota(jnp.int32, on.shape, on.ndim - 1)
    return jnp.where(lane == 0, on, other)


def first_row(on, other):
    row = lax.broadcasted_iota(jnp.int32, on.shape, on.ndim - 2)
    return jnp.where(row == 0, on, other)


def other_rows(on, other):
    return other


def spread(cos_re, sin_re, cos_im, sin_im, pick):
    add_re = pick(sin_re, sin_im)
    add_im = pick(sin_im, -sin_re)
    return cos_re + add_re, cos_re - add_re, cos_im + add_im, cos_im - add_im


def folded(plus_re, minus_re, plus_im, minus_im, pick):
    sum_re, odd_re = plus_re + minus_re, plus_re - minus_re
    sum_im, odd_im = plus_im + minus_im, plus_im - minus_im
    return sum_re, pick(odd_re, -odd_im), sum_im, pick(odd_im, odd_re)


def joined(parts, axis):
    return jnp.concatenate([part.astype(BF) for part in parts], axis=axis)


def consistency_kernel(phases, width, cascade, neighbours, place_ref, base_ref, *refs):
    part_refs = refs[:neighbours]
    (
        maps_ref,
        adjoint_ref,
        mask_ref,
        pack_ref,
        table_z,
        table_zt,
        table_y,
        table_yt,
        rows_ref,
        dc_ref,
        v_ref,
        image,
        total,
        rounded,
        kz,
        kspace,
        spectrum,
        along_z,
    ) = refs[neighbours:]
    channels, length_y, length_z = base_ref.shape
    half_z = length_z // 2
    for channel in range(channels):
        value = base_ref[channel].astype(F32)
        for part in part_refs:
            value = value + part[channel].astype(F32)
        image[channel] = value
        rounded[channel] = value.astype(BF).astype(F32)
        total[channel] = -adjoint_ref[channel].astype(F32)
    row_count = rows_ref.shape[1]
    start = pl.multiple_of(place_ref[0] * row_count, row_count)
    rows_ref[...] = image[:, pl.ds(start, row_count), :]

    def multiplied(index, phase):
        parts = []
        for at in range(0, length_y, ROWS):
            rows = slice(at, at + ROWS)
            map_re = maps_ref[2 * index, rows]
            map_im = maps_ref[2 * index + 1, rows]
            image_re = rounded[2 * phase, rows]
            image_im = rounded[2 * phase + 1, rows]
            parts.append(map_re * image_re - map_im * image_im)
            parts.append(map_re * image_im + map_im * image_re)
        value = dot(joined(parts, 0), table_zt[...]).reshape(length_y // ROWS, 2, ROWS, length_z)
        kz[phase, :, :length_z] = value[:, 0].reshape(length_y, length_z).astype(BF)
        kz[phase, :, length_z:] = value[:, 1].reshape(length_y, length_z).astype(BF)

    def transformed(phase):
        kspace[phase] = dot(table_y[...], kz[phase])

    def masked(phase):
        for at in range(0, length_y, 2 * ROWS):
            upper = kspace[phase, at : at + ROWS]
            lower = kspace[phase, at + ROWS : at + 2 * ROWS]
            pick = other_rows if at else first_row
            cut = [slice(half_z * part, half_z * (part + 1)) for part in range(4)]
            even_re, odd_re, even_im, odd_im = cut
            cos = spread(
                upper[:, even_re], lower[:, even_re], upper[:, even_im], lower[:, even_im], pick
            )
            sin = spread(
                upper[:, odd_re], lower[:, odd_re], upper[:, odd_im], lower[:, odd_im], pick
            )
            sides = []
            for side in range(2):
                plus_re, minus_re, plus_im, minus_im = spread(
                    cos[side], sin[side], cos[2 + side], sin[2 + side], first_lane
                )
                rows = slice(at + side * ROWS, at + (side + 1) * ROWS)
                plus = mask_ref[phase, rows, :half_z]
                minus = mask_ref[phase, rows, half_z:]
                sides.append(
                    folded(
                        plus_re * plus, minus_re * minus, plus_im * plus, minus_im * minus,
                        first_lane,
                    )
                )
            cos = folded(sides[0][0], sides[1][0], sides[0][2], sides[1][2], pick)
            sin = folded(sides[0][1], sides[1][1], sides[0][3], sides[1][3], pick)
            spectrum[phase, at : at + 2 * ROWS, :] = jnp.concatenate(
                [
                    jnp.concatenate([cos[0], sin[0], cos[2], sin[2]], axis=1),
                    jnp.concatenate([cos[1], sin[1], cos[3], sin[3]], axis=1),
                ],
                axis=0,
            ).astype(BF)

    def returned(phase):
        value = dot(table_yt[...], spectrum[phase])
        shape = (length_y // ROWS, ROWS, length_z)
        value = jnp.stack(
            [value[:, :length_z].reshape(shape), value[:, length_z:].reshape(shape)], axis=1
        )
        along_z[phase] = value.reshape(2 * length_y, length_z).astype(BF)

    def summed(index, phase):
        back = dot(along_z[phase], table_z[...])
        for at in range(0, length_y, ROWS):
            rows = slice(at, at + ROWS)
            map_re = maps_ref[2 * index, rows]
            map_im = maps_ref[2 * index + 1, rows]
            back_re = back[2 * at : 2 * at + ROWS]
            back_im = back[2 * at + ROWS : 2 * at + 2 * ROWS]
            total[2 * phase, rows] += map_re * back_re + map_im * back_im
            total[2 * phase + 1, rows] += map_re * back_im - map_im * back_re

    coils = maps_ref.shape[0] // 2
    for phase in range(phases):
        multiplied(0, phase)
    transformed(0)
    along_z[phases - 1] = jnp.zeros(along_z.shape[1:], BF)

    def coil(index, carry):
        after = jnp.minimum(index + 1, coils - 1)
        for phase in range(phases):
            before = index if phase else jnp.maximum(index - 1, 0)
            transformed((phase + 1) % phases)
            masked(phase)
            multiplied(after, phase)
            returned(phase)
            summed(before, (phase - 1) % phases)
        return carry

    lax.fori_loop(0, coils, coil, 0)
    summed(coils - 1, phases - 1)
    step = pack_ref[cascade, 2 * width : 2 * width + 1, 1:2]
    for channel in range(channels):
        value = image[channel] - step * total[channel]
        dc_ref[channel] = value
        v_ref[channel] = value.astype(BF)


def refine_kernel(neighbours, width, cascade, place_ref, v_ref, *refs):
    other_refs = refs[:neighbours]
    dc_ref, weight1_ref, weight2_ref, base_ref = refs[neighbours : neighbours + 4]
    send_refs = refs[neighbours + 4 : 2 * neighbours + 4]
    mixed, taps, hidden = refs[2 * neighbours + 4 :]
    channels, length_y, length_z = v_ref.shape
    tiles, mixed_rows, lanes = mixed.shape
    padded = length_y + 2 * ROWS
    per_row = mixed_rows // padded
    total_blocks = length_y // ROWS
    out_rows = base_ref.shape[1]
    if out_rows == length_y:
        first_block, out_block, blocks = 0, 0, total_blocks
    else:
        wanted = out_rows // ROWS + 2
        blocks = min(total_blocks, -(-wanted // UNROLL) * UNROLL)
        out_block = place_ref[0] * (out_rows // ROWS)
        first_block = jnp.clip(out_block - 1, 0, total_blocks - blocks)

    for tile in range(tiles):
        mixed[tile, 0:per_row, :] = jnp.zeros((per_row, lanes), F32)
        tail = (length_y + 1) * per_row
        mixed[tile, tail:, :] = jnp.zeros((mixed_rows - tail, lanes), F32)
    hidden[0:width, :] = jnp.zeros((width, length_z), BF)
    hidden[(length_y + 1) * width :, :] = jnp.zeros((width, length_z), BF)
    sources = [v_ref, *other_refs]
    for at in range(per_row):
        plane, channel = divmod(at, channels)
        if plane < len(sources):
            value = sources[plane][channel].astype(F32)
        else:
            value = jnp.zeros((length_y, length_z), F32)
        for tile in range(tiles):
            mixed[tile, pl.ds(per_row + at, length_y, stride=per_row), :] = value[
                :, tile * lanes : (tile + 1) * lanes
            ]

    group = 2 * ROWS

    def build(block, carry):
        start = pl.multiple_of(block * (group * per_row), group * per_row)
        window = jnp.concatenate(
            [mixed[tile, pl.ds(start, group * per_row), :] for tile in range(tiles)], axis=1
        )
        shape = (group, per_row, length_z)
        value = jnp.stack(
            [
                shifted_lanes(window, 1).reshape(shape),
                window.reshape(shape),
                shifted_lanes(window, -1).reshape(shape),
            ],
            axis=1,
        )
        store = pl.multiple_of(block * (group * 3 * per_row), group * 3 * per_row)
        taps[pl.ds(store, group * 3 * per_row), :] = value.reshape(-1, length_z).astype(BF)
        return carry

    builds = min(padded // group, blocks * ROWS // group + 2)
    if builds == padded // group:
        build_at = 0
    else:
        build_at = jnp.minimum(first_block * ROWS // group, padded // group - builds)
    skewed = out_rows == length_y and blocks // UNROLL > 2
    per_group = UNROLL * ROWS // group
    early = 2 * per_group + per_group + 1
    lax.fori_loop(build_at, build_at + (early if skewed else builds), build, 0)
    spare = weight1_ref.shape[2] - (ROWS + 2) * 3 * per_row
    ones_row = lax.broadcasted_iota(jnp.int32, (spare, length_z), 0)
    ones = jnp.where(ones_row < 3, 1.0, 0.0).astype(BF)

    def first(block, carry):
        for part in range(UNROLL):
            at = first_block + block * UNROLL + part
            start = pl.multiple_of(at * (ROWS * 3 * per_row), ROWS * 3 * per_row)
            window = jnp.concatenate(
                [taps[pl.ds(start, (ROWS + 2) * 3 * per_row), :], ones], axis=0
            )
            value = dot(weight1_ref[cascade], window)
            store = pl.multiple_of((at * ROWS + 1) * width, width)
            hidden[pl.ds(store, ROWS * width), :] = jnp.maximum(value, 0.0).astype(BF)
        return carry

    lax.fori_loop(0, 2 if skewed else blocks // UNROLL, first, 0)
    block_rows = channels * ROWS
    unroll = min(UNROLL, out_rows // ROWS)
    span = unroll * ROWS

    def second(block, carry):
        results = []
        for part in range(unroll):
            at = out_block + block * unroll + part
            start = pl.multiple_of(at * (ROWS * width), ROWS * width)
            parts = dot(weight2_ref[cascade], hidden[pl.ds(start, (ROWS + 2) * width), :])
            third = parts.shape[0] // 3
            results.append(
                shifted_lanes(parts[:third], 1)
                + parts[third : 2 * third]
                + shifted_lanes(parts[2 * third :], -1)
            )
        rows = pl.ds(pl.multiple_of(block * span, span), span)
        from_rows = pl.ds(pl.multiple_of(out_block * ROWS + block * span, ROWS * 2), span)
        for plane in range(neighbours + 1):
            for channel in range(channels):
                lo = plane * block_rows + channel * ROWS
                value = jnp.concatenate([piece[lo : lo + ROWS] for piece in results], axis=0)
                if plane == 0:
                    base_ref[channel, rows, :] = dc_ref[channel, from_rows, :] + value
                else:
                    send_refs[plane - 1][channel, rows, :] = value.astype(BF)
        return carry

    def both(block, carry):
        second(block - 2, 0)
        first(block, 0)
        for part in range(per_group):
            at = (block + 1) * per_group + 1 + part
            build(jnp.minimum(at, padded // group - 1), 0)
        return carry

    if skewed:
        lax.fori_loop(2, blocks // UNROLL, both, 0)
        lax.fori_loop(blocks // UNROLL - 2, blocks // UNROLL, second, 0)
    else:
        lax.fori_loop(0, out_rows // span, second, 0)


def prepare_kernel(
    width,
    per_row,
    place_ref,
    pack_ref,
    bits_ref,
    columns_ref,
    order_ref,
    select1_ref,
    select2_ref,
    weight1_ref,
    weight2_ref,
    mask_ref,
):
    phases, length_y, length_z = mask_ref.shape
    for phase in range(phases):
        bits = bits_ref[phase]
        chosen = jnp.zeros((length_y, length_z), jnp.int32)
        for word in range(bits.shape[1]):
            chosen = jnp.where(columns_ref[0:1] == word, bits[:, word : word + 1], chosen)
        shift = jnp.broadcast_to(columns_ref[1:2], chosen.shape)
        taken = lax.shift_right_logical(chosen, shift) & 1
        mask_ref[phase] = dot(order_ref[...], taken.astype(F32).astype(BF))

    variant = place_ref[1] if select1_ref.shape[0] > 1 else 0
    count = select1_ref.shape[1]
    for cascade in range(pack_ref.shape[0]):
        small1 = pack_ref[cascade, :width, :count].astype(BF)
        small2 = pack_ref[cascade, width : 2 * width, :count].astype(BF)
        bias = pack_ref[cascade, 2 * width :, 0:1]
        terms = []
        for _ in range(3):
            terms.append(bias.astype(BF).astype(F32))
            bias = bias - terms[-1]
        base = dot(small1, select1_ref[variant])
        column = lax.broadcasted_iota(jnp.int32, base.shape, 1)
        step = per_row
        for row in range(ROWS):
            value = base if row == 0 else pltpu.roll(base, row * 3 * step, 1)
            for at, term in enumerate(terms):
                value = jnp.where(column == (ROWS + 2) * 3 * step + at, term, value)
            weight1_ref[cascade, row * width : (row + 1) * width, :] = value.astype(BF)
        repeated = jnp.concatenate([small2] * (ROWS + 2), axis=0)
        shape = weight2_ref.shape[1:]
        column = lax.broadcasted_iota(jnp.int32, shape, 1)
        lower = (lax.broadcasted_iota(jnp.int32, shape, 0) & (ROWS - 1)) * width
        value = jnp.zeros(shape, F32)
        for tap in range(3):
            placed = lax.dot_general(
                select2_ref[variant, tap],
                repeated,
                (((1,), (1,)), ((), ())),
                preferred_element_type=F32,
            )
            low = lower + tap * width
            value = jnp.where((column >= low) & (column < low + width), placed, value)
        weight2_ref[cascade] = value.astype(BF)


def assemble_kernel(members, spaces, steps, place_ref, local_ref, *refs):
    block_refs = refs[: len(steps) * members]
    out_refs = refs[len(steps) * members :]
    rows = local_ref.shape[2]

    def put(owner, at, block):
        where = pl.ds(pl.multiple_of(at * rows, rows), rows)
        taken = 0
        for out_ref in out_refs:
            size = out_ref.shape[0] // members
            for index in range(size):
                out_ref[owner * size + index, where, :] = block[taken + index].astype(out_ref.dtype)
            taken += size

    for member in range(members):
        put(member, place_ref[0], local_ref[member])
    for turn, step in enumerate(steps):
        at = lax.rem(place_ref[0] - step + spaces, spaces)
        for offset in range(members):
            owner = lax.rem(place_ref[2] + offset, members)
            put(owner, at, block_refs[turn * members + offset])


def ring(value, axis, step):
    count = lax.axis_size(axis)
    return lax.ppermute(value, axis, [(i, (i + step) % count) for i in range(count)])


def gathered(value, axis):
    count = lax.axis_size(axis)
    index = lax.axis_index(axis)
    whole = jnp.zeros((count,) + value.shape, value.dtype)
    for step in range(count):
        block = ring(value, axis, step) if step else value
        whole = lax.dynamic_update_index_in_dim(whole, block, (index - step) % count, 0)
    return whole


def per_device(image, sens, adjoint, mask_bits, step_size, conv1_w, conv1_b, conv2_w):
    channels, slab_count, _, row_count, length_z = image.shape
    phases, length_y = mask_bits.shape[:2]
    planes = lax.axis_size("coil")
    coil_local = sens.shape[0]
    width = conv1_w.shape[1]
    groups = lax.axis_size("group")
    members = lax.axis_size("member")
    cascades = groups * members
    group = lax.axis_index("group")
    member = lax.axis_index("member")
    plane = lax.axis_index("coil")
    section = group * members + member
    table_z = half_tables(length_z)
    alternate = np.arange(length_y).reshape(2, -1, ROWS).swapaxes(0, 1).reshape(-1)
    table_y = half_tables(length_y)[alternate]
    tables = tuple(jnp.asarray(value) for value in (table_z, table_z.T, table_y, table_y.T))
    count = conv1_w.shape[2]
    extra = jnp.concatenate(
        [conv1_b.T, jnp.broadcast_to(step_size.reshape(1, 1), (width, 1))], axis=1
    )
    packed = jnp.concatenate(
        [
            jnp.pad(part, ((0, 0), (0, -(-count // LANES) * LANES - part.shape[1])))
            for part in (conv1_w[0].astype(F32), conv2_w[0].astype(F32), extra)
        ],
        axis=0,
    )
    packed = gathered(gathered(packed, "member"), "group")
    packed = packed.reshape((cascades,) + packed.shape[2:])

    if planes == 1:
        sides, variants = [], [[0]]
    elif planes == 2:
        sides, variants = [None], [[0, 1], [0, -1]]
    else:
        sides, variants = [-1, 1], [[0, -1, 1]]
    neighbours = len(sides)
    involved = neighbours + 1
    per_row = -(-(involved * channels) // 8) * 8
    chosen = [tap_selectors(channels, per_row, offsets) for offsets in variants]
    select1, select2 = (jnp.asarray(np.stack(parts)) for parts in zip(*chosen))

    place = jnp.stack([lax.axis_index("space"), plane, member]).astype(jnp.int32)
    spaces = lax.axis_size("space")
    slab_sens = lax.dynamic_index_in_dim(sens, group, 1, keepdims=False)
    own_image = lax.dynamic_index_in_dim(image, group, 1, keepdims=False)[:, 0].astype(BF)
    own_adjoint = lax.dynamic_index_in_dim(adjoint, group, 1, keepdims=False)[:, 0].astype(BF)
    if planes == 2:
        own = lax.dynamic_index_in_dim(slab_sens, plane, 1, keepdims=False)
        sent = lax.dynamic_index_in_dim(slab_sens, 1 - plane, 1, keepdims=False)
        maps = jnp.concatenate([own, ring(sent, "coil", 1)], axis=0)
    else:
        maps = lax.all_to_all(slab_sens, "coil", split_axis=1, concat_axis=0, tiled=True)[:, 0]
    coils = maps.shape[0]
    maps = maps.reshape(coils, row_count, 2, length_z).transpose(0, 2, 1, 3)
    shared = members if phases % members == 0 and coils % members == 0 else 1
    steps = sorted(range(1, spaces), key=lambda step: min(step, spaces - step))

    def joined_rows(parts, dtypes):
        local = jnp.concatenate(
            [part.reshape(shared, -1, row_count, length_z) for part in parts], axis=1
        )
        mine = lax.dynamic_index_in_dim(local, member % shared, 0, keepdims=False)
        blocks = []
        for step in steps:
            block = ring(mine, "space", step)
            blocks.append(block)
            for offset in range(1, shared):
                blocks.append(ring(block, "member", -offset))
        return pl.pallas_call(
            functools.partial(assemble_kernel, shared, spaces, steps),
            out_shape=tuple(
                jax.ShapeDtypeStruct((part.shape[0], length_y, length_z), dtype)
                for part, dtype in zip(parts, dtypes)
            ),
            in_specs=[smem] + [vmem] * (1 + len(blocks)),
            out_specs=(vmem,) * len(parts),
            compiler_params=params,
        )(place, local, *blocks)

    full = jax.ShapeDtypeStruct((channels, length_y, length_z), F32)
    half = jax.ShapeDtypeStruct((channels, length_y, length_z), BF)
    vmem = pl.BlockSpec(memory_space=pltpu.VMEM)
    smem = pl.BlockSpec(memory_space=pltpu.SMEM)
    params = pltpu.CompilerParams(vmem_limit_bytes=32 * 1024 * 1024)
    base, target = joined_rows([own_image, own_adjoint], [BF, BF])
    (maps,) = joined_rows([maps.reshape(2 * coils, row_count, length_z)], [F32])
    order = np.eye(length_y)[slot_order(length_y)[alternate]].astype(BF)
    column = slot_order(length_z)
    columns = np.stack([column // 30, column % 30]).astype(np.int32)
    weight1, weight2, sampled = pl.pallas_call(
        functools.partial(prepare_kernel, width, per_row),
        out_shape=(
            jax.ShapeDtypeStruct((cascades, ROWS * width, select1.shape[2]), BF),
            jax.ShapeDtypeStruct((cascades, select2.shape[2], (ROWS + 2) * width), BF),
            jax.ShapeDtypeStruct((phases, length_y, length_z), F32),
        ),
        in_specs=[smem] + [vmem] * 6,
        out_specs=(vmem,) * 3,
        compiler_params=params,
    )(place, packed, mask_bits, jnp.asarray(columns), jnp.asarray(order), select1, select2)

    rows_shape = jax.ShapeDtypeStruct((channels, row_count, length_z), F32)

    def consistency(cascade, base, parts):
        return pl.pallas_call(
            functools.partial(consistency_kernel, phases, width, cascade, len(parts)),
            out_shape=(rows_shape, full, half),
            in_specs=[smem] + [vmem] * (9 + len(parts)),
            out_specs=(vmem, vmem, vmem),
            scratch_shapes=[pltpu.VMEM((channels, length_y, length_z), F32)] * 3
            + [pltpu.VMEM((phases, length_y, 2 * length_z), dtype) for dtype in (BF, F32, BF)]
            + [pltpu.VMEM((phases, 2 * length_y, length_z), BF)],
            compiler_params=params,
        )(place, base, *parts, maps, target, sampled, packed, *tables)

    def refine(cascade, value, others, updated):
        padded = length_y + 2 * ROWS
        height = row_count if cascade == cascades - 1 and row_count % (2 * ROWS) == 0 else length_y
        shape = (channels, height, length_z)
        return pl.pallas_call(
            functools.partial(refine_kernel, neighbours, width, cascade),
            out_shape=(jax.ShapeDtypeStruct(shape, F32),)
            + (jax.ShapeDtypeStruct(shape, BF),) * neighbours,
            in_specs=[smem] + [vmem] * (4 + neighbours),
            out_specs=(vmem,) * (1 + neighbours),
            scratch_shapes=[
                pltpu.VMEM((length_z // LANES, padded * per_row, LANES), F32),
                pltpu.VMEM((padded * 3 * per_row, length_z), BF),
                pltpu.VMEM(((length_y + 2) * width, length_z), BF),
            ],
            compiler_params=params,
        )(place, value, *others, updated, weight1, weight2)

    def exchanged(values):
        received = []
        for value, side in zip(values, sides):
            if side is None:
                pairs = [(0, 1), (1, 0)]
            else:
                pairs = [(i, i - side) for i in range(planes) if 0 <= i - side < planes]
            received.append(lax.ppermute(value, "coil", pairs))
        return received

    row_start = lax.axis_index("space") * row_count

    def own_rows(value):
        if value.shape[1] == row_count:
            return value
        return lax.dynamic_slice_in_dim(value, row_start, row_count, 1)

    results = []
    parts = []
    for cascade in range(cascades):
        rows, updated, value = consistency(cascade, base, parts)
        if cascade:
            results.append(rows)
        others = exchanged([value] * neighbours)
        base, *sends = refine(cascade, value, others, updated)
        turned = sends[::-1] if neighbours == 2 else sends
        parts = exchanged(turned)[::-1] if neighbours == 2 else exchanged(turned)
    last = own_rows(base)
    for part in parts:
        last = last + own_rows(part).astype(F32)
    results.append(last)

    def result_of(wanted):
        chosen = results[0]
        for cascade in range(1, cascades):
            chosen = jnp.where(wanted == cascade, results[cascade], chosen)
        return chosen

    output = jnp.zeros((channels, slab_count, row_count, length_z), F32)
    for step in range(groups):
        if step == 0:
            chosen = result_of(section)
        else:
            target_group = (group - step) % groups
            chosen = result_of(target_group * members + member).astype(BF)
            chosen = lax.ppermute(
                chosen, "group", [(i, (i - step) % groups) for i in range(groups)]
            ).astype(F32)
        output = lax.dynamic_update_slice_in_dim(
            output, chosen[:, None], (group + step) % groups, 1
        )
    return output[None, :, :, None]


def solution(mesh):
    sections, coils, spaces = mesh.devices.shape
    def run(image, *args):
        groups = image.shape[1]
        fine = Mesh(
            mesh.devices.reshape(groups, sections // groups, coils, spaces),
            ("group", "member", "coil", "space"),
        )
        section = ("group", "member")
        in_specs = (
            P(None, None, "coil", "space", None),
            P("coil", None, None, "space", None),
            P(None, None, "coil", "space", None),
            P(),
            P(section),
            P(section, None, None),
            P(section, None),
            P(section, None, None),
        )
        out_specs = P(section, None, None, "coil", "space", None)
        return jax.shard_map(
            per_device, mesh=fine, in_specs=in_specs, out_specs=out_specs, check_vma=False
        )(image, *args)

    return run
```

```python
import functools

import jax
import jax.numpy as jnp
import numpy as np
from jax import lax
from jax.experimental import pallas as pl
from jax.experimental.pallas import tpu as pltpu
from jax.sharding import Mesh
from jax.sharding import PartitionSpec as P

BF = jnp.bfloat16
F32 = jnp.float32
ROWS = 8
UNROLL = 4
LANES = 128


def half_tables(length):
    half = length // 2
    index = np.arange(length)
    angle = np.arange(half)[:, None] * index[None, :] % length * (2.0 * np.pi / length)
    scale = 1.0 / np.sqrt(length)
    cos = np.cos(angle) * scale
    sin = np.sin(angle) * scale
    cos[0] = np.where(index % 2 == 0, scale, 0.0)
    sin[0] = np.where(index % 2 == 0, 0.0, scale)
    return np.concatenate([cos, sin], axis=0).astype(BF)


def slot_order(length):
    half = length // 2
    slot = np.arange(length)
    return np.where(slot <= half, slot, length + half - slot)


def tap_selectors(channels, per_row, offsets):
    count = 27 * channels
    involved = len(offsets)
    used = (ROWS + 2) * 3 * per_row
    columns = -(-(used + 3) // LANES) * LANES
    tap = np.arange(count)
    plane, tap_y, tap_z, channel = (
        tap // (9 * channels),
        tap // (3 * channels) % 3,
        tap // channels % 3,
        tap % channels,
    )
    column = np.arange(columns)
    slot = column % per_row
    offset = np.array(list(offsets) + [9] * (per_row // channels + 1))[slot // channels]
    first = (
        (column[None] < 9 * per_row)
        & (plane[:, None] == 1 + offset[None])
        & (tap_y[:, None] == column[None] // (3 * per_row))
        & (tap_z[:, None] == column[None] // per_row % 3)
        & (channel[:, None] == slot[None] % channels)
    )
    row = np.arange(3 * involved * channels * ROWS)
    offset = np.array(offsets)[row // (channels * ROWS) % involved]
    second = (
        (plane[None] == 1 - offset[:, None])
        & (tap_z[None] == row[:, None] // (involved * channels * ROWS))
        & (channel[None] == row[:, None] // ROWS % channels)
    )
    second = np.stack([second & (tap_y[None] == at) for at in range(3)])
    return first.astype(BF), second.astype(BF)


def dot(left, right):
    return jnp.dot(left, right, preferred_element_type=F32)


def shifted_lanes(values, step):
    length = values.shape[1]
    lane = lax.broadcasted_iota(jnp.int32, values.shape, 1)
    if step > 0:
        return jnp.where(lane == 0, 0.0, pltpu.roll(values, 1, 1))
    return jnp.where(lane == length - 1, 0.0, pltpu.roll(values, length - 1, 1))


def first_lane(on, other):
    lane = lax.broadcasted_iota(jnp.int32, on.shape, on.ndim - 1)
    return jnp.where(lane == 0, on, other)


def first_row(on, other):
    row = lax.broadcasted_iota(jnp.int32, on.shape, on.ndim - 2)
    return jnp.where(row == 0, on, other)


def other_rows(on, other):
    return other


def spread(cos_re, sin_re, cos_im, sin_im, pick):
    add_re = pick(sin_re, sin_im)
    add_im = pick(sin_im, -sin_re)
    return cos_re + add_re, cos_re - add_re, cos_im + add_im, cos_im - add_im


def folded(plus_re, minus_re, plus_im, minus_im, pick):
    sum_re, odd_re = plus_re + minus_re, plus_re - minus_re
    sum_im, odd_im = plus_im + minus_im, plus_im - minus_im
    return sum_re, pick(odd_re, -odd_im), sum_im, pick(odd_im, odd_re)


def joined(parts, axis):
    return jnp.concatenate([part.astype(BF) for part in parts], axis=axis)


def consistency_kernel(phases, width, cascade, neighbours, place_ref, base_ref, *refs):
    part_refs = refs[:neighbours]
    (
        maps_ref,
        adjoint_ref,
        mask_ref,
        pack_ref,
        table_z,
        table_zt,
        table_y,
        table_yt,
        rows_ref,
        dc_ref,
        v_ref,
        image,
        total,
        rounded,
        kz,
        kspace,
        spectrum,
        along_z,
    ) = refs[neighbours:]
    channels, length_y, length_z = base_ref.shape
    half_z = length_z // 2
    for channel in range(channels):
        value = base_ref[channel].astype(F32)
        for part in part_refs:
            value = value + part[channel].astype(F32)
        image[channel] = value
        rounded[channel] = value.astype(BF).astype(F32)
        total[channel] = -adjoint_ref[channel].astype(F32)
    row_count = rows_ref.shape[1]
    start = pl.multiple_of(place_ref[0] * row_count, row_count)
    rows_ref[...] = image[:, pl.ds(start, row_count), :]

    def multiplied(index, phase):
        parts = []
        for at in range(0, length_y, ROWS):
            rows = slice(at, at + ROWS)
            map_re = maps_ref[2 * index, rows]
            map_im = maps_ref[2 * index + 1, rows]
            image_re = rounded[2 * phase, rows]
            image_im = rounded[2 * phase + 1, rows]
            parts.append(map_re * image_re - map_im * image_im)
            parts.append(map_re * image_im + map_im * image_re)
        value = dot(joined(parts, 0), table_zt[...]).reshape(length_y // ROWS, 2, ROWS, length_z)
        kz[phase, :, :length_z] = value[:, 0].reshape(length_y, length_z).astype(BF)
        kz[phase, :, length_z:] = value[:, 1].reshape(length_y, length_z).astype(BF)

    def transformed(phase):
        kspace[phase] = dot(table_y[...], kz[phase])

    def masked(phase):
        for at in range(0, length_y, 2 * ROWS):
            upper = kspace[phase, at : at + ROWS]
            lower = kspace[phase, at + ROWS : at + 2 * ROWS]
            pick = other_rows if at else first_row
            cut = [slice(half_z * part, half_z * (part + 1)) for part in range(4)]
            even_re, odd_re, even_im, odd_im = cut
            cos = spread(
                upper[:, even_re], lower[:, even_re], upper[:, even_im], lower[:, even_im], pick
            )
            sin = spread(
                upper[:, odd_re], lower[:, odd_re], upper[:, odd_im], lower[:, odd_im], pick
            )
            sides = []
            for side in range(2):
                plus_re, minus_re, plus_im, minus_im = spread(
                    cos[side], sin[side], cos[2 + side], sin[2 + side], first_lane
                )
                rows = slice(at + side * ROWS, at + (side + 1) * ROWS)
                plus = mask_ref[phase, rows, :half_z]
                minus = mask_ref[phase, rows, half_z:]
                sides.append(
                    folded(
                        plus_re * plus, minus_re * minus, plus_im * plus, minus_im * minus,
                        first_lane,
                    )
                )
            cos = folded(sides[0][0], sides[1][0], sides[0][2], sides[1][2], pick)
            sin = folded(sides[0][1], sides[1][1], sides[0][3], sides[1][3], pick)
            spectrum[phase, at : at + 2 * ROWS, :] = jnp.concatenate(
                [
                    jnp.concatenate([cos[0], sin[0], cos[2], sin[2]], axis=1),
                    jnp.concatenate([cos[1], sin[1], cos[3], sin[3]], axis=1),
                ],
                axis=0,
            ).astype(BF)

    def returned(phase):
        value = dot(table_yt[...], spectrum[phase])
        shape = (length_y // ROWS, ROWS, length_z)
        value = jnp.stack(
            [value[:, :length_z].reshape(shape), value[:, length_z:].reshape(shape)], axis=1
        )
        along_z[phase] = value.reshape(2 * length_y, length_z).astype(BF)

    def summed(index, phase):
        back = dot(along_z[phase], table_z[...])
        for at in range(0, length_y, ROWS):
            rows = slice(at, at + ROWS)
            map_re = maps_ref[2 * index, rows]
            map_im = maps_ref[2 * index + 1, rows]
            back_re = back[2 * at : 2 * at + ROWS]
            back_im = back[2 * at + ROWS : 2 * at + 2 * ROWS]
            total[2 * phase, rows] += map_re * back_re + map_im * back_im
            total[2 * phase + 1, rows] += map_re * back_im - map_im * back_re

    coils = maps_ref.shape[0] // 2
    for phase in range(phases):
        multiplied(0, phase)
    transformed(0)
    along_z[phases - 1] = jnp.zeros(along_z.shape[1:], BF)

    def coil(index, carry):
        after = jnp.minimum(index + 1, coils - 1)
        for phase in range(phases):
            before = index if phase else jnp.maximum(index - 1, 0)
            transformed((phase + 1) % phases)
            masked(phase)
            multiplied(after, phase)
            returned(phase)
            summed(before, (phase - 1) % phases)
        return carry

    lax.fori_loop(0, coils, coil, 0)
    summed(coils - 1, phases - 1)
    step = pack_ref[cascade, 2 * width : 2 * width + 1, 1:2]
    for channel in range(channels):
        value = image[channel] - step * total[channel]
        dc_ref[channel] = value
        v_ref[channel] = value.astype(BF)


def refine_kernel(neighbours, width, cascade, place_ref, v_ref, *refs):
    other_refs = refs[:neighbours]
    dc_ref, weight1_ref, weight2_ref, base_ref = refs[neighbours : neighbours + 4]
    send_refs = refs[neighbours + 4 : 2 * neighbours + 4]
    mixed, taps, hidden = refs[2 * neighbours + 4 :]
    channels, length_y, length_z = v_ref.shape
    tiles, mixed_rows, lanes = mixed.shape
    padded = length_y + 2 * ROWS
    per_row = mixed_rows // padded
    total_blocks = length_y // ROWS
    out_rows = base_ref.shape[1]
    if out_rows == length_y:
        first_block, out_block, blocks = 0, 0, total_blocks
    else:
        wanted = out_rows // ROWS + 2
        blocks = min(total_blocks, -(-wanted // UNROLL) * UNROLL)
        out_block = place_ref[0] * (out_rows // ROWS)
        first_block = jnp.clip(out_block - 1, 0, total_blocks - blocks)

    for tile in range(tiles):
        mixed[tile, 0:per_row, :] = jnp.zeros((per_row, lanes), F32)
        tail = (length_y + 1) * per_row
        mixed[tile, tail:, :] = jnp.zeros((mixed_rows - tail, lanes), F32)
    hidden[0:width, :] = jnp.zeros((width, length_z), BF)
    hidden[(length_y + 1) * width :, :] = jnp.zeros((width, length_z), BF)
    sources = [v_ref, *other_refs]
    for at in range(per_row):
        plane, channel = divmod(at, channels)
        if plane < len(sources):
            value = sources[plane][channel].astype(F32)
        else:
            value = jnp.zeros((length_y, length_z), F32)
        for tile in range(tiles):
            mixed[tile, pl.ds(per_row + at, length_y, stride=per_row), :] = value[
                :, tile * lanes : (tile + 1) * lanes
            ]

    group = 2 * ROWS

    def build(block, carry):
        start = pl.multiple_of(block * (group * per_row), group * per_row)
        window = jnp.concatenate(
            [mixed[tile, pl.ds(start, group * per_row), :] for tile in range(tiles)], axis=1
        )
        shape = (group, per_row, length_z)
        value = jnp.stack(
            [
                shifted_lanes(window, 1).reshape(shape),
                window.reshape(shape),
                shifted_lanes(window, -1).reshape(shape),
            ],
            axis=1,
        )
        store = pl.multiple_of(block * (group * 3 * per_row), group * 3 * per_row)
        taps[pl.ds(store, group * 3 * per_row), :] = value.reshape(-1, length_z).astype(BF)
        return carry

    builds = min(padded // group, blocks * ROWS // group + 2)
    if builds == padded // group:
        build_at = 0
    else:
        build_at = jnp.minimum(first_block * ROWS // group, padded // group - builds)
    skewed = out_rows == length_y and blocks // UNROLL > 2
    per_group = UNROLL * ROWS // group
    early = 2 * per_group + per_group + 1
    lax.fori_loop(build_at, build_at + (early if skewed else builds), build, 0)
    spare = weight1_ref.shape[2] - (ROWS + 2) * 3 * per_row
    ones_row = lax.broadcasted_iota(jnp.int32, (spare, length_z), 0)
    ones = jnp.where(ones_row < 3, 1.0, 0.0).astype(BF)

    def first(block, carry):
        for part in range(UNROLL):
            at = first_block + block * UNROLL + part
            start = pl.multiple_of(at * (ROWS * 3 * per_row), ROWS * 3 * per_row)
            window = jnp.concatenate(
                [taps[pl.ds(start, (ROWS + 2) * 3 * per_row), :], ones], axis=0
            )
            value = dot(weight1_ref[cascade], window)
            store = pl.multiple_of((at * ROWS + 1) * width, width)
            hidden[pl.ds(store, ROWS * width), :] = jnp.maximum(value, 0.0).astype(BF)
        return carry

    lax.fori_loop(0, 2 if skewed else blocks // UNROLL, first, 0)
    block_rows = channels * ROWS
    unroll = min(UNROLL, out_rows // ROWS)
    span = unroll * ROWS

    def second(block, carry):
        results = []
        for part in range(unroll):
            at = out_block + block * unroll + part
            start = pl.multiple_of(at * (ROWS * width), ROWS * width)
            parts = dot(weight2_ref[cascade], hidden[pl.ds(start, (ROWS + 2) * width), :])
            third = parts.shape[0] // 3
            results.append(
                shifted_lanes(parts[:third], 1)
                + parts[third : 2 * third]
                + shifted_lanes(parts[2 * third :], -1)
            )
        rows = pl.ds(pl.multiple_of(block * span, span), span)
        from_rows = pl.ds(pl.multiple_of(out_block * ROWS + block * span, ROWS * 2), span)
        for plane in range(neighbours + 1):
            for channel in range(channels):
                lo = plane * block_rows + channel * ROWS
                value = jnp.concatenate([piece[lo : lo + ROWS] for piece in results], axis=0)
                if plane == 0:
                    base_ref[channel, rows, :] = dc_ref[channel, from_rows, :] + value
                else:
                    send_refs[plane - 1][channel, rows, :] = value.astype(BF)
        return carry

    def both(block, carry):
        second(block - 2, 0)
        first(block, 0)
        for part in range(per_group):
            at = (block + 1) * per_group + 1 + part
            build(jnp.minimum(at, padded // group - 1), 0)
        return carry

    if skewed:
        lax.fori_loop(2, blocks // UNROLL, both, 0)
        lax.fori_loop(blocks // UNROLL - 2, blocks // UNROLL, second, 0)
    else:
        lax.fori_loop(0, out_rows // span, second, 0)


def prepare_kernel(
    width,
    per_row,
    place_ref,
    pack_ref,
    bits_ref,
    columns_ref,
    order_ref,
    select1_ref,
    select2_ref,
    weight1_ref,
    weight2_ref,
    mask_ref,
):
    phases, length_y, length_z = mask_ref.shape
    for phase in range(phases):
        bits = bits_ref[phase]
        chosen = jnp.zeros((length_y, length_z), jnp.int32)
        for word in range(bits.shape[1]):
            chosen = jnp.where(columns_ref[0:1] == word, bits[:, word : word + 1], chosen)
        shift = jnp.broadcast_to(columns_ref[1:2], chosen.shape)
        taken = lax.shift_right_logical(chosen, shift) & 1
        mask_ref[phase] = dot(order_ref[...], taken.astype(F32).astype(BF))

    variant = place_ref[1] if select1_ref.shape[0] > 1 else 0
    count = select1_ref.shape[1]
    for cascade in range(pack_ref.shape[0]):
        small1 = pack_ref[cascade, :width, :count].astype(BF)
        small2 = pack_ref[cascade, width : 2 * width, :count].astype(BF)
        bias = pack_ref[cascade, 2 * width :, 0:1]
        terms = []
        for _ in range(3):
            terms.append(bias.astype(BF).astype(F32))
            bias = bias - terms[-1]
        base = dot(small1, select1_ref[variant])
        column = lax.broadcasted_iota(jnp.int32, base.shape, 1)
        step = per_row
        for row in range(ROWS):
            value = base if row == 0 else pltpu.roll(base, row * 3 * step, 1)
            for at, term in enumerate(terms):
                value = jnp.where(column == (ROWS + 2) * 3 * step + at, term, value)
            weight1_ref[cascade, row * width : (row + 1) * width, :] = value.astype(BF)
        repeated = jnp.concatenate([small2] * (ROWS + 2), axis=0)
        shape = weight2_ref.shape[1:]
        column = lax.broadcasted_iota(jnp.int32, shape, 1)
        lower = (lax.broadcasted_iota(jnp.int32, shape, 0) & (ROWS - 1)) * width
        value = jnp.zeros(shape, F32)
        for tap in range(3):
            placed = lax.dot_general(
                select2_ref[variant, tap],
                repeated,
                (((1,), (1,)), ((), ())),
                preferred_element_type=F32,
            )
            low = lower + tap * width
            value = jnp.where((column >= low) & (column < low + width), placed, value)
        weight2_ref[cascade] = value.astype(BF)


def assemble_kernel(members, spaces, steps, place_ref, local_ref, *refs):
    block_refs = refs[: len(steps) * members]
    out_refs = refs[len(steps) * members :]
    rows = local_ref.shape[2]

    def put(owner, at, block):
        where = pl.ds(pl.multiple_of(at * rows, rows), rows)
        taken = 0
        for out_ref in out_refs:
            size = out_ref.shape[0] // members
            for index in range(size):
                out_ref[owner * size + index, where, :] = block[taken + index].astype(out_ref.dtype)
            taken += size

    for member in range(members):
        put(member, place_ref[0], local_ref[member])
    for turn, step in enumerate(steps):
        at = lax.rem(place_ref[0] - step + spaces, spaces)
        for offset in range(members):
            owner = lax.rem(place_ref[2] + offset, members)
            put(owner, at, block_refs[turn * members + offset])


def ring(value, axis, step):
    count = lax.axis_size(axis)
    return lax.ppermute(value, axis, [(i, (i + step) % count) for i in range(count)])


def gathered(value, axis):
    count = lax.axis_size(axis)
    index = lax.axis_index(axis)
    whole = jnp.zeros((count,) + value.shape, value.dtype)
    for step in range(count):
        block = ring(value, axis, step) if step else value
        whole = lax.dynamic_update_index_in_dim(whole, block, (index - step) % count, 0)
    return whole


def per_device(image, sens, adjoint, mask_bits, step_size, conv1_w, conv1_b, conv2_w):
    channels, slab_count, _, row_count, length_z = image.shape
    phases, length_y = mask_bits.shape[:2]
    planes = lax.axis_size("coil")
    coil_local = sens.shape[0]
    width = conv1_w.shape[1]
    groups = lax.axis_size("group")
    members = lax.axis_size("member")
    cascades = groups * members
    group = lax.axis_index("group")
    member = lax.axis_index("member")
    plane = lax.axis_index("coil")
    section = group * members + member
    table_z = half_tables(length_z)
    alternate = np.arange(length_y).reshape(2, -1, ROWS).swapaxes(0, 1).reshape(-1)
    table_y = half_tables(length_y)[alternate]
    tables = tuple(jnp.asarray(value) for value in (table_z, table_z.T, table_y, table_y.T))
    count = conv1_w.shape[2]

    if planes == 1:
        sides, variants = [], [[0]]
    elif planes == 2:
        sides, variants = [None], [[0, 1], [0, -1]]
    else:
        sides, variants = [-1, 1], [[0, -1, 1]]
    neighbours = len(sides)
    involved = neighbours + 1
    per_row = -(-(involved * channels) // 8) * 8
    chosen = [tap_selectors(channels, per_row, offsets) for offsets in variants]
    select1, select2 = (jnp.asarray(np.stack(parts)) for parts in zip(*chosen))

    place = jnp.stack([lax.axis_index("space"), plane, member]).astype(jnp.int32)
    spaces = lax.axis_size("space")
    if planes == 2:
        sent = lax.dynamic_slice(
            sens, (0, group, 1 - plane, 0, 0), (coil_local, 1, 1) + sens.shape[3:]
        )[:, 0, 0]
        received = ring(sent, "coil", 1)
        own = lax.dynamic_slice(
            sens, (0, group, plane, 0, 0), (coil_local, 1, 1) + sens.shape[3:]
        )[:, 0, 0]
    else:
        slab_sens = lax.dynamic_index_in_dim(sens, group, 1, keepdims=False)
        sent = slab_sens
        received = lax.all_to_all(sent, "coil", split_axis=1, concat_axis=0, tiled=True)[:, 0]
        own = received[:0]
    image, adjoint, sent = lax.optimization_barrier((image, adjoint, sent))
    own_image = lax.dynamic_index_in_dim(image, group, 1, keepdims=False)[:, 0].astype(BF)
    own_adjoint = lax.dynamic_index_in_dim(adjoint, group, 1, keepdims=False)[:, 0].astype(BF)
    coils = own.shape[0] + received.shape[0]
    shared = members if phases % members == 0 and coils % members == 0 else 1
    steps = sorted(range(1, spaces), key=lambda step: min(step, spaces - step))

    def shares(parts):
        local = jnp.concatenate(
            [part.reshape(shared, -1, row_count, length_z) for part in parts], axis=1
        )
        return local, lax.dynamic_index_in_dim(local, member % shared, 0, keepdims=False)

    def sent_blocks(mine):
        blocks = []
        for step in steps:
            if blocks and 2 * step == spaces:
                mine, blocks[0] = lax.optimization_barrier((mine, blocks[0]))
            block = ring(mine, "space", step)
            blocks.append(block)
        return blocks

    def traded(blocks):
        pairs = []
        for block in blocks:
            pairs.append(block)
            for offset in range(1, shared):
                pairs.append(ring(block, "member", -offset))
        return pairs

    def put_together(local, blocks, sizes, dtypes):
        return pl.pallas_call(
            functools.partial(assemble_kernel, shared, spaces, steps),
            out_shape=tuple(
                jax.ShapeDtypeStruct((size, length_y, length_z), dtype)
                for size, dtype in zip(sizes, dtypes)
            ),
            in_specs=[smem] + [vmem] * (1 + len(blocks)),
            out_specs=(vmem,) * len(sizes),
            compiler_params=params,
        )(place, local, *blocks)

    local1, mine1 = shares([own_image, own_adjoint])
    blocks1 = [ring(mine1, "space", step) for step in steps]
    maps = jnp.concatenate([own, received], axis=0)
    maps = maps.reshape(coils, row_count, 2, length_z).transpose(0, 2, 1, 3)
    local2, mine2 = shares([maps.reshape(2 * coils, row_count, length_z)])
    blocks2 = sent_blocks(mine2)
    conv1_w, conv2_w, conv1_b, step_size, mine2 = lax.optimization_barrier(
        (conv1_w, conv2_w, conv1_b, step_size, mine2)
    )
    extra = jnp.concatenate(
        [conv1_b.T, jnp.broadcast_to(step_size.reshape(1, 1), (width, 1))], axis=1
    )
    packed = jnp.concatenate(
        [
            jnp.pad(part, ((0, 0), (0, -(-count // LANES) * LANES - part.shape[1])))
            for part in (conv1_w[0].astype(F32), conv2_w[0].astype(F32), extra)
        ],
        axis=0,
    )
    packed = gathered(gathered(packed, "member"), "group")
    packed = packed.reshape((cascades,) + packed.shape[2:])

    full = jax.ShapeDtypeStruct((channels, length_y, length_z), F32)
    half = jax.ShapeDtypeStruct((channels, length_y, length_z), BF)
    vmem = pl.BlockSpec(memory_space=pltpu.VMEM)
    smem = pl.BlockSpec(memory_space=pltpu.SMEM)
    params = pltpu.CompilerParams(vmem_limit_bytes=32 * 1024 * 1024)
    base, target = put_together(local1, traded(blocks1), [channels, channels], [BF, BF])
    (maps,) = put_together(local2, traded(blocks2), [2 * coils], [F32])
    order = np.eye(length_y)[slot_order(length_y)[alternate]].astype(BF)
    column = slot_order(length_z)
    columns = np.stack([column // 30, column % 30]).astype(np.int32)
    weight1, weight2, sampled = pl.pallas_call(
        functools.partial(prepare_kernel, width, per_row),
        out_shape=(
            jax.ShapeDtypeStruct((cascades, ROWS * width, select1.shape[2]), BF),
            jax.ShapeDtypeStruct((cascades, select2.shape[2], (ROWS + 2) * width), BF),
            jax.ShapeDtypeStruct((phases, length_y, length_z), F32),
        ),
        in_specs=[smem] + [vmem] * 6,
        out_specs=(vmem,) * 3,
        compiler_params=params,
    )(place, packed, mask_bits, jnp.asarray(columns), jnp.asarray(order), select1, select2)

    rows_shape = jax.ShapeDtypeStruct((channels, row_count, length_z), F32)

    def consistency(cascade, base, parts):
        return pl.pallas_call(
            functools.partial(consistency_kernel, phases, width, cascade, len(parts)),
            out_shape=(rows_shape, full, half),
            in_specs=[smem] + [vmem] * (9 + len(parts)),
            out_specs=(vmem, vmem, vmem),
            scratch_shapes=[pltpu.VMEM((channels, length_y, length_z), F32)] * 3
            + [pltpu.VMEM((phases, length_y, 2 * length_z), dtype) for dtype in (BF, F32, BF)]
            + [pltpu.VMEM((phases, 2 * length_y, length_z), BF)],
            compiler_params=params,
        )(place, base, *parts, maps, target, sampled, packed, *tables)

    def refine(cascade, value, others, updated):
        padded = length_y + 2 * ROWS
        height = row_count if cascade == cascades - 1 and row_count % (2 * ROWS) == 0 else length_y
        shape = (channels, height, length_z)
        return pl.pallas_call(
            functools.partial(refine_kernel, neighbours, width, cascade),
            out_shape=(jax.ShapeDtypeStruct(shape, F32),)
            + (jax.ShapeDtypeStruct(shape, BF),) * neighbours,
            in_specs=[smem] + [vmem] * (4 + neighbours),
            out_specs=(vmem,) * (1 + neighbours),
            scratch_shapes=[
                pltpu.VMEM((length_z // LANES, padded * per_row, LANES), F32),
                pltpu.VMEM((padded * 3 * per_row, length_z), BF),
                pltpu.VMEM(((length_y + 2) * width, length_z), BF),
            ],
            compiler_params=params,
        )(place, value, *others, updated, weight1, weight2)

    def exchanged(values):
        received = []
        for value, side in zip(values, sides):
            if side is None:
                pairs = [(0, 1), (1, 0)]
            else:
                pairs = [(i, i - side) for i in range(planes) if 0 <= i - side < planes]
            received.append(lax.ppermute(value, "coil", pairs))
        return received

    row_start = lax.axis_index("space") * row_count

    def own_rows(value):
        if value.shape[1] == row_count:
            return value
        return lax.dynamic_slice_in_dim(value, row_start, row_count, 1)

    results = []
    parts = []
    for cascade in range(cascades):
        rows, updated, value = consistency(cascade, base, parts)
        if cascade:
            results.append(rows)
        others = exchanged([value] * neighbours)
        base, *sends = refine(cascade, value, others, updated)
        turned = sends[::-1] if neighbours == 2 else sends
        parts = exchanged(turned)[::-1] if neighbours == 2 else exchanged(turned)
    last = own_rows(base)
    for part in parts:
        last = last + own_rows(part).astype(F32)
    results.append(last)

    def result_of(wanted):
        chosen = results[0]
        for cascade in range(1, cascades):
            chosen = jnp.where(wanted == cascade, results[cascade], chosen)
        return chosen

    output = jnp.zeros((channels, slab_count, row_count, length_z), F32)
    for step in range(groups):
        if step == 0:
            chosen = result_of(section)
        else:
            target_group = (group - step) % groups
            chosen = result_of(target_group * members + member).astype(BF)
            chosen = lax.ppermute(
                chosen, "group", [(i, (i - step) % groups) for i in range(groups)]
            ).astype(F32)
        output = lax.dynamic_update_slice_in_dim(
            output, chosen[:, None], (group + step) % groups, 1
        )
    return output[None, :, :, None]


def solution(mesh):
    sections, coils, spaces = mesh.devices.shape
    def run(image, *args):
        groups = image.shape[1]
        fine = Mesh(
            mesh.devices.reshape(groups, sections // groups, coils, spaces),
            ("group", "member", "coil", "space"),
        )
        section = ("group", "member")
        in_specs = (
            P(None, None, "coil", "space", None),
            P("coil", None, None, "space", None),
            P(None, None, "coil", "space", None),
            P(),
            P(section),
            P(section, None, None),
            P(section, None),
            P(section, None, None),
        )
        out_specs = P(section, None, None, "coil", "space", None)
        return jax.shard_map(
            per_device, mesh=fine, in_specs=in_specs, out_specs=out_specs, check_vma=False
        )(image, *args)

    return run
```

```python
import functools

import jax
import jax.numpy as jnp
import numpy as np
from jax import lax
from jax.experimental import pallas as pl
from jax.experimental.pallas import tpu as pltpu
from jax.sharding import Mesh
from jax.sharding import PartitionSpec as P

BF = jnp.bfloat16
F32 = jnp.float32
ROWS = 8
UNROLL = 4
LANES = 128


def half_tables(length):
    half = length // 2
    index = np.arange(length)
    angle = np.arange(half)[:, None] * index[None, :] % length * (2.0 * np.pi / length)
    scale = 1.0 / np.sqrt(length)
    cos = np.cos(angle) * scale
    sin = np.sin(angle) * scale
    cos[0] = np.where(index % 2 == 0, scale, 0.0)
    sin[0] = np.where(index % 2 == 0, 0.0, scale)
    return np.concatenate([cos, sin], axis=0).astype(BF)


def slot_order(length):
    half = length // 2
    slot = np.arange(length)
    return np.where(slot <= half, slot, length + half - slot)


def tap_selectors(channels, per_row, offsets):
    count = 27 * channels
    involved = len(offsets)
    used = (ROWS + 2) * 3 * per_row
    columns = -(-(used + 3) // LANES) * LANES
    tap = np.arange(count)
    plane, tap_y, tap_z, channel = (
        tap // (9 * channels),
        tap // (3 * channels) % 3,
        tap // channels % 3,
        tap % channels,
    )
    column = np.arange(columns)
    slot = column % per_row
    offset = np.array(list(offsets) + [9] * (per_row // channels + 1))[slot // channels]
    first = (
        (column[None] < 9 * per_row)
        & (plane[:, None] == 1 + offset[None])
        & (tap_y[:, None] == column[None] // (3 * per_row))
        & (tap_z[:, None] == column[None] // per_row % 3)
        & (channel[:, None] == slot[None] % channels)
    )
    row = np.arange(3 * involved * channels * ROWS)
    offset = np.array(offsets)[row // (channels * ROWS) % involved]
    second = (
        (plane[None] == 1 - offset[:, None])
        & (tap_z[None] == row[:, None] // (involved * channels * ROWS))
        & (channel[None] == row[:, None] // ROWS % channels)
    )
    second = np.stack([second & (tap_y[None] == at) for at in range(3)])
    return first.astype(BF), second.astype(BF)


def dot(left, right):
    return jnp.dot(left, right, preferred_element_type=F32)


def shifted_lanes(values, step):
    length = values.shape[1]
    lane = lax.broadcasted_iota(jnp.int32, values.shape, 1)
    if step > 0:
        return jnp.where(lane == 0, 0.0, pltpu.roll(values, 1, 1))
    return jnp.where(lane == length - 1, 0.0, pltpu.roll(values, length - 1, 1))


def first_lane(on, other):
    lane = lax.broadcasted_iota(jnp.int32, on.shape, on.ndim - 1)
    return jnp.where(lane == 0, on, other)


def first_row(on, other):
    row = lax.broadcasted_iota(jnp.int32, on.shape, on.ndim - 2)
    return jnp.where(row == 0, on, other)


def other_rows(on, other):
    return other


def spread(cos_re, sin_re, cos_im, sin_im, pick):
    add_re = pick(sin_re, sin_im)
    add_im = pick(sin_im, -sin_re)
    return cos_re + add_re, cos_re - add_re, cos_im + add_im, cos_im - add_im


def folded(plus_re, minus_re, plus_im, minus_im, pick):
    sum_re, odd_re = plus_re + minus_re, plus_re - minus_re
    sum_im, odd_im = plus_im + minus_im, plus_im - minus_im
    return sum_re, pick(odd_re, -odd_im), sum_im, pick(odd_im, odd_re)


def joined(parts, axis):
    return jnp.concatenate([part.astype(BF) for part in parts], axis=axis)


def window_start(index, rows, height, length):
    return jnp.clip(index * rows - (height - rows) // 2, 0, length - height)


def consistency_kernel(phases, width, cascade, neighbours, place_ref, base_ref, *refs):
    part_refs = refs[:neighbours]
    (
        maps_ref,
        adjoint_ref,
        mask_ref,
        pack_ref,
        table_z,
        table_zt,
        table_y,
        table_yt,
        rows_ref,
        dc_ref,
        v_ref,
        image,
        total,
        rounded,
        kz,
        kspace,
        spectrum,
        along_z,
    ) = refs[neighbours:]
    channels, length_y, length_z = base_ref.shape
    half_z = length_z // 2
    height = dc_ref.shape[1]
    row_count = rows_ref.shape[1]
    first_row_out = window_start(place_ref[0], row_count, height, length_y)

    def window(at, size):
        if height == length_y:
            return slice(at, at + size)
        return pl.ds(pl.multiple_of(first_row_out + at, ROWS), size)

    for channel in range(channels):
        value = base_ref[channel].astype(F32)
        for part in part_refs:
            value = value + part[channel].astype(F32)
        image[channel] = value
        rounded[channel] = value.astype(BF).astype(F32)
    total[...] = -adjoint_ref[:, window(0, height), :].astype(F32)
    start = pl.multiple_of(place_ref[0] * row_count, row_count)
    rows_ref[...] = image[:, pl.ds(start, row_count), :]

    def multiplied(index, phase):
        parts = []
        for at in range(0, length_y, ROWS):
            rows = slice(at, at + ROWS)
            map_re = maps_ref[2 * index, rows]
            map_im = maps_ref[2 * index + 1, rows]
            image_re = rounded[2 * phase, rows]
            image_im = rounded[2 * phase + 1, rows]
            parts.append(map_re * image_re - map_im * image_im)
            parts.append(map_re * image_im + map_im * image_re)
        value = dot(joined(parts, 0), table_zt[...]).reshape(length_y // ROWS, 2, ROWS, length_z)
        kz[phase, :, :length_z] = value[:, 0].reshape(length_y, length_z).astype(BF)
        kz[phase, :, length_z:] = value[:, 1].reshape(length_y, length_z).astype(BF)

    def transformed(phase):
        kspace[phase] = dot(table_y[...], kz[phase])

    def masked(phase):
        for at in range(0, length_y, 2 * ROWS):
            upper = kspace[phase, at : at + ROWS]
            lower = kspace[phase, at + ROWS : at + 2 * ROWS]
            pick = other_rows if at else first_row
            cut = [slice(half_z * part, half_z * (part + 1)) for part in range(4)]
            even_re, odd_re, even_im, odd_im = cut
            cos = spread(
                upper[:, even_re], lower[:, even_re], upper[:, even_im], lower[:, even_im], pick
            )
            sin = spread(
                upper[:, odd_re], lower[:, odd_re], upper[:, odd_im], lower[:, odd_im], pick
            )
            sides = []
            for side in range(2):
                plus_re, minus_re, plus_im, minus_im = spread(
                    cos[side], sin[side], cos[2 + side], sin[2 + side], first_lane
                )
                rows = slice(at + side * ROWS, at + (side + 1) * ROWS)
                plus = mask_ref[phase, rows, :half_z]
                minus = mask_ref[phase, rows, half_z:]
                sides.append(
                    folded(
                        plus_re * plus, minus_re * minus, plus_im * plus, minus_im * minus,
                        first_lane,
                    )
                )
            cos = folded(sides[0][0], sides[1][0], sides[0][2], sides[1][2], pick)
            sin = folded(sides[0][1], sides[1][1], sides[0][3], sides[1][3], pick)
            spectrum[phase, at : at + 2 * ROWS, :] = jnp.concatenate(
                [
                    jnp.concatenate([cos[0], sin[0], cos[2], sin[2]], axis=1),
                    jnp.concatenate([cos[1], sin[1], cos[3], sin[3]], axis=1),
                ],
                axis=0,
            ).astype(BF)

    def returned(phase):
        value = dot(table_yt[window(0, height), :], spectrum[phase])
        shape = (height // ROWS, ROWS, length_z)
        value = jnp.stack(
            [value[:, :length_z].reshape(shape), value[:, length_z:].reshape(shape)], axis=1
        )
        along_z[phase] = value.reshape(2 * height, length_z).astype(BF)

    def summed(index, phase):
        back = dot(along_z[phase], table_z[...])
        for at in range(0, height, ROWS):
            rows = slice(at, at + ROWS)
            map_re = maps_ref[2 * index, window(at, ROWS)]
            map_im = maps_ref[2 * index + 1, window(at, ROWS)]
            back_re = back[2 * at : 2 * at + ROWS]
            back_im = back[2 * at + ROWS : 2 * at + 2 * ROWS]
            total[2 * phase, rows] += map_re * back_re + map_im * back_im
            total[2 * phase + 1, rows] += map_re * back_im - map_im * back_re

    coils = maps_ref.shape[0] // 2
    for phase in range(phases):
        multiplied(0, phase)
    transformed(0)
    along_z[phases - 1] = jnp.zeros(along_z.shape[1:], BF)

    def coil(index, carry):
        after = jnp.minimum(index + 1, coils - 1)
        for phase in range(phases):
            before = index if phase else jnp.maximum(index - 1, 0)
            transformed((phase + 1) % phases)
            masked(phase)
            multiplied(after, phase)
            returned(phase)
            summed(before, (phase - 1) % phases)
        return carry

    lax.fori_loop(0, coils, coil, 0)
    summed(coils - 1, phases - 1)
    step = pack_ref[cascade, 2 * width : 2 * width + 1, 1:2]
    for channel in range(channels):
        value = image[channel, window(0, height), :] - step * total[channel]
        dc_ref[channel] = value
        v_ref[channel] = value.astype(BF)


def refine_kernel(neighbours, width, cascade, whole_rows, place_ref, v_ref, *refs):
    other_refs = refs[:neighbours]
    dc_ref, weight1_ref, weight2_ref, base_ref = refs[neighbours : neighbours + 4]
    send_refs = refs[neighbours + 4 : 2 * neighbours + 4]
    mixed, taps, hidden = refs[2 * neighbours + 4 :]
    channels, length_y, length_z = v_ref.shape
    tiles, mixed_rows, lanes = mixed.shape
    padded = length_y + 2 * ROWS
    per_row = mixed_rows // padded
    total_blocks = length_y // ROWS
    out_rows = base_ref.shape[1]
    first_block, blocks = 0, total_blocks
    out_block = 0
    if out_rows != length_y:
        start = window_start(place_ref[0], out_rows, length_y, whole_rows)
        out_block = (place_ref[0] * out_rows - start) // ROWS

    for tile in range(tiles):
        mixed[tile, 0:per_row, :] = jnp.zeros((per_row, lanes), F32)
        tail = (length_y + 1) * per_row
        mixed[tile, tail:, :] = jnp.zeros((mixed_rows - tail, lanes), F32)
    hidden[0:width, :] = jnp.zeros((width, length_z), BF)
    hidden[(length_y + 1) * width :, :] = jnp.zeros((width, length_z), BF)
    sources = [v_ref, *other_refs]
    for at in range(per_row):
        plane, channel = divmod(at, channels)
        if plane < len(sources):
            value = sources[plane][channel].astype(F32)
        else:
            value = jnp.zeros((length_y, length_z), F32)
        for tile in range(tiles):
            mixed[tile, pl.ds(per_row + at, length_y, stride=per_row), :] = value[
                :, tile * lanes : (tile + 1) * lanes
            ]

    group = 2 * ROWS

    def build(block, carry):
        start = pl.multiple_of(block * (group * per_row), group * per_row)
        window = jnp.concatenate(
            [mixed[tile, pl.ds(start, group * per_row), :] for tile in range(tiles)], axis=1
        )
        shape = (group, per_row, length_z)
        value = jnp.stack(
            [
                shifted_lanes(window, 1).reshape(shape),
                window.reshape(shape),
                shifted_lanes(window, -1).reshape(shape),
            ],
            axis=1,
        )
        store = pl.multiple_of(block * (group * 3 * per_row), group * 3 * per_row)
        taps[pl.ds(store, group * 3 * per_row), :] = value.reshape(-1, length_z).astype(BF)
        return carry

    skewed = out_rows == length_y and blocks // UNROLL > 2
    per_group = UNROLL * ROWS // group
    early = 2 * per_group + per_group + 1
    lax.fori_loop(0, early if skewed else padded // group, build, 0)
    spare = weight1_ref.shape[2] - (ROWS + 2) * 3 * per_row
    ones_row = lax.broadcasted_iota(jnp.int32, (spare, length_z), 0)
    ones = jnp.where(ones_row < 3, 1.0, 0.0).astype(BF)

    def first(block, carry):
        for part in range(UNROLL):
            at = first_block + block * UNROLL + part
            start = pl.multiple_of(at * (ROWS * 3 * per_row), ROWS * 3 * per_row)
            window = jnp.concatenate(
                [taps[pl.ds(start, (ROWS + 2) * 3 * per_row), :], ones], axis=0
            )
            value = dot(weight1_ref[cascade], window)
            store = pl.multiple_of((at * ROWS + 1) * width, width)
            hidden[pl.ds(store, ROWS * width), :] = jnp.maximum(value, 0.0).astype(BF)
        return carry

    lax.fori_loop(0, 2 if skewed else blocks // UNROLL, first, 0)
    block_rows = channels * ROWS
    unroll = min(UNROLL, out_rows // ROWS)
    span = unroll * ROWS

    def second(block, carry):
        results = []
        for part in range(unroll):
            at = out_block + block * unroll + part
            start = pl.multiple_of(at * (ROWS * width), ROWS * width)
            parts = dot(weight2_ref[cascade], hidden[pl.ds(start, (ROWS + 2) * width), :])
            third = parts.shape[0] // 3
            results.append(
                shifted_lanes(parts[:third], 1)
                + parts[third : 2 * third]
                + shifted_lanes(parts[2 * third :], -1)
            )
        rows = pl.ds(pl.multiple_of(block * span, span), span)
        from_rows = pl.ds(pl.multiple_of(out_block * ROWS + block * span, ROWS * 2), span)
        for plane in range(neighbours + 1):
            for channel in range(channels):
                lo = plane * block_rows + channel * ROWS
                value = jnp.concatenate([piece[lo : lo + ROWS] for piece in results], axis=0)
                if plane == 0:
                    base_ref[channel, rows, :] = dc_ref[channel, from_rows, :] + value
                else:
                    send_refs[plane - 1][channel, rows, :] = value.astype(BF)
        return carry

    def both(block, carry):
        second(block - 2, 0)
        first(block, 0)
        for part in range(per_group):
            at = (block + 1) * per_group + 1 + part
            build(jnp.minimum(at, padded // group - 1), 0)
        return carry

    if skewed:
        lax.fori_loop(2, blocks // UNROLL, both, 0)
        lax.fori_loop(blocks // UNROLL - 2, blocks // UNROLL, second, 0)
    else:
        lax.fori_loop(0, out_rows // span, second, 0)


def prepare_kernel(
    width,
    per_row,
    place_ref,
    pack_ref,
    bits_ref,
    columns_ref,
    order_ref,
    select1_ref,
    select2_ref,
    weight1_ref,
    weight2_ref,
    mask_ref,
):
    phases, length_y, length_z = mask_ref.shape
    for phase in range(phases):
        bits = bits_ref[phase]
        chosen = jnp.zeros((length_y, length_z), jnp.int32)
        for word in range(bits.shape[1]):
            chosen = jnp.where(columns_ref[0:1] == word, bits[:, word : word + 1], chosen)
        shift = jnp.broadcast_to(columns_ref[1:2], chosen.shape)
        taken = lax.shift_right_logical(chosen, shift) & 1
        mask_ref[phase] = dot(order_ref[...], taken.astype(F32).astype(BF))

    variant = place_ref[1] if select1_ref.shape[0] > 1 else 0
    count = select1_ref.shape[1]
    for cascade in range(pack_ref.shape[0]):
        small1 = pack_ref[cascade, :width, :count].astype(BF)
        small2 = pack_ref[cascade, width : 2 * width, :count].astype(BF)
        bias = pack_ref[cascade, 2 * width :, 0:1]
        terms = []
        for _ in range(3):
            terms.append(bias.astype(BF).astype(F32))
            bias = bias - terms[-1]
        base = dot(small1, select1_ref[variant])
        column = lax.broadcasted_iota(jnp.int32, base.shape, 1)
        step = per_row
        for row in range(ROWS):
            value = base if row == 0 else pltpu.roll(base, row * 3 * step, 1)
            for at, term in enumerate(terms):
                value = jnp.where(column == (ROWS + 2) * 3 * step + at, term, value)
            weight1_ref[cascade, row * width : (row + 1) * width, :] = value.astype(BF)
        repeated = jnp.concatenate([small2] * (ROWS + 2), axis=0)
        shape = weight2_ref.shape[1:]
        column = lax.broadcasted_iota(jnp.int32, shape, 1)
        lower = (lax.broadcasted_iota(jnp.int32, shape, 0) & (ROWS - 1)) * width
        value = jnp.zeros(shape, F32)
        for tap in range(3):
            placed = lax.dot_general(
                select2_ref[variant, tap],
                repeated,
                (((1,), (1,)), ((), ())),
                preferred_element_type=F32,
            )
            low = lower + tap * width
            value = jnp.where((column >= low) & (column < low + width), placed, value)
        weight2_ref[cascade] = value.astype(BF)


def assemble_kernel(members, spaces, steps, place_ref, local_ref, *refs):
    block_refs = refs[: len(steps) * members]
    out_refs = refs[len(steps) * members :]
    rows = local_ref.shape[2]

    def put(owner, at, block):
        where = pl.ds(pl.multiple_of(at * rows, rows), rows)
        taken = 0
        for out_ref in out_refs:
            size = out_ref.shape[0] // members
            for index in range(size):
                out_ref[owner * size + index, where, :] = block[taken + index].astype(out_ref.dtype)
            taken += size

    for member in range(members):
        put(member, place_ref[0], local_ref[member])
    for turn, step in enumerate(steps):
        at = lax.rem(place_ref[0] - step + spaces, spaces)
        for offset in range(members):
            owner = lax.rem(place_ref[2] + offset, members)
            put(owner, at, block_refs[turn * members + offset])


def ring(value, axis, step):
    count = lax.axis_size(axis)
    return lax.ppermute(value, axis, [(i, (i + step) % count) for i in range(count)])


def gathered(value, axis):
    count = lax.axis_size(axis)
    index = lax.axis_index(axis)
    whole = jnp.zeros((count,) + value.shape, value.dtype)
    for step in range(count):
        block = ring(value, axis, step) if step else value
        whole = lax.dynamic_update_index_in_dim(whole, block, (index - step) % count, 0)
    return whole


def per_device(image, sens, adjoint, mask_bits, step_size, conv1_w, conv1_b, conv2_w):
    channels, slab_count, _, row_count, length_z = image.shape
    phases, length_y = mask_bits.shape[:2]
    planes = lax.axis_size("coil")
    coil_local = sens.shape[0]
    width = conv1_w.shape[1]
    groups = lax.axis_size("group")
    members = lax.axis_size("member")
    cascades = groups * members
    group = lax.axis_index("group")
    member = lax.axis_index("member")
    plane = lax.axis_index("coil")
    section = group * members + member
    table_z = half_tables(length_z)
    alternate = np.arange(length_y).reshape(2, -1, ROWS).swapaxes(0, 1).reshape(-1)
    table_y = half_tables(length_y)[alternate]
    tables = tuple(jnp.asarray(value) for value in (table_z, table_z.T, table_y, table_y.T))
    count = conv1_w.shape[2]

    if planes == 1:
        sides, variants = [], [[0]]
    elif planes == 2:
        sides, variants = [None], [[0, 1], [0, -1]]
    else:
        sides, variants = [-1, 1], [[0, -1, 1]]
    neighbours = len(sides)
    involved = neighbours + 1
    per_row = -(-(involved * channels) // 8) * 8
    chosen = [tap_selectors(channels, per_row, offsets) for offsets in variants]
    select1, select2 = (jnp.asarray(np.stack(parts)) for parts in zip(*chosen))

    place = jnp.stack([lax.axis_index("space"), plane, member]).astype(jnp.int32)
    spaces = lax.axis_size("space")
    if planes == 2:
        sent = lax.dynamic_slice(
            sens, (0, group, 1 - plane, 0, 0), (coil_local, 1, 1) + sens.shape[3:]
        )[:, 0, 0]
        received = ring(sent, "coil", 1)
        own = lax.dynamic_slice(
            sens, (0, group, plane, 0, 0), (coil_local, 1, 1) + sens.shape[3:]
        )[:, 0, 0]
    else:
        slab_sens = lax.dynamic_index_in_dim(sens, group, 1, keepdims=False)
        sent = slab_sens
        received = lax.all_to_all(sent, "coil", split_axis=1, concat_axis=0, tiled=True)[:, 0]
        own = received[:0]
    image, adjoint, sent = lax.optimization_barrier((image, adjoint, sent))
    own_image = lax.dynamic_index_in_dim(image, group, 1, keepdims=False)[:, 0].astype(BF)
    own_adjoint = lax.dynamic_index_in_dim(adjoint, group, 1, keepdims=False)[:, 0].astype(BF)
    coils = own.shape[0] + received.shape[0]
    shared = members if phases % members == 0 and coils % members == 0 else 1
    steps = sorted(range(1, spaces), key=lambda step: min(step, spaces - step))

    def shares(parts):
        local = jnp.concatenate(
            [part.reshape(shared, -1, row_count, length_z) for part in parts], axis=1
        )
        return local, lax.dynamic_index_in_dim(local, member % shared, 0, keepdims=False)

    def sent_blocks(mine):
        blocks = []
        for step in steps:
            if blocks and 2 * step == spaces:
                mine, blocks[0] = lax.optimization_barrier((mine, blocks[0]))
            block = ring(mine, "space", step)
            blocks.append(block)
        return blocks

    def traded(blocks):
        pairs = []
        for block in blocks:
            pairs.append(block)
            for offset in range(1, shared):
                pairs.append(ring(block, "member", -offset))
        return pairs

    def put_together(local, blocks, sizes, dtypes):
        return pl.pallas_call(
            functools.partial(assemble_kernel, shared, spaces, steps),
            out_shape=tuple(
                jax.ShapeDtypeStruct((size, length_y, length_z), dtype)
                for size, dtype in zip(sizes, dtypes)
            ),
            in_specs=[smem] + [vmem] * (1 + len(blocks)),
            out_specs=(vmem,) * len(sizes),
            compiler_params=params,
        )(place, local, *blocks)

    local1, mine1 = shares([own_image, own_adjoint])
    blocks1 = [ring(mine1, "space", step) for step in steps]
    maps = jnp.concatenate([own, received], axis=0)
    maps = maps.reshape(coils, row_count, 2, length_z).transpose(0, 2, 1, 3)
    local2, mine2 = shares([maps.reshape(2 * coils, row_count, length_z)])
    blocks2 = sent_blocks(mine2)
    conv1_w, conv2_w, conv1_b, step_size, mine2 = lax.optimization_barrier(
        (conv1_w, conv2_w, conv1_b, step_size, mine2)
    )
    extra = jnp.concatenate(
        [conv1_b.T, jnp.broadcast_to(step_size.reshape(1, 1), (width, 1))], axis=1
    )
    packed = jnp.concatenate(
        [
            jnp.pad(part, ((0, 0), (0, -(-count // LANES) * LANES - part.shape[1])))
            for part in (conv1_w[0].astype(F32), conv2_w[0].astype(F32), extra)
        ],
        axis=0,
    )
    packed = gathered(gathered(packed, "member"), "group")
    packed = packed.reshape((cascades,) + packed.shape[2:])

    full = jax.ShapeDtypeStruct((channels, length_y, length_z), F32)
    half = jax.ShapeDtypeStruct((channels, length_y, length_z), BF)
    vmem = pl.BlockSpec(memory_space=pltpu.VMEM)
    smem = pl.BlockSpec(memory_space=pltpu.SMEM)
    params = pltpu.CompilerParams(vmem_limit_bytes=32 * 1024 * 1024)
    base, target = put_together(local1, traded(blocks1), [channels, channels], [BF, BF])
    (maps,) = put_together(local2, traded(blocks2), [2 * coils], [F32])
    order = np.eye(length_y)[slot_order(length_y)[alternate]].astype(BF)
    column = slot_order(length_z)
    columns = np.stack([column // 30, column % 30]).astype(np.int32)
    weight1, weight2, sampled = pl.pallas_call(
        functools.partial(prepare_kernel, width, per_row),
        out_shape=(
            jax.ShapeDtypeStruct((cascades, ROWS * width, select1.shape[2]), BF),
            jax.ShapeDtypeStruct((cascades, select2.shape[2], (ROWS + 2) * width), BF),
            jax.ShapeDtypeStruct((phases, length_y, length_z), F32),
        ),
        in_specs=[smem] + [vmem] * 6,
        out_specs=(vmem,) * 3,
        compiler_params=params,
    )(place, packed, mask_bits, jnp.asarray(columns), jnp.asarray(order), select1, select2)

    rows_shape = jax.ShapeDtypeStruct((channels, row_count, length_z), F32)

    margin = 2 * ROWS
    windowed = row_count + 2 * margin
    if row_count % margin or windowed % (UNROLL * ROWS) or windowed >= length_y:
        windowed = length_y

    def consistency(cascade, base, parts):
        height = windowed if cascade == cascades - 1 else length_y
        shape = (channels, height, length_z)
        return pl.pallas_call(
            functools.partial(consistency_kernel, phases, width, cascade, len(parts)),
            out_shape=(
                rows_shape,
                jax.ShapeDtypeStruct(shape, F32),
                jax.ShapeDtypeStruct(shape, BF),
            ),
            in_specs=[smem] + [vmem] * (9 + len(parts)),
            out_specs=(vmem, vmem, vmem),
            scratch_shapes=[
                pltpu.VMEM((channels, length_y, length_z), F32),
                pltpu.VMEM(shape, F32),
                pltpu.VMEM((channels, length_y, length_z), F32),
            ]
            + [pltpu.VMEM((phases, length_y, 2 * length_z), dtype) for dtype in (BF, F32, BF)]
            + [pltpu.VMEM((phases, 2 * height, length_z), BF)],
            compiler_params=params,
        )(place, base, *parts, maps, target, sampled, packed, *tables)

    def refine(cascade, value, others, updated):
        rows = value.shape[1]
        padded = rows + 2 * ROWS
        shape = (channels, rows if rows == length_y else row_count, length_z)
        return pl.pallas_call(
            functools.partial(refine_kernel, neighbours, width, cascade, length_y),
            out_shape=(jax.ShapeDtypeStruct(shape, F32),)
            + (jax.ShapeDtypeStruct(shape, BF),) * neighbours,
            in_specs=[smem] + [vmem] * (4 + neighbours),
            out_specs=(vmem,) * (1 + neighbours),
            scratch_shapes=[
                pltpu.VMEM((length_z // LANES, padded * per_row, LANES), F32),
                pltpu.VMEM((padded * 3 * per_row, length_z), BF),
                pltpu.VMEM(((rows + 2) * width, length_z), BF),
            ],
            compiler_params=params,
        )(place, value, *others, updated, weight1, weight2)

    def exchanged(values):
        received = []
        for value, side in zip(values, sides):
            if side is None:
                pairs = [(0, 1), (1, 0)]
            else:
                pairs = [(i, i - side) for i in range(planes) if 0 <= i - side < planes]
            received.append(lax.ppermute(value, "coil", pairs))
        return received

    row_start = lax.axis_index("space") * row_count

    def own_rows(value):
        if value.shape[1] == row_count:
            return value
        return lax.dynamic_slice_in_dim(value, row_start, row_count, 1)

    results = []
    parts = []
    for cascade in range(cascades):
        rows, updated, value = consistency(cascade, base, parts)
        if cascade:
            results.append(rows)
        others = exchanged([value] * neighbours)
        base, *sends = refine(cascade, value, others, updated)
        turned = sends[::-1] if neighbours == 2 else sends
        parts = exchanged(turned)[::-1] if neighbours == 2 else exchanged(turned)
    last = own_rows(base)
    for part in parts:
        last = last + own_rows(part).astype(F32)
    results.append(last)

    def result_of(wanted):
        chosen = results[0]
        for cascade in range(1, cascades):
            chosen = jnp.where(wanted == cascade, results[cascade], chosen)
        return chosen

    output = jnp.zeros((channels, slab_count, row_count, length_z), F32)
    for step in range(groups):
        if step == 0:
            chosen = result_of(section)
        else:
            target_group = (group - step) % groups
            chosen = result_of(target_group * members + member).astype(BF)
            chosen = lax.ppermute(
                chosen, "group", [(i, (i - step) % groups) for i in range(groups)]
            ).astype(F32)
        output = lax.dynamic_update_slice_in_dim(
            output, chosen[:, None], (group + step) % groups, 1
        )
    return output[None, :, :, None]


def solution(mesh):
    sections, coils, spaces = mesh.devices.shape
    def run(image, *args):
        groups = image.shape[1]
        fine = Mesh(
            mesh.devices.reshape(groups, sections // groups, coils, spaces),
            ("group", "member", "coil", "space"),
        )
        section = ("group", "member")
        in_specs = (
            P(None, None, "coil", "space", None),
            P("coil", None, None, "space", None),
            P(None, None, "coil", "space", None),
            P(),
            P(section),
            P(section, None, None),
            P(section, None),
            P(section, None, None),
        )
        out_specs = P(section, None, None, "coil", "space", None)
        return jax.shard_map(
            per_device, mesh=fine, in_specs=in_specs, out_specs=out_specs, check_vma=False
        )(image, *args)

    return run
```

```python
import functools

import jax
import jax.numpy as jnp
import numpy as np
from jax import lax
from jax.experimental import pallas as pl
from jax.experimental.pallas import tpu as pltpu
from jax.sharding import Mesh
from jax.sharding import PartitionSpec as P

BF = jnp.bfloat16
F32 = jnp.float32
ROWS = 8
UNROLL = 4
LANES = 128


def half_tables(length):
    half = length // 2
    index = np.arange(length)
    angle = np.arange(half)[:, None] * index[None, :] % length * (2.0 * np.pi / length)
    scale = 1.0 / np.sqrt(length)
    cos = np.cos(angle) * scale
    sin = np.sin(angle) * scale
    cos[0] = np.where(index % 2 == 0, scale, 0.0)
    sin[0] = np.where(index % 2 == 0, 0.0, scale)
    return np.concatenate([cos, sin], axis=0).astype(BF)


def slot_order(length):
    half = length // 2
    slot = np.arange(length)
    return np.where(slot <= half, slot, length + half - slot)


def tap_selectors(channels, per_row, offsets):
    count = 27 * channels
    involved = len(offsets)
    used = (ROWS + 2) * 3 * per_row
    columns = -(-(used + 3) // LANES) * LANES
    tap = np.arange(count)
    plane, tap_y, tap_z, channel = (
        tap // (9 * channels),
        tap // (3 * channels) % 3,
        tap // channels % 3,
        tap % channels,
    )
    column = np.arange(columns)
    slot = column % per_row
    offset = np.array(list(offsets) + [9] * (per_row // channels + 1))[slot // channels]
    first = (
        (column[None] < 9 * per_row)
        & (plane[:, None] == 1 + offset[None])
        & (tap_y[:, None] == column[None] // (3 * per_row))
        & (tap_z[:, None] == column[None] // per_row % 3)
        & (channel[:, None] == slot[None] % channels)
    )
    row = np.arange(3 * involved * channels * ROWS)
    offset = np.array(offsets)[row // (channels * ROWS) % involved]
    second = (
        (plane[None] == 1 - offset[:, None])
        & (tap_z[None] == row[:, None] // (involved * channels * ROWS))
        & (channel[None] == row[:, None] // ROWS % channels)
    )
    second = np.stack([second & (tap_y[None] == at) for at in range(3)])
    return first.astype(BF), second.astype(BF)


def dot(left, right):
    return jnp.dot(left, right, preferred_element_type=F32)


def shifted_lanes(values, step):
    length = values.shape[1]
    lane = lax.broadcasted_iota(jnp.int32, values.shape, 1)
    if step > 0:
        return jnp.where(lane == 0, 0.0, pltpu.roll(values, 1, 1))
    return jnp.where(lane == length - 1, 0.0, pltpu.roll(values, length - 1, 1))


def first_lane(on, other):
    lane = lax.broadcasted_iota(jnp.int32, on.shape, on.ndim - 1)
    return jnp.where(lane == 0, on, other)


def first_row(on, other):
    row = lax.broadcasted_iota(jnp.int32, on.shape, on.ndim - 2)
    return jnp.where(row == 0, on, other)


def other_rows(on, other):
    return other


def spread(cos_re, sin_re, cos_im, sin_im, pick):
    add_re = pick(sin_re, sin_im)
    add_im = pick(sin_im, -sin_re)
    return cos_re + add_re, cos_re - add_re, cos_im + add_im, cos_im - add_im


def folded(plus_re, minus_re, plus_im, minus_im, pick):
    sum_re, odd_re = plus_re + minus_re, plus_re - minus_re
    sum_im, odd_im = plus_im + minus_im, plus_im - minus_im
    return sum_re, pick(odd_re, -odd_im), sum_im, pick(odd_im, odd_re)


def joined(parts, axis):
    return jnp.concatenate([part.astype(BF) for part in parts], axis=axis)


def window_start(index, rows, height, length):
    return jnp.clip(index * rows - (height - rows) // 2, 0, length - height)


def consistency_kernel(
    phases, width, cascade, neighbours, first_coil, carried, final, place_ref, base_ref, *refs
):
    refs = list(refs)
    part_refs = [refs.pop(0) for _ in range(neighbours)]
    carried_ref = refs.pop(0) if carried else None
    maps_ref, mask_ref, table_z, table_zt, table_y, table_yt = (refs.pop(0) for _ in range(6))
    if final:
        adjoint_ref, pack_ref, rows_ref, dc_ref, v_ref, total = (refs.pop(0) for _ in range(6))
    else:
        total = refs.pop(0)
    image, rounded, kz, kspace, spectrum, along_z = refs
    channels, length_y, length_z = base_ref.shape
    half_z = length_z // 2
    height = total.shape[1]
    first_row_out = 0
    if height != length_y:
        first_row_out = window_start(place_ref[0], rows_ref.shape[1], height, length_y)

    def window(at, size):
        if height == length_y:
            return slice(at, at + size)
        return pl.ds(pl.multiple_of(first_row_out + at, ROWS), size)

    for channel in range(channels):
        value = base_ref[channel].astype(F32)
        for part in part_refs:
            value = value + part[channel].astype(F32)
        image[channel] = value
        rounded[channel] = value.astype(BF).astype(F32)
    if carried:
        begin = carried_ref[...]
    else:
        begin = jnp.zeros(total.shape, F32)
    if final:
        begin = begin - adjoint_ref[:, window(0, height), :].astype(F32)
    total[...] = begin
    if final:
        row_count = rows_ref.shape[1]
        start = pl.multiple_of(place_ref[0] * row_count, row_count)
        rows_ref[...] = image[:, pl.ds(start, row_count), :]

    def multiplied(index, phase):
        parts = []
        for at in range(0, length_y, ROWS):
            rows = slice(at, at + ROWS)
            map_re = maps_ref[2 * index, rows]
            map_im = maps_ref[2 * index + 1, rows]
            image_re = rounded[2 * phase, rows]
            image_im = rounded[2 * phase + 1, rows]
            parts.append(map_re * image_re - map_im * image_im)
            parts.append(map_re * image_im + map_im * image_re)
        value = dot(joined(parts, 0), table_zt[...]).reshape(length_y // ROWS, 2, ROWS, length_z)
        kz[phase, :, :length_z] = value[:, 0].reshape(length_y, length_z).astype(BF)
        kz[phase, :, length_z:] = value[:, 1].reshape(length_y, length_z).astype(BF)

    def transformed(phase):
        kspace[phase] = dot(table_y[...], kz[phase])

    def masked(phase):
        for at in range(0, length_y, 2 * ROWS):
            upper = kspace[phase, at : at + ROWS]
            lower = kspace[phase, at + ROWS : at + 2 * ROWS]
            pick = other_rows if at else first_row
            cut = [slice(half_z * part, half_z * (part + 1)) for part in range(4)]
            even_re, odd_re, even_im, odd_im = cut
            cos = spread(
                upper[:, even_re], lower[:, even_re], upper[:, even_im], lower[:, even_im], pick
            )
            sin = spread(
                upper[:, odd_re], lower[:, odd_re], upper[:, odd_im], lower[:, odd_im], pick
            )
            sides = []
            for side in range(2):
                plus_re, minus_re, plus_im, minus_im = spread(
                    cos[side], sin[side], cos[2 + side], sin[2 + side], first_lane
                )
                rows = slice(at + side * ROWS, at + (side + 1) * ROWS)
                plus = mask_ref[phase, rows, :half_z]
                minus = mask_ref[phase, rows, half_z:]
                sides.append(
                    folded(
                        plus_re * plus, minus_re * minus, plus_im * plus, minus_im * minus,
                        first_lane,
                    )
                )
            cos = folded(sides[0][0], sides[1][0], sides[0][2], sides[1][2], pick)
            sin = folded(sides[0][1], sides[1][1], sides[0][3], sides[1][3], pick)
            spectrum[phase, at : at + 2 * ROWS, :] = jnp.concatenate(
                [
                    jnp.concatenate([cos[0], sin[0], cos[2], sin[2]], axis=1),
                    jnp.concatenate([cos[1], sin[1], cos[3], sin[3]], axis=1),
                ],
                axis=0,
            ).astype(BF)

    def returned(phase):
        value = dot(table_yt[window(0, height), :], spectrum[phase])
        shape = (height // ROWS, ROWS, length_z)
        value = jnp.stack(
            [value[:, :length_z].reshape(shape), value[:, length_z:].reshape(shape)], axis=1
        )
        along_z[phase] = value.reshape(2 * height, length_z).astype(BF)

    def summed(index, phase):
        back = dot(along_z[phase], table_z[...])
        for at in range(0, height, ROWS):
            rows = slice(at, at + ROWS)
            map_re = maps_ref[2 * index, window(at, ROWS)]
            map_im = maps_ref[2 * index + 1, window(at, ROWS)]
            back_re = back[2 * at : 2 * at + ROWS]
            back_im = back[2 * at + ROWS : 2 * at + 2 * ROWS]
            total[2 * phase, rows] += map_re * back_re + map_im * back_im
            total[2 * phase + 1, rows] += map_re * back_im - map_im * back_re

    last_coil = maps_ref.shape[0] // 2 - 1
    for phase in range(phases):
        multiplied(first_coil, phase)
    transformed(0)
    along_z[phases - 1] = jnp.zeros(along_z.shape[1:], BF)

    def coil(index, carry):
        after = jnp.minimum(index + 1, last_coil)
        for phase in range(phases):
            before = index if phase else jnp.maximum(index - 1, first_coil)
            transformed((phase + 1) % phases)
            masked(phase)
            multiplied(after, phase)
            returned(phase)
            summed(before, (phase - 1) % phases)
        return carry

    lax.fori_loop(first_coil, last_coil + 1, coil, 0)
    summed(last_coil, phases - 1)
    if final:
        step = pack_ref[cascade, 2 * width : 2 * width + 1, 1:2]
        for channel in range(channels):
            value = image[channel, window(0, height), :] - step * total[channel]
            dc_ref[channel] = value
            v_ref[channel] = value.astype(BF)


def refine_kernel(neighbours, width, cascade, whole_rows, place_ref, v_ref, *refs):
    other_refs = refs[:neighbours]
    dc_ref, weight1_ref, weight2_ref, base_ref = refs[neighbours : neighbours + 4]
    send_refs = refs[neighbours + 4 : 2 * neighbours + 4]
    mixed, taps, hidden = refs[2 * neighbours + 4 :]
    channels, length_y, length_z = v_ref.shape
    tiles, mixed_rows, lanes = mixed.shape
    padded = length_y + 2 * ROWS
    per_row = mixed_rows // padded
    total_blocks = length_y // ROWS
    out_rows = base_ref.shape[1]
    first_block, blocks = 0, total_blocks
    out_block = 0
    if out_rows != length_y:
        start = window_start(place_ref[0], out_rows, length_y, whole_rows)
        out_block = (place_ref[0] * out_rows - start) // ROWS

    for tile in range(tiles):
        mixed[tile, 0:per_row, :] = jnp.zeros((per_row, lanes), F32)
        tail = (length_y + 1) * per_row
        mixed[tile, tail:, :] = jnp.zeros((mixed_rows - tail, lanes), F32)
    hidden[0:width, :] = jnp.zeros((width, length_z), BF)
    hidden[(length_y + 1) * width :, :] = jnp.zeros((width, length_z), BF)
    sources = [v_ref, *other_refs]
    for at in range(per_row):
        plane, channel = divmod(at, channels)
        if plane < len(sources):
            value = sources[plane][channel].astype(F32)
        else:
            value = jnp.zeros((length_y, length_z), F32)
        for tile in range(tiles):
            mixed[tile, pl.ds(per_row + at, length_y, stride=per_row), :] = value[
                :, tile * lanes : (tile + 1) * lanes
            ]

    group = 2 * ROWS

    def build(block, carry):
        start = pl.multiple_of(block * (group * per_row), group * per_row)
        window = jnp.concatenate(
            [mixed[tile, pl.ds(start, group * per_row), :] for tile in range(tiles)], axis=1
        )
        shape = (group, per_row, length_z)
        value = jnp.stack(
            [
                shifted_lanes(window, 1).reshape(shape),
                window.reshape(shape),
                shifted_lanes(window, -1).reshape(shape),
            ],
            axis=1,
        )
        store = pl.multiple_of(block * (group * 3 * per_row), group * 3 * per_row)
        taps[pl.ds(store, group * 3 * per_row), :] = value.reshape(-1, length_z).astype(BF)
        return carry

    skewed = out_rows == length_y and blocks // UNROLL > 2
    per_group = UNROLL * ROWS // group
    early = 2 * per_group + per_group + 1
    lax.fori_loop(0, early if skewed else padded // group, build, 0)
    spare = weight1_ref.shape[2] - (ROWS + 2) * 3 * per_row
    ones_row = lax.broadcasted_iota(jnp.int32, (spare, length_z), 0)
    ones = jnp.where(ones_row < 3, 1.0, 0.0).astype(BF)

    def first(block, carry):
        for part in range(UNROLL):
            at = first_block + block * UNROLL + part
            start = pl.multiple_of(at * (ROWS * 3 * per_row), ROWS * 3 * per_row)
            window = jnp.concatenate(
                [taps[pl.ds(start, (ROWS + 2) * 3 * per_row), :], ones], axis=0
            )
            value = dot(weight1_ref[cascade], window)
            store = pl.multiple_of((at * ROWS + 1) * width, width)
            hidden[pl.ds(store, ROWS * width), :] = jnp.maximum(value, 0.0).astype(BF)
        return carry

    lax.fori_loop(0, 2 if skewed else blocks // UNROLL, first, 0)
    block_rows = channels * ROWS
    unroll = min(UNROLL, out_rows // ROWS)
    span = unroll * ROWS

    def second(block, carry):
        results = []
        for part in range(unroll):
            at = out_block + block * unroll + part
            start = pl.multiple_of(at * (ROWS * width), ROWS * width)
            parts = dot(weight2_ref[cascade], hidden[pl.ds(start, (ROWS + 2) * width), :])
            third = parts.shape[0] // 3
            results.append(
                shifted_lanes(parts[:third], 1)
                + parts[third : 2 * third]
                + shifted_lanes(parts[2 * third :], -1)
            )
        rows = pl.ds(pl.multiple_of(block * span, span), span)
        from_rows = pl.ds(pl.multiple_of(out_block * ROWS + block * span, ROWS * 2), span)
        for plane in range(neighbours + 1):
            for channel in range(channels):
                lo = plane * block_rows + channel * ROWS
                value = jnp.concatenate([piece[lo : lo + ROWS] for piece in results], axis=0)
                if plane == 0:
                    base_ref[channel, rows, :] = dc_ref[channel, from_rows, :] + value
                else:
                    send_refs[plane - 1][channel, rows, :] = value.astype(BF)
        return carry

    def both(block, carry):
        second(block - 2, 0)
        first(block, 0)
        for part in range(per_group):
            at = (block + 1) * per_group + 1 + part
            build(jnp.minimum(at, padded // group - 1), 0)
        return carry

    if skewed:
        lax.fori_loop(2, blocks // UNROLL, both, 0)
        lax.fori_loop(blocks // UNROLL - 2, blocks // UNROLL, second, 0)
    else:
        lax.fori_loop(0, out_rows // span, second, 0)


def mask_kernel(bits_ref, columns_ref, order_ref, mask_ref):
    phases, length_y, length_z = mask_ref.shape
    for phase in range(phases):
        bits = bits_ref[phase]
        chosen = jnp.zeros((length_y, length_z), jnp.int32)
        for word in range(bits.shape[1]):
            chosen = jnp.where(columns_ref[0:1] == word, bits[:, word : word + 1], chosen)
        shift = jnp.broadcast_to(columns_ref[1:2], chosen.shape)
        taken = lax.shift_right_logical(chosen, shift) & 1
        mask_ref[phase] = dot(order_ref[...], taken.astype(F32).astype(BF))


def prepare_kernel(
    width, per_row, place_ref, pack_ref, select1_ref, select2_ref, weight1_ref, weight2_ref
):
    variant = place_ref[1] if select1_ref.shape[0] > 1 else 0
    count = select1_ref.shape[1]
    for cascade in range(pack_ref.shape[0]):
        small1 = pack_ref[cascade, :width, :count].astype(BF)
        small2 = pack_ref[cascade, width : 2 * width, :count].astype(BF)
        bias = pack_ref[cascade, 2 * width :, 0:1]
        terms = []
        for _ in range(3):
            terms.append(bias.astype(BF).astype(F32))
            bias = bias - terms[-1]
        base = dot(small1, select1_ref[variant])
        column = lax.broadcasted_iota(jnp.int32, base.shape, 1)
        step = per_row
        for row in range(ROWS):
            value = base if row == 0 else pltpu.roll(base, row * 3 * step, 1)
            for at, term in enumerate(terms):
                value = jnp.where(column == (ROWS + 2) * 3 * step + at, term, value)
            weight1_ref[cascade, row * width : (row + 1) * width, :] = value.astype(BF)
        repeated = jnp.concatenate([small2] * (ROWS + 2), axis=0)
        shape = weight2_ref.shape[1:]
        column = lax.broadcasted_iota(jnp.int32, shape, 1)
        lower = (lax.broadcasted_iota(jnp.int32, shape, 0) & (ROWS - 1)) * width
        value = jnp.zeros(shape, F32)
        for tap in range(3):
            placed = lax.dot_general(
                select2_ref[variant, tap],
                repeated,
                (((1,), (1,)), ((), ())),
                preferred_element_type=F32,
            )
            low = lower + tap * width
            value = jnp.where((column >= low) & (column < low + width), placed, value)
        weight2_ref[cascade] = value.astype(BF)


def assemble_kernel(members, spaces, steps, place_ref, local_ref, *refs):
    block_refs = refs[: len(steps) * members]
    out_refs = refs[len(steps) * members :]
    rows = local_ref.shape[2]

    def put(owner, at, block):
        where = pl.ds(pl.multiple_of(at * rows, rows), rows)
        taken = 0
        for out_ref in out_refs:
            size = out_ref.shape[0] // members
            for index in range(size):
                out_ref[owner * size + index, where, :] = block[taken + index].astype(out_ref.dtype)
            taken += size

    for member in range(members):
        put(member, place_ref[0], local_ref[member])
    for turn, step in enumerate(steps):
        at = lax.rem(place_ref[0] - step + spaces, spaces)
        for offset in range(members):
            owner = lax.rem(place_ref[2] + offset, members)
            put(owner, at, block_refs[turn * members + offset])


def stack_kernel(shared, spaces, steps, offsets, heads, place_ref, *refs):
    head_refs = refs[:heads]
    local_ref = refs[heads]
    block_refs = refs[heads + 1 : -1]
    out_ref = refs[-1]
    share, rows = local_ref.shape[1:3]
    base = 0
    for head_ref in head_refs:
        base = head_ref.shape[0]
        out_ref[:base] = head_ref[...]
    for turn, offset in enumerate(offsets):
        owner = lax.rem(place_ref[2] + offset, shared)
        for nth, step in enumerate((0, *steps)):
            at = lax.rem(place_ref[0] - step + spaces, spaces)
            where = pl.ds(pl.multiple_of(at * rows, rows), rows)
            for index in range(share):
                if nth:
                    block = block_refs[turn * len(steps) + nth - 1][index]
                else:
                    block = local_ref[owner, index]
                out_ref[base + turn * share + index, where, :] = block.astype(out_ref.dtype)


def ring(value, axis, step):
    count = lax.axis_size(axis)
    return lax.ppermute(value, axis, [(i, (i + step) % count) for i in range(count)])


def gathered(value, axis):
    count = lax.axis_size(axis)
    index = lax.axis_index(axis)
    whole = jnp.zeros((count,) + value.shape, value.dtype)
    for step in range(count):
        block = ring(value, axis, step) if step else value
        whole = lax.dynamic_update_index_in_dim(whole, block, (index - step) % count, 0)
    return whole


def per_device(image, sens, adjoint, mask_bits, step_size, conv1_w, conv1_b, conv2_w):
    channels, slab_count, _, row_count, length_z = image.shape
    phases, length_y = mask_bits.shape[:2]
    planes = lax.axis_size("coil")
    coil_local = sens.shape[0]
    width = conv1_w.shape[1]
    groups = lax.axis_size("group")
    members = lax.axis_size("member")
    cascades = groups * members
    group = lax.axis_index("group")
    member = lax.axis_index("member")
    plane = lax.axis_index("coil")
    section = group * members + member
    table_z = half_tables(length_z)
    alternate = np.arange(length_y).reshape(2, -1, ROWS).swapaxes(0, 1).reshape(-1)
    table_y = half_tables(length_y)[alternate]
    tables = tuple(jnp.asarray(value) for value in (table_z, table_z.T, table_y, table_y.T))
    count = conv1_w.shape[2]

    if planes == 1:
        sides, variants = [], [[0]]
    elif planes == 2:
        sides, variants = [None], [[0, 1], [0, -1]]
    else:
        sides, variants = [-1, 1], [[0, -1, 1]]
    neighbours = len(sides)
    involved = neighbours + 1
    per_row = -(-(involved * channels) // 8) * 8
    chosen = [tap_selectors(channels, per_row, offsets) for offsets in variants]
    select1, select2 = (jnp.asarray(np.stack(parts)) for parts in zip(*chosen))

    place = jnp.stack([lax.axis_index("space"), plane, member]).astype(jnp.int32)
    spaces = lax.axis_size("space")
    if planes == 2:
        sent = lax.dynamic_slice(
            sens, (0, group, 1 - plane, 0, 0), (coil_local, 1, 1) + sens.shape[3:]
        )[:, 0, 0]
        received = ring(sent, "coil", 1)
        own = lax.dynamic_slice(
            sens, (0, group, plane, 0, 0), (coil_local, 1, 1) + sens.shape[3:]
        )[:, 0, 0]
    else:
        slab_sens = lax.dynamic_index_in_dim(sens, group, 1, keepdims=False)
        sent = slab_sens
        received = lax.all_to_all(sent, "coil", split_axis=1, concat_axis=0, tiled=True)[:, 0]
        own = received[:0]
    image, adjoint, sent = lax.optimization_barrier((image, adjoint, sent))
    own_image = lax.dynamic_index_in_dim(image, group, 1, keepdims=False)[:, 0].astype(BF)
    own_adjoint = lax.dynamic_index_in_dim(adjoint, group, 1, keepdims=False)[:, 0].astype(BF)
    coils = own.shape[0] + received.shape[0]
    shared = members if phases % members == 0 and coils % members == 0 else 1
    steps = sorted(range(1, spaces), key=lambda step: min(step, spaces - step))

    def shares(parts):
        local = jnp.concatenate(
            [part.reshape(shared, -1, row_count, length_z) for part in parts], axis=1
        )
        return local, lax.dynamic_index_in_dim(local, member % shared, 0, keepdims=False)

    def sent_blocks(mine):
        blocks = []
        for step in steps:
            if blocks and 2 * step == spaces:
                mine, blocks[0] = lax.optimization_barrier((mine, blocks[0]))
            block = ring(mine, "space", step)
            blocks.append(block)
        return blocks

    def traded(blocks):
        pairs = []
        for block in blocks:
            pairs.append(block)
            for offset in range(1, shared):
                pairs.append(ring(block, "member", -offset))
        return pairs

    def put_together(local, blocks, sizes, dtypes):
        return pl.pallas_call(
            functools.partial(assemble_kernel, shared, spaces, steps),
            out_shape=tuple(
                jax.ShapeDtypeStruct((size, length_y, length_z), dtype)
                for size, dtype in zip(sizes, dtypes)
            ),
            in_specs=[smem] + [vmem] * (1 + len(blocks)),
            out_specs=(vmem,) * len(sizes),
            compiler_params=params,
        )(place, local, *blocks)

    local1, mine1 = shares([own_image, own_adjoint])
    blocks1 = [ring(mine1, "space", step) for step in steps]
    maps = jnp.concatenate([own, received], axis=0)
    maps = maps.reshape(coils, row_count, 2, length_z).transpose(0, 2, 1, 3)
    local2, mine2 = shares([maps.reshape(2 * coils, row_count, length_z)])
    blocks2 = sent_blocks(mine2)
    conv1_w, conv2_w, conv1_b, step_size, mine2 = lax.optimization_barrier(
        (conv1_w, conv2_w, conv1_b, step_size, mine2)
    )
    extra = jnp.concatenate(
        [conv1_b.T, jnp.broadcast_to(step_size.reshape(1, 1), (width, 1))], axis=1
    )
    packed = jnp.concatenate(
        [
            jnp.pad(part, ((0, 0), (0, -(-count // LANES) * LANES - part.shape[1])))
            for part in (conv1_w[0].astype(F32), conv2_w[0].astype(F32), extra)
        ],
        axis=0,
    )
    packed = gathered(gathered(packed, "member"), "group")
    packed = packed.reshape((cascades,) + packed.shape[2:])

    full = jax.ShapeDtypeStruct((channels, length_y, length_z), F32)
    half = jax.ShapeDtypeStruct((channels, length_y, length_z), BF)
    vmem = pl.BlockSpec(memory_space=pltpu.VMEM)
    smem = pl.BlockSpec(memory_space=pltpu.SMEM)
    params = pltpu.CompilerParams(vmem_limit_bytes=32 * 1024 * 1024)
    base, target = put_together(local1, traded(blocks1), [channels, channels], [BF, BF])

    def stacked(offsets, heads, pieces):
        size = local2.shape[1] * len(offsets) + sum(head.shape[0] for head in heads)
        return pl.pallas_call(
            functools.partial(stack_kernel, shared, spaces, steps, offsets, len(heads)),
            out_shape=jax.ShapeDtypeStruct((size, length_y, length_z), F32),
            in_specs=[smem] + [vmem] * (1 + len(heads) + len(pieces)),
            out_specs=vmem,
            compiler_params=params,
        )(place, *heads, local2, *pieces)

    own_maps = maps = stacked((0,), [], blocks2)
    if shared > 1:
        others = tuple(range(1, shared))
        pieces = [ring(block, "member", -offset) for offset in others for block in blocks2]
        maps = stacked(others, [own_maps], pieces)
    order = np.eye(length_y)[slot_order(length_y)[alternate]].astype(BF)
    column = slot_order(length_z)
    columns = np.stack([column // 30, column % 30]).astype(np.int32)
    sampled = pl.pallas_call(
        mask_kernel,
        out_shape=jax.ShapeDtypeStruct((phases, length_y, length_z), F32),
        in_specs=[vmem] * 3,
        out_specs=vmem,
        compiler_params=params,
    )(mask_bits, jnp.asarray(columns), jnp.asarray(order))
    weight1, weight2 = pl.pallas_call(
        functools.partial(prepare_kernel, width, per_row),
        out_shape=(
            jax.ShapeDtypeStruct((cascades, ROWS * width, select1.shape[2]), BF),
            jax.ShapeDtypeStruct((cascades, select2.shape[2], (ROWS + 2) * width), BF),
        ),
        in_specs=[smem] + [vmem] * 3,
        out_specs=(vmem,) * 2,
        compiler_params=params,
    )(place, packed, select1, select2)
    rows_shape = jax.ShapeDtypeStruct((channels, row_count, length_z), F32)

    margin = 2 * ROWS
    windowed = row_count + 2 * margin
    if row_count % margin or windowed % (UNROLL * ROWS) or windowed >= length_y:
        windowed = length_y

    def consistency(cascade, base, parts, maps, first_coil=0, carried=None, final=True):
        height = windowed if cascade == cascades - 1 else length_y
        shape = (channels, height, length_z)
        operands = [base, *parts] + ([] if carried is None else [carried])
        operands += [maps, sampled, *tables] + ([target, packed] if final else [])
        sums = jax.ShapeDtypeStruct(shape, F32)
        return pl.pallas_call(
            functools.partial(
                consistency_kernel,
                phases,
                width,
                cascade,
                len(parts),
                first_coil,
                carried is not None,
                final,
            ),
            out_shape=(rows_shape, sums, jax.ShapeDtypeStruct(shape, BF)) if final else sums,
            in_specs=[smem] + [vmem] * len(operands),
            out_specs=(vmem,) * 3 if final else vmem,
            scratch_shapes=([pltpu.VMEM(shape, F32)] if final else [])
            + [pltpu.VMEM((channels, length_y, length_z), F32)] * 2
            + [pltpu.VMEM((phases, length_y, 2 * length_z), dtype) for dtype in (BF, F32, BF)]
            + [pltpu.VMEM((phases, 2 * height, length_z), BF)],
            compiler_params=params,
        )(place, *operands)

    def refine(cascade, value, others, updated):
        rows = value.shape[1]
        padded = rows + 2 * ROWS
        shape = (channels, rows if rows == length_y else row_count, length_z)
        return pl.pallas_call(
            functools.partial(refine_kernel, neighbours, width, cascade, length_y),
            out_shape=(jax.ShapeDtypeStruct(shape, F32),)
            + (jax.ShapeDtypeStruct(shape, BF),) * neighbours,
            in_specs=[smem] + [vmem] * (4 + neighbours),
            out_specs=(vmem,) * (1 + neighbours),
            scratch_shapes=[
                pltpu.VMEM((length_z // LANES, padded * per_row, LANES), F32),
                pltpu.VMEM((padded * 3 * per_row, length_z), BF),
                pltpu.VMEM(((rows + 2) * width, length_z), BF),
            ],
            compiler_params=params,
        )(place, value, *others, updated, weight1, weight2)

    def exchanged(values):
        received = []
        for value, side in zip(values, sides):
            if side is None:
                pairs = [(0, 1), (1, 0)]
            else:
                pairs = [(i, i - side) for i in range(planes) if 0 <= i - side < planes]
            received.append(lax.ppermute(value, "coil", pairs))
        return received

    row_start = lax.axis_index("space") * row_count

    def own_rows(value):
        if value.shape[1] == row_count:
            return value
        return lax.dynamic_slice_in_dim(value, row_start, row_count, 1)

    results = []
    parts = []
    for cascade in range(cascades):
        if cascade == 0 and cascades > 1 and shared > 1:
            carried = consistency(0, base, [], own_maps, final=False)
            first_coil = own_maps.shape[0] // 2
            rows, updated, value = consistency(0, base, [], maps, first_coil, carried)
        else:
            rows, updated, value = consistency(cascade, base, parts, maps)
        if cascade:
            results.append(rows)
        others = exchanged([value] * neighbours)
        base, *sends = refine(cascade, value, others, updated)
        turned = sends[::-1] if neighbours == 2 else sends
        parts = exchanged(turned)[::-1] if neighbours == 2 else exchanged(turned)
    last = own_rows(base)
    for part in parts:
        last = last + own_rows(part).astype(F32)
    results.append(last)

    def result_of(wanted):
        chosen = results[0]
        for cascade in range(1, cascades):
            chosen = jnp.where(wanted == cascade, results[cascade], chosen)
        return chosen

    output = jnp.zeros((channels, slab_count, row_count, length_z), F32)
    for step in range(groups):
        if step == 0:
            chosen = result_of(section)
        else:
            target_group = (group - step) % groups
            chosen = result_of(target_group * members + member).astype(BF)
            chosen = lax.ppermute(
                chosen, "group", [(i, (i - step) % groups) for i in range(groups)]
            ).astype(F32)
        output = lax.dynamic_update_slice_in_dim(
            output, chosen[:, None], (group + step) % groups, 1
        )
    return output[None, :, :, None]


def solution(mesh):
    sections, coils, spaces = mesh.devices.shape
    def run(image, *args):
        groups = image.shape[1]
        fine = Mesh(
            mesh.devices.reshape(groups, sections // groups, coils, spaces),
            ("group", "member", "coil", "space"),
        )
        section = ("group", "member")
        in_specs = (
            P(None, None, "coil", "space", None),
            P("coil", None, None, "space", None),
            P(None, None, "coil", "space", None),
            P(),
            P(section),
            P(section, None, None),
            P(section, None),
            P(section, None, None),
        )
        out_specs = P(section, None, None, "coil", "space", None)
        return jax.shard_map(
            per_device, mesh=fine, in_specs=in_specs, out_specs=out_specs, check_vma=False
        )(image, *args)

    return run
```

```python
import functools

import jax
import jax.numpy as jnp
import numpy as np
from jax import lax
from jax.experimental import pallas as pl
from jax.experimental.pallas import tpu as pltpu
from jax.sharding import Mesh
from jax.sharding import PartitionSpec as P

BF = jnp.bfloat16
F32 = jnp.float32
ROWS = 8
UNROLL = 4
LANES = 128


def half_tables(length):
    half = length // 2
    index = np.arange(length)
    angle = np.arange(half)[:, None] * index[None, :] % length * (2.0 * np.pi / length)
    scale = 1.0 / np.sqrt(length)
    cos = np.cos(angle) * scale
    sin = np.sin(angle) * scale
    cos[0] = np.where(index % 2 == 0, scale, 0.0)
    sin[0] = np.where(index % 2 == 0, 0.0, scale)
    return np.concatenate([cos, sin], axis=0).astype(BF)


def slot_order(length):
    half = length // 2
    slot = np.arange(length)
    return np.where(slot <= half, slot, length + half - slot)


def tap_selectors(channels, per_row, offsets):
    count = 27 * channels
    involved = len(offsets)
    used = (ROWS + 2) * 3 * per_row
    columns = -(-(used + 3) // LANES) * LANES
    tap = np.arange(count)
    plane, tap_y, tap_z, channel = (
        tap // (9 * channels),
        tap // (3 * channels) % 3,
        tap // channels % 3,
        tap % channels,
    )
    column = np.arange(columns)
    slot = column % per_row
    offset = np.array(list(offsets) + [9] * (per_row // channels + 1))[slot // channels]
    first = (
        (column[None] < 9 * per_row)
        & (plane[:, None] == 1 + offset[None])
        & (tap_y[:, None] == column[None] // (3 * per_row))
        & (tap_z[:, None] == column[None] // per_row % 3)
        & (channel[:, None] == slot[None] % channels)
    )
    row = np.arange(3 * involved * channels * ROWS)
    offset = np.array(offsets)[row // (channels * ROWS) % involved]
    second = (
        (plane[None] == 1 - offset[:, None])
        & (tap_z[None] == row[:, None] // (involved * channels * ROWS))
        & (channel[None] == row[:, None] // ROWS % channels)
    )
    second = np.stack([second & (tap_y[None] == at) for at in range(3)])
    return first.astype(BF), second.astype(BF)


def dot(left, right):
    return jnp.dot(left, right, preferred_element_type=F32)


def shifted_lanes(values, step):
    length = values.shape[1]
    lane = lax.broadcasted_iota(jnp.int32, values.shape, 1)
    if step > 0:
        return jnp.where(lane == 0, 0.0, pltpu.roll(values, 1, 1))
    return jnp.where(lane == length - 1, 0.0, pltpu.roll(values, length - 1, 1))


def first_lane(on, other):
    lane = lax.broadcasted_iota(jnp.int32, on.shape, on.ndim - 1)
    return jnp.where(lane == 0, on, other)


def first_row(on, other):
    row = lax.broadcasted_iota(jnp.int32, on.shape, on.ndim - 2)
    return jnp.where(row == 0, on, other)


def other_rows(on, other):
    return other


def spread(cos_re, sin_re, cos_im, sin_im, pick):
    add_re = pick(sin_re, sin_im)
    add_im = pick(sin_im, -sin_re)
    return cos_re + add_re, cos_re - add_re, cos_im + add_im, cos_im - add_im


def folded(plus_re, minus_re, plus_im, minus_im, pick):
    sum_re, odd_re = plus_re + minus_re, plus_re - minus_re
    sum_im, odd_im = plus_im + minus_im, plus_im - minus_im
    return sum_re, pick(odd_re, -odd_im), sum_im, pick(odd_im, odd_re)


def joined(parts, axis):
    return jnp.concatenate([part.astype(BF) for part in parts], axis=axis)


def window_start(index, rows, height, length):
    return jnp.clip(index * rows - (height - rows) // 2, 0, length - height)


def consistency_kernel(
    phases, width, cascade, neighbours, first_coil, carried, final, place_ref, base_ref, *refs
):
    refs = list(refs)
    part_refs = [refs.pop(0) for _ in range(neighbours)]
    carried_ref = refs.pop(0) if carried else None
    maps_ref, mask_ref, table_z, table_zt, table_y, table_yt = (refs.pop(0) for _ in range(6))
    if final:
        adjoint_ref, pack_ref, rows_ref, dc_ref, v_ref, total = (refs.pop(0) for _ in range(6))
    else:
        total = refs.pop(0)
    image, rounded, kz, kspace, spectrum, along_z = refs
    channels, length_y, length_z = base_ref.shape
    half_z = length_z // 2
    height = total.shape[1]
    first_row_out = 0
    if height != length_y:
        first_row_out = window_start(place_ref[0], rows_ref.shape[1], height, length_y)

    def window(at, size):
        if height == length_y:
            return slice(at, at + size)
        return pl.ds(pl.multiple_of(first_row_out + at, ROWS), size)

    for channel in range(channels):
        value = base_ref[channel].astype(F32)
        for part in part_refs:
            value = value + part[channel].astype(F32)
        image[channel] = value
        rounded[channel] = value.astype(BF).astype(F32)
    if carried:
        begin = carried_ref[...]
    else:
        begin = jnp.zeros(total.shape, F32)
    if final:
        begin = begin - adjoint_ref[:, window(0, height), :].astype(F32)
    total[...] = begin
    if final:
        row_count = rows_ref.shape[1]
        start = pl.multiple_of(place_ref[0] * row_count, row_count)
        rows_ref[...] = image[:, pl.ds(start, row_count), :]

    def multiplied(index, phase):
        parts = []
        for at in range(0, length_y, ROWS):
            rows = slice(at, at + ROWS)
            map_re = maps_ref[2 * index, rows]
            map_im = maps_ref[2 * index + 1, rows]
            image_re = rounded[2 * phase, rows]
            image_im = rounded[2 * phase + 1, rows]
            parts.append(map_re * image_re - map_im * image_im)
            parts.append(map_re * image_im + map_im * image_re)
        value = dot(joined(parts, 0), table_zt[...]).reshape(length_y // ROWS, 2, ROWS, length_z)
        kz[phase, :, :length_z] = value[:, 0].reshape(length_y, length_z).astype(BF)
        kz[phase, :, length_z:] = value[:, 1].reshape(length_y, length_z).astype(BF)

    def transformed(phase):
        kspace[phase] = dot(table_y[...], kz[phase])

    def masked(phase):
        for at in range(0, length_y, 2 * ROWS):
            upper = kspace[phase, at : at + ROWS]
            lower = kspace[phase, at + ROWS : at + 2 * ROWS]
            pick = other_rows if at else first_row
            cut = [slice(half_z * part, half_z * (part + 1)) for part in range(4)]
            even_re, odd_re, even_im, odd_im = cut
            cos = spread(
                upper[:, even_re], lower[:, even_re], upper[:, even_im], lower[:, even_im], pick
            )
            sin = spread(
                upper[:, odd_re], lower[:, odd_re], upper[:, odd_im], lower[:, odd_im], pick
            )
            sides = []
            for side in range(2):
                plus_re, minus_re, plus_im, minus_im = spread(
                    cos[side], sin[side], cos[2 + side], sin[2 + side], first_lane
                )
                rows = slice(at + side * ROWS, at + (side + 1) * ROWS)
                plus = mask_ref[phase, rows, :half_z]
                minus = mask_ref[phase, rows, half_z:]
                sides.append(
                    folded(
                        plus_re * plus, minus_re * minus, plus_im * plus, minus_im * minus,
                        first_lane,
                    )
                )
            cos = folded(sides[0][0], sides[1][0], sides[0][2], sides[1][2], pick)
            sin = folded(sides[0][1], sides[1][1], sides[0][3], sides[1][3], pick)
            spectrum[phase, at : at + 2 * ROWS, :] = jnp.concatenate(
                [
                    jnp.concatenate([cos[0], sin[0], cos[2], sin[2]], axis=1),
                    jnp.concatenate([cos[1], sin[1], cos[3], sin[3]], axis=1),
                ],
                axis=0,
            ).astype(BF)

    def returned(phase):
        value = dot(table_yt[window(0, height), :], spectrum[phase])
        shape = (height // ROWS, ROWS, length_z)
        value = jnp.stack(
            [value[:, :length_z].reshape(shape), value[:, length_z:].reshape(shape)], axis=1
        )
        along_z[phase] = value.reshape(2 * height, length_z).astype(BF)

    def summed(index, phase):
        back = dot(along_z[phase], table_z[...])
        for at in range(0, height, ROWS):
            rows = slice(at, at + ROWS)
            map_re = maps_ref[2 * index, window(at, ROWS)]
            map_im = maps_ref[2 * index + 1, window(at, ROWS)]
            back_re = back[2 * at : 2 * at + ROWS]
            back_im = back[2 * at + ROWS : 2 * at + 2 * ROWS]
            total[2 * phase, rows] += map_re * back_re + map_im * back_im
            total[2 * phase + 1, rows] += map_re * back_im - map_im * back_re

    last_coil = maps_ref.shape[0] // 2 - 1
    for phase in range(phases):
        multiplied(first_coil, phase)
    transformed(0)
    along_z[phases - 1] = jnp.zeros(along_z.shape[1:], BF)

    def coil(index, carry):
        after = jnp.minimum(index + 1, last_coil)
        for phase in range(phases):
            before = index if phase else jnp.maximum(index - 1, first_coil)
            transformed((phase + 1) % phases)
            masked(phase)
            multiplied(after, phase)
            returned(phase)
            summed(before, (phase - 1) % phases)
        return carry

    lax.fori_loop(first_coil, last_coil + 1, coil, 0)
    summed(last_coil, phases - 1)
    if final:
        step = pack_ref[cascade, 2 * width : 2 * width + 1, 1:2]
        for channel in range(channels):
            value = image[channel, window(0, height), :] - step * total[channel]
            dc_ref[channel] = value
            v_ref[channel] = value.astype(BF)


def refine_kernel(neighbours, width, cascade, whole_rows, place_ref, v_ref, *refs):
    other_refs = refs[:neighbours]
    dc_ref, weight1_ref, weight2_ref, base_ref = refs[neighbours : neighbours + 4]
    send_refs = refs[neighbours + 4 : 2 * neighbours + 4]
    mixed, taps, hidden = refs[2 * neighbours + 4 :]
    channels, length_y, length_z = v_ref.shape
    tiles, mixed_rows, lanes = mixed.shape
    padded = length_y + 2 * ROWS
    per_row = mixed_rows // padded
    total_blocks = length_y // ROWS
    out_rows = base_ref.shape[1]
    first_block, blocks = 0, total_blocks
    out_block = 0
    if out_rows != length_y:
        start = window_start(place_ref[0], out_rows, length_y, whole_rows)
        out_block = (place_ref[0] * out_rows - start) // ROWS

    for tile in range(tiles):
        mixed[tile, 0:per_row, :] = jnp.zeros((per_row, lanes), F32)
        tail = (length_y + 1) * per_row
        mixed[tile, tail:, :] = jnp.zeros((mixed_rows - tail, lanes), F32)
    hidden[0:width, :] = jnp.zeros((width, length_z), BF)
    hidden[(length_y + 1) * width :, :] = jnp.zeros((width, length_z), BF)
    sources = [v_ref, *other_refs]
    for at in range(per_row):
        plane, channel = divmod(at, channels)
        if plane < len(sources):
            value = sources[plane][channel].astype(F32)
        else:
            value = jnp.zeros((length_y, length_z), F32)
        for tile in range(tiles):
            mixed[tile, pl.ds(per_row + at, length_y, stride=per_row), :] = value[
                :, tile * lanes : (tile + 1) * lanes
            ]

    group = 2 * ROWS

    def build(block, carry):
        start = pl.multiple_of(block * (group * per_row), group * per_row)
        window = jnp.concatenate(
            [mixed[tile, pl.ds(start, group * per_row), :] for tile in range(tiles)], axis=1
        )
        shape = (group, per_row, length_z)
        value = jnp.stack(
            [
                shifted_lanes(window, 1).reshape(shape),
                window.reshape(shape),
                shifted_lanes(window, -1).reshape(shape),
            ],
            axis=1,
        )
        store = pl.multiple_of(block * (group * 3 * per_row), group * 3 * per_row)
        taps[pl.ds(store, group * 3 * per_row), :] = value.reshape(-1, length_z).astype(BF)
        return carry

    skewed = out_rows == length_y and blocks // UNROLL > 2
    per_group = UNROLL * ROWS // group
    early = 2 * per_group + per_group + 1
    lax.fori_loop(0, early if skewed else padded // group, build, 0)
    spare = weight1_ref.shape[2] - (ROWS + 2) * 3 * per_row
    ones_row = lax.broadcasted_iota(jnp.int32, (spare, length_z), 0)
    ones = jnp.where(ones_row < 3, 1.0, 0.0).astype(BF)

    def first(block, carry):
        for part in range(UNROLL):
            at = first_block + block * UNROLL + part
            start = pl.multiple_of(at * (ROWS * 3 * per_row), ROWS * 3 * per_row)
            window = jnp.concatenate(
                [taps[pl.ds(start, (ROWS + 2) * 3 * per_row), :], ones], axis=0
            )
            value = dot(weight1_ref[cascade], window)
            store = pl.multiple_of((at * ROWS + 1) * width, width)
            hidden[pl.ds(store, ROWS * width), :] = jnp.maximum(value, 0.0).astype(BF)
        return carry

    lax.fori_loop(0, 2 if skewed else blocks // UNROLL, first, 0)
    block_rows = channels * ROWS
    unroll = min(UNROLL, out_rows // ROWS)
    span = unroll * ROWS

    def second(block, carry):
        results = []
        for part in range(unroll):
            at = out_block + block * unroll + part
            start = pl.multiple_of(at * (ROWS * width), ROWS * width)
            parts = dot(weight2_ref[cascade], hidden[pl.ds(start, (ROWS + 2) * width), :])
            third = parts.shape[0] // 3
            results.append(
                shifted_lanes(parts[:third], 1)
                + parts[third : 2 * third]
                + shifted_lanes(parts[2 * third :], -1)
            )
        rows = pl.ds(pl.multiple_of(block * span, span), span)
        from_rows = pl.ds(pl.multiple_of(out_block * ROWS + block * span, ROWS * 2), span)
        for plane in range(neighbours + 1):
            for channel in range(channels):
                lo = plane * block_rows + channel * ROWS
                value = jnp.concatenate([piece[lo : lo + ROWS] for piece in results], axis=0)
                if plane == 0:
                    base_ref[channel, rows, :] = dc_ref[channel, from_rows, :] + value
                else:
                    send_refs[plane - 1][channel, rows, :] = value.astype(BF)
        return carry

    def both(block, carry):
        second(block - 2, 0)
        first(block, 0)
        for part in range(per_group):
            at = (block + 1) * per_group + 1 + part
            build(jnp.minimum(at, padded // group - 1), 0)
        return carry

    if skewed:
        lax.fori_loop(2, blocks // UNROLL, both, 0)
        lax.fori_loop(blocks // UNROLL - 2, blocks // UNROLL, second, 0)
    else:
        lax.fori_loop(0, out_rows // span, second, 0)


def mask_kernel(bits_ref, columns_ref, order_ref, mask_ref):
    phases, length_y, length_z = mask_ref.shape
    for phase in range(phases):
        bits = bits_ref[phase]
        chosen = jnp.zeros((length_y, length_z), jnp.int32)
        for word in range(bits.shape[1]):
            chosen = jnp.where(columns_ref[0:1] == word, bits[:, word : word + 1], chosen)
        shift = jnp.broadcast_to(columns_ref[1:2], chosen.shape)
        taken = lax.shift_right_logical(chosen, shift) & 1
        mask_ref[phase] = dot(order_ref[...], taken.astype(F32).astype(BF))


def prepare_kernel(
    width, per_row, place_ref, pack_ref, select1_ref, select2_ref, weight1_ref, weight2_ref
):
    variant = place_ref[1] if select1_ref.shape[0] > 1 else 0
    count = select1_ref.shape[1]
    for cascade in range(pack_ref.shape[0]):
        small1 = pack_ref[cascade, :width, :count].astype(BF)
        small2 = pack_ref[cascade, width : 2 * width, :count].astype(BF)
        bias = pack_ref[cascade, 2 * width :, 0:1]
        terms = []
        for _ in range(3):
            terms.append(bias.astype(BF).astype(F32))
            bias = bias - terms[-1]
        base = dot(small1, select1_ref[variant])
        column = lax.broadcasted_iota(jnp.int32, base.shape, 1)
        step = per_row
        for row in range(ROWS):
            value = base if row == 0 else pltpu.roll(base, row * 3 * step, 1)
            for at, term in enumerate(terms):
                value = jnp.where(column == (ROWS + 2) * 3 * step + at, term, value)
            weight1_ref[cascade, row * width : (row + 1) * width, :] = value.astype(BF)
        repeated = jnp.concatenate([small2] * (ROWS + 2), axis=0)
        shape = weight2_ref.shape[1:]
        column = lax.broadcasted_iota(jnp.int32, shape, 1)
        lower = (lax.broadcasted_iota(jnp.int32, shape, 0) & (ROWS - 1)) * width
        value = jnp.zeros(shape, F32)
        for tap in range(3):
            placed = lax.dot_general(
                select2_ref[variant, tap],
                repeated,
                (((1,), (1,)), ((), ())),
                preferred_element_type=F32,
            )
            low = lower + tap * width
            value = jnp.where((column >= low) & (column < low + width), placed, value)
        weight2_ref[cascade] = value.astype(BF)


def assemble_kernel(members, spaces, steps, place_ref, local_ref, *refs):
    block_refs = refs[: len(steps) * members]
    out_refs = refs[len(steps) * members :]
    rows = local_ref.shape[2]

    def put(owner, at, block):
        where = pl.ds(pl.multiple_of(at * rows, rows), rows)
        taken = 0
        for out_ref in out_refs:
            size = out_ref.shape[0] // members
            for index in range(size):
                out_ref[owner * size + index, where, :] = block[taken + index].astype(out_ref.dtype)
            taken += size

    for member in range(members):
        put(member, place_ref[0], local_ref[member])
    for turn, step in enumerate(steps):
        at = lax.rem(place_ref[0] - step + spaces, spaces)
        for offset in range(members):
            owner = lax.rem(place_ref[2] + offset, members)
            put(owner, at, block_refs[turn * members + offset])


def stack_kernel(shared, spaces, steps, offsets, heads, place_ref, *refs):
    head_refs = refs[:heads]
    local_ref = refs[heads]
    block_refs = refs[heads + 1 : -1]
    out_ref = refs[-1]
    share, rows = local_ref.shape[1:3]
    base = 0
    for head_ref in head_refs:
        base = head_ref.shape[0]
        out_ref[:base] = head_ref[...]
    for turn, offset in enumerate(offsets):
        owner = lax.rem(place_ref[2] + offset, shared)
        for nth, step in enumerate((0, *steps)):
            at = lax.rem(place_ref[0] - step + spaces, spaces)
            where = pl.ds(pl.multiple_of(at * rows, rows), rows)
            for index in range(share):
                if nth:
                    block = block_refs[turn * len(steps) + nth - 1][index]
                else:
                    block = local_ref[owner, index]
                out_ref[base + turn * share + index, where, :] = block.astype(out_ref.dtype)


def ring(value, axis, step):
    count = lax.axis_size(axis)
    return lax.ppermute(value, axis, [(i, (i + step) % count) for i in range(count)])


def gathered(value, axis):
    count = lax.axis_size(axis)
    index = lax.axis_index(axis)
    whole = jnp.zeros((count,) + value.shape, value.dtype)
    for step in range(count):
        block = ring(value, axis, step) if step else value
        whole = lax.dynamic_update_index_in_dim(whole, block, (index - step) % count, 0)
    return whole


def per_device(image, sens, adjoint, mask_bits, step_size, conv1_w, conv1_b, conv2_w):
    channels, slab_count, _, row_count, length_z = image.shape
    phases, length_y = mask_bits.shape[:2]
    planes = lax.axis_size("coil")
    coil_local = sens.shape[0]
    width = conv1_w.shape[1]
    groups = lax.axis_size("group")
    members = lax.axis_size("member")
    cascades = groups * members
    group = lax.axis_index("group")
    member = lax.axis_index("member")
    plane = lax.axis_index("coil")
    section = group * members + member
    table_z = half_tables(length_z)
    alternate = np.arange(length_y).reshape(2, -1, ROWS).swapaxes(0, 1).reshape(-1)
    table_y = half_tables(length_y)[alternate]
    tables = tuple(jnp.asarray(value) for value in (table_z, table_z.T, table_y, table_y.T))
    count = conv1_w.shape[2]

    if planes == 1:
        sides, variants = [], [[0]]
    elif planes == 2:
        sides, variants = [None], [[0, 1], [0, -1]]
    else:
        sides, variants = [-1, 1], [[0, -1, 1]]
    neighbours = len(sides)
    involved = neighbours + 1
    per_row = -(-(involved * channels) // 8) * 8
    chosen = [tap_selectors(channels, per_row, offsets) for offsets in variants]
    select1, select2 = (jnp.asarray(np.stack(parts)) for parts in zip(*chosen))

    place = jnp.stack([lax.axis_index("space"), plane, member]).astype(jnp.int32)
    spaces = lax.axis_size("space")
    own_image = lax.dynamic_index_in_dim(image, group, 1, keepdims=False)[:, 0].astype(BF)
    own_adjoint = lax.dynamic_index_in_dim(adjoint, group, 1, keepdims=False)[:, 0].astype(BF)
    coils = coil_local * planes
    shared = members if phases % members == 0 and coils % members == 0 else 1
    steps = sorted(range(1, spaces), key=lambda step: min(step, spaces - step))

    def shares(parts):
        local = jnp.concatenate(
            [part.reshape(shared, -1, row_count, length_z) for part in parts], axis=1
        )
        return local, lax.dynamic_index_in_dim(local, member % shared, 0, keepdims=False)

    def sent_blocks(mine):
        blocks = []
        for step in steps:
            if blocks and 2 * step == spaces:
                mine, blocks[0] = lax.optimization_barrier((mine, blocks[0]))
            block = ring(mine, "space", step)
            blocks.append(block)
        return blocks

    def traded(blocks):
        pairs = []
        for block in blocks:
            pairs.append(block)
            for offset in range(1, shared):
                pairs.append(ring(block, "member", -offset))
        return pairs

    def put_together(local, blocks, sizes, dtypes):
        return pl.pallas_call(
            functools.partial(assemble_kernel, shared, spaces, steps),
            out_shape=tuple(
                jax.ShapeDtypeStruct((size, length_y, length_z), dtype)
                for size, dtype in zip(sizes, dtypes)
            ),
            in_specs=[smem] + [vmem] * (1 + len(blocks)),
            out_specs=(vmem,) * len(sizes),
            compiler_params=params,
        )(place, local, *blocks)

    local1, mine1 = shares([own_image, own_adjoint])
    sens, mine1 = lax.optimization_barrier((sens, mine1))
    blocks1 = [ring(mine1, "space", step) for step in steps]
    if planes == 2:
        sent = lax.dynamic_slice(
            sens, (0, group, 1 - plane, 0, 0), (coil_local, 1, 1) + sens.shape[3:]
        )[:, 0, 0]
        received = ring(sent, "coil", 1)
        own = lax.dynamic_slice(
            sens, (0, group, plane, 0, 0), (coil_local, 1, 1) + sens.shape[3:]
        )[:, 0, 0]
    else:
        slab_sens = lax.dynamic_index_in_dim(sens, group, 1, keepdims=False)
        sent = slab_sens
        received = lax.all_to_all(sent, "coil", split_axis=1, concat_axis=0, tiled=True)[:, 0]
        own = received[:0]
    maps = jnp.concatenate([own, received], axis=0)
    maps = maps.reshape(coils, row_count, 2, length_z).transpose(0, 2, 1, 3)
    local2, mine2 = shares([maps.reshape(2 * coils, row_count, length_z)])
    blocks2 = sent_blocks(mine2)
    conv1_w, conv2_w, conv1_b, step_size, mine2 = lax.optimization_barrier(
        (conv1_w, conv2_w, conv1_b, step_size, mine2)
    )
    extra = jnp.concatenate(
        [conv1_b.T, jnp.broadcast_to(step_size.reshape(1, 1), (width, 1))], axis=1
    )
    packed = jnp.concatenate(
        [
            jnp.pad(part, ((0, 0), (0, -(-count // LANES) * LANES - part.shape[1])))
            for part in (conv1_w[0].astype(F32), conv2_w[0].astype(F32), extra)
        ],
        axis=0,
    )
    packed = gathered(gathered(packed, "member"), "group")
    packed = packed.reshape((cascades,) + packed.shape[2:])

    full = jax.ShapeDtypeStruct((channels, length_y, length_z), F32)
    half = jax.ShapeDtypeStruct((channels, length_y, length_z), BF)
    vmem = pl.BlockSpec(memory_space=pltpu.VMEM)
    smem = pl.BlockSpec(memory_space=pltpu.SMEM)
    params = pltpu.CompilerParams(vmem_limit_bytes=32 * 1024 * 1024)
    base, target = put_together(local1, traded(blocks1), [channels, channels], [BF, BF])

    def stacked(offsets, heads, pieces):
        size = local2.shape[1] * len(offsets) + sum(head.shape[0] for head in heads)
        return pl.pallas_call(
            functools.partial(stack_kernel, shared, spaces, steps, offsets, len(heads)),
            out_shape=jax.ShapeDtypeStruct((size, length_y, length_z), F32),
            in_specs=[smem] + [vmem] * (1 + len(heads) + len(pieces)),
            out_specs=vmem,
            compiler_params=params,
        )(place, *heads, local2, *pieces)

    own_maps = maps = stacked((0,), [], blocks2)
    if shared > 1:
        others = tuple(range(1, shared))
        pieces = [ring(block, "member", -offset) for offset in others for block in blocks2]
        maps = stacked(others, [own_maps], pieces)
    order = np.eye(length_y)[slot_order(length_y)[alternate]].astype(BF)
    column = slot_order(length_z)
    columns = np.stack([column // 30, column % 30]).astype(np.int32)
    sampled = pl.pallas_call(
        mask_kernel,
        out_shape=jax.ShapeDtypeStruct((phases, length_y, length_z), F32),
        in_specs=[vmem] * 3,
        out_specs=vmem,
        compiler_params=params,
    )(mask_bits, jnp.asarray(columns), jnp.asarray(order))
    weight1, weight2 = pl.pallas_call(
        functools.partial(prepare_kernel, width, per_row),
        out_shape=(
            jax.ShapeDtypeStruct((cascades, ROWS * width, select1.shape[2]), BF),
            jax.ShapeDtypeStruct((cascades, select2.shape[2], (ROWS + 2) * width), BF),
        ),
        in_specs=[smem] + [vmem] * 3,
        out_specs=(vmem,) * 2,
        compiler_params=params,
    )(place, packed, select1, select2)
    rows_shape = jax.ShapeDtypeStruct((channels, row_count, length_z), F32)

    margin = 2 * ROWS
    windowed = row_count + 2 * margin
    if row_count % margin or windowed % (UNROLL * ROWS) or windowed >= length_y:
        windowed = length_y

    def consistency(cascade, base, parts, maps, first_coil=0, carried=None, final=True):
        height = windowed if cascade == cascades - 1 else length_y
        shape = (channels, height, length_z)
        operands = [base, *parts] + ([] if carried is None else [carried])
        operands += [maps, sampled, *tables] + ([target, packed] if final else [])
        sums = jax.ShapeDtypeStruct(shape, F32)
        return pl.pallas_call(
            functools.partial(
                consistency_kernel,
                phases,
                width,
                cascade,
                len(parts),
                first_coil,
                carried is not None,
                final,
            ),
            out_shape=(rows_shape, sums, jax.ShapeDtypeStruct(shape, BF)) if final else sums,
            in_specs=[smem] + [vmem] * len(operands),
            out_specs=(vmem,) * 3 if final else vmem,
            scratch_shapes=([pltpu.VMEM(shape, F32)] if final else [])
            + [pltpu.VMEM((channels, length_y, length_z), F32)] * 2
            + [pltpu.VMEM((phases, length_y, 2 * length_z), dtype) for dtype in (BF, F32, BF)]
            + [pltpu.VMEM((phases, 2 * height, length_z), BF)],
            compiler_params=params,
        )(place, *operands)

    def refine(cascade, value, others, updated):
        rows = value.shape[1]
        padded = rows + 2 * ROWS
        shape = (channels, rows if rows == length_y else row_count, length_z)
        return pl.pallas_call(
            functools.partial(refine_kernel, neighbours, width, cascade, length_y),
            out_shape=(jax.ShapeDtypeStruct(shape, F32),)
            + (jax.ShapeDtypeStruct(shape, BF),) * neighbours,
            in_specs=[smem] + [vmem] * (4 + neighbours),
            out_specs=(vmem,) * (1 + neighbours),
            scratch_shapes=[
                pltpu.VMEM((length_z // LANES, padded * per_row, LANES), F32),
                pltpu.VMEM((padded * 3 * per_row, length_z), BF),
                pltpu.VMEM(((rows + 2) * width, length_z), BF),
            ],
            compiler_params=params,
        )(place, value, *others, updated, weight1, weight2)

    def exchanged(values):
        received = []
        for value, side in zip(values, sides):
            if side is None:
                pairs = [(0, 1), (1, 0)]
            else:
                pairs = [(i, i - side) for i in range(planes) if 0 <= i - side < planes]
            received.append(lax.ppermute(value, "coil", pairs))
        return received

    row_start = lax.axis_index("space") * row_count

    def own_rows(value):
        if value.shape[1] == row_count:
            return value
        return lax.dynamic_slice_in_dim(value, row_start, row_count, 1)

    results = []
    parts = []
    for cascade in range(cascades):
        if cascade == 0 and cascades > 1 and shared > 1:
            carried = consistency(0, base, [], own_maps, final=False)
            first_coil = own_maps.shape[0] // 2
            rows, updated, value = consistency(0, base, [], maps, first_coil, carried)
        else:
            rows, updated, value = consistency(cascade, base, parts, maps)
        if cascade:
            results.append(rows)
        others = exchanged([value] * neighbours)
        base, *sends = refine(cascade, value, others, updated)
        turned = sends[::-1] if neighbours == 2 else sends
        parts = exchanged(turned)[::-1] if neighbours == 2 else exchanged(turned)
    last = own_rows(base)
    for part in parts:
        last = last + own_rows(part).astype(F32)
    results.append(last)

    def result_of(wanted):
        chosen = results[0]
        for cascade in range(1, cascades):
            chosen = jnp.where(wanted == cascade, results[cascade], chosen)
        return chosen

    output = jnp.zeros((channels, slab_count, row_count, length_z), F32)
    for step in range(groups):
        if step == 0:
            chosen = result_of(section)
        else:
            target_group = (group - step) % groups
            chosen = result_of(target_group * members + member).astype(BF)
            chosen = lax.ppermute(
                chosen, "group", [(i, (i - step) % groups) for i in range(groups)]
            ).astype(F32)
        output = lax.dynamic_update_slice_in_dim(
            output, chosen[:, None], (group + step) % groups, 1
        )
    return output[None, :, :, None]


def solution(mesh):
    sections, coils, spaces = mesh.devices.shape
    def run(image, *args):
        groups = image.shape[1]
        fine = Mesh(
            mesh.devices.reshape(groups, sections // groups, coils, spaces),
            ("group", "member", "coil", "space"),
        )
        section = ("group", "member")
        in_specs = (
            P(None, None, "coil", "space", None),
            P("coil", None, None, "space", None),
            P(None, None, "coil", "space", None),
            P(),
            P(section),
            P(section, None, None),
            P(section, None),
            P(section, None, None),
        )
        out_specs = P(section, None, None, "coil", "space", None)
        return jax.shard_map(
            per_device, mesh=fine, in_specs=in_specs, out_specs=out_specs, check_vma=False
        )(image, *args)

    return run
```

```python
import functools

import jax
import jax.numpy as jnp
import numpy as np
from jax import lax
from jax.experimental import pallas as pl
from jax.experimental.pallas import tpu as pltpu
from jax.sharding import Mesh
from jax.sharding import PartitionSpec as P

BF = jnp.bfloat16
F32 = jnp.float32
ROWS = 8
UNROLL = 4
LANES = 128


def half_tables(length):
    half = length // 2
    index = np.arange(length)
    angle = np.arange(half)[:, None] * index[None, :] % length * (2.0 * np.pi / length)
    scale = 1.0 / np.sqrt(length)
    cos = np.cos(angle) * scale
    sin = np.sin(angle) * scale
    cos[0] = np.where(index % 2 == 0, scale, 0.0)
    sin[0] = np.where(index % 2 == 0, 0.0, scale)
    return np.concatenate([cos, sin], axis=0).astype(BF)


def slot_order(length):
    half = length // 2
    slot = np.arange(length)
    return np.where(slot <= half, slot, length + half - slot)


def tap_selectors(channels, per_row, offsets):
    count = 27 * channels
    involved = len(offsets)
    used = (ROWS + 2) * 3 * per_row
    columns = -(-(used + 3) // LANES) * LANES
    tap = np.arange(count)
    plane, tap_y, tap_z, channel = (
        tap // (9 * channels),
        tap // (3 * channels) % 3,
        tap // channels % 3,
        tap % channels,
    )
    column = np.arange(columns)
    slot = column % per_row
    offset = np.array(list(offsets) + [9] * (per_row // channels + 1))[slot // channels]
    first = (
        (column[None] < 9 * per_row)
        & (plane[:, None] == 1 + offset[None])
        & (tap_y[:, None] == column[None] // (3 * per_row))
        & (tap_z[:, None] == column[None] // per_row % 3)
        & (channel[:, None] == slot[None] % channels)
    )
    row = np.arange(3 * involved * channels * ROWS)
    offset = np.array(offsets)[row // (channels * ROWS) % involved]
    second = (
        (plane[None] == 1 - offset[:, None])
        & (tap_z[None] == row[:, None] // (involved * channels * ROWS))
        & (channel[None] == row[:, None] // ROWS % channels)
    )
    second = np.stack([second & (tap_y[None] == at) for at in range(3)])
    return first.astype(BF), second.astype(BF)


def dot(left, right):
    return jnp.dot(left, right, preferred_element_type=F32)


def shifted_lanes(values, step):
    length = values.shape[1]
    lane = lax.broadcasted_iota(jnp.int32, values.shape, 1)
    if step > 0:
        return jnp.where(lane == 0, 0.0, pltpu.roll(values, 1, 1))
    return jnp.where(lane == length - 1, 0.0, pltpu.roll(values, length - 1, 1))


def first_lane(on, other):
    lane = lax.broadcasted_iota(jnp.int32, on.shape, on.ndim - 1)
    return jnp.where(lane == 0, on, other)


def first_row(on, other):
    row = lax.broadcasted_iota(jnp.int32, on.shape, on.ndim - 2)
    return jnp.where(row == 0, on, other)


def other_rows(on, other):
    return other


def spread(cos_re, sin_re, cos_im, sin_im, pick):
    add_re = pick(sin_re, sin_im)
    add_im = pick(sin_im, -sin_re)
    return cos_re + add_re, cos_re - add_re, cos_im + add_im, cos_im - add_im


def folded(plus_re, minus_re, plus_im, minus_im, pick):
    sum_re, odd_re = plus_re + minus_re, plus_re - minus_re
    sum_im, odd_im = plus_im + minus_im, plus_im - minus_im
    return sum_re, pick(odd_re, -odd_im), sum_im, pick(odd_im, odd_re)


def joined(parts, axis):
    return jnp.concatenate([part.astype(BF) for part in parts], axis=axis)


def window_start(index, rows, height, length):
    return jnp.clip(index * rows - (height - rows) // 2, 0, length - height)


def consistency_kernel(
    phases, width, cascade, neighbours, first_coil, carried, final, place_ref, base_ref, *refs
):
    refs = list(refs)
    part_refs = [refs.pop(0) for _ in range(neighbours)]
    carried_ref = refs.pop(0) if carried else None
    maps_ref, mask_ref, table_z, table_zt, table_y, table_yt = (refs.pop(0) for _ in range(6))
    if final:
        adjoint_ref, pack_ref, rows_ref, dc_ref, v_ref, total = (refs.pop(0) for _ in range(6))
    else:
        total = refs.pop(0)
    image, rounded, kz, kspace, spectrum, along_z = refs
    channels, length_y, length_z = base_ref.shape
    half_z = length_z // 2
    height = total.shape[1]
    first_row_out = 0
    if height != length_y:
        first_row_out = window_start(place_ref[0], rows_ref.shape[1], height, length_y)

    def window(at, size):
        if height == length_y:
            return slice(at, at + size)
        return pl.ds(pl.multiple_of(first_row_out + at, ROWS), size)

    for channel in range(channels):
        value = base_ref[channel].astype(F32)
        for part in part_refs:
            value = value + part[channel].astype(F32)
        image[channel] = value
        rounded[channel] = value.astype(BF).astype(F32)
    if carried:
        begin = carried_ref[...]
    else:
        begin = jnp.zeros(total.shape, F32)
    if final:
        begin = begin - adjoint_ref[:, window(0, height), :].astype(F32)
    total[...] = begin
    if final:
        row_count = rows_ref.shape[1]
        start = pl.multiple_of(place_ref[0] * row_count, row_count)
        rows_ref[...] = image[:, pl.ds(start, row_count), :]

    def multiplied(index, phase):
        parts = []
        for at in range(0, length_y, ROWS):
            rows = slice(at, at + ROWS)
            map_re = maps_ref[2 * index, rows]
            map_im = maps_ref[2 * index + 1, rows]
            image_re = rounded[2 * phase, rows]
            image_im = rounded[2 * phase + 1, rows]
            parts.append(map_re * image_re - map_im * image_im)
            parts.append(map_re * image_im + map_im * image_re)
        value = dot(joined(parts, 0), table_zt[...]).reshape(length_y // ROWS, 2, ROWS, length_z)
        kz[phase, :, :length_z] = value[:, 0].reshape(length_y, length_z).astype(BF)
        kz[phase, :, length_z:] = value[:, 1].reshape(length_y, length_z).astype(BF)

    def transformed(phase):
        kspace[phase] = dot(table_y[...], kz[phase])

    def masked(phase):
        for at in range(0, length_y, 2 * ROWS):
            upper = kspace[phase, at : at + ROWS]
            lower = kspace[phase, at + ROWS : at + 2 * ROWS]
            pick = other_rows if at else first_row
            cut = [slice(half_z * part, half_z * (part + 1)) for part in range(4)]
            even_re, odd_re, even_im, odd_im = cut
            cos = spread(
                upper[:, even_re], lower[:, even_re], upper[:, even_im], lower[:, even_im], pick
            )
            sin = spread(
                upper[:, odd_re], lower[:, odd_re], upper[:, odd_im], lower[:, odd_im], pick
            )
            sides = []
            for side in range(2):
                plus_re, minus_re, plus_im, minus_im = spread(
                    cos[side], sin[side], cos[2 + side], sin[2 + side], first_lane
                )
                rows = slice(at + side * ROWS, at + (side + 1) * ROWS)
                plus = mask_ref[phase, rows, :half_z]
                minus = mask_ref[phase, rows, half_z:]
                sides.append(
                    folded(
                        plus_re * plus, minus_re * minus, plus_im * plus, minus_im * minus,
                        first_lane,
                    )
                )
            cos = folded(sides[0][0], sides[1][0], sides[0][2], sides[1][2], pick)
            sin = folded(sides[0][1], sides[1][1], sides[0][3], sides[1][3], pick)
            spectrum[phase, at : at + 2 * ROWS, :] = jnp.concatenate(
                [
                    jnp.concatenate([cos[0], sin[0], cos[2], sin[2]], axis=1),
                    jnp.concatenate([cos[1], sin[1], cos[3], sin[3]], axis=1),
                ],
                axis=0,
            ).astype(BF)

    def returned(phase):
        value = dot(table_yt[window(0, height), :], spectrum[phase])
        shape = (height // ROWS, ROWS, length_z)
        value = jnp.stack(
            [value[:, :length_z].reshape(shape), value[:, length_z:].reshape(shape)], axis=1
        )
        along_z[phase] = value.reshape(2 * height, length_z).astype(BF)

    def summed(index, phase):
        back = dot(along_z[phase], table_z[...])
        for at in range(0, height, ROWS):
            rows = slice(at, at + ROWS)
            map_re = maps_ref[2 * index, window(at, ROWS)]
            map_im = maps_ref[2 * index + 1, window(at, ROWS)]
            back_re = back[2 * at : 2 * at + ROWS]
            back_im = back[2 * at + ROWS : 2 * at + 2 * ROWS]
            total[2 * phase, rows] += map_re * back_re + map_im * back_im
            total[2 * phase + 1, rows] += map_re * back_im - map_im * back_re

    last_coil = maps_ref.shape[0] // 2 - 1
    for phase in range(phases):
        multiplied(first_coil, phase)
    transformed(0)
    along_z[phases - 1] = jnp.zeros(along_z.shape[1:], BF)

    def coil(index, carry):
        after = jnp.minimum(index + 1, last_coil)
        for phase in range(phases):
            before = index if phase else jnp.maximum(index - 1, first_coil)
            transformed((phase + 1) % phases)
            masked(phase)
            multiplied(after, phase)
            returned(phase)
            summed(before, (phase - 1) % phases)
        return carry

    lax.fori_loop(first_coil, last_coil + 1, coil, 0)
    summed(last_coil, phases - 1)
    if final:
        step = pack_ref[cascade, 2 * width : 2 * width + 1, 1:2]
        for channel in range(channels):
            value = image[channel, window(0, height), :] - step * total[channel]
            dc_ref[channel] = value
            v_ref[channel] = value.astype(BF)


def refine_kernel(neighbours, width, cascade, whole_rows, place_ref, v_ref, *refs):
    other_refs = refs[:neighbours]
    dc_ref, weight1_ref, weight2_ref, base_ref = refs[neighbours : neighbours + 4]
    send_refs = refs[neighbours + 4 : 2 * neighbours + 4]
    mixed, taps, hidden = refs[2 * neighbours + 4 :]
    channels, length_y, length_z = v_ref.shape
    tiles, mixed_rows, lanes = mixed.shape
    padded = length_y + 2 * ROWS
    per_row = mixed_rows // padded
    total_blocks = length_y // ROWS
    out_rows = base_ref.shape[1]
    first_block, blocks = 0, total_blocks
    out_block = 0
    if out_rows != length_y:
        start = window_start(place_ref[0], out_rows, length_y, whole_rows)
        out_block = (place_ref[0] * out_rows - start) // ROWS

    for tile in range(tiles):
        mixed[tile, 0:per_row, :] = jnp.zeros((per_row, lanes), F32)
        tail = (length_y + 1) * per_row
        mixed[tile, tail:, :] = jnp.zeros((mixed_rows - tail, lanes), F32)
    hidden[0:width, :] = jnp.zeros((width, length_z), BF)
    hidden[(length_y + 1) * width :, :] = jnp.zeros((width, length_z), BF)
    sources = [v_ref, *other_refs]
    for at in range(per_row):
        plane, channel = divmod(at, channels)
        if plane < len(sources):
            value = sources[plane][channel].astype(F32)
        else:
            value = jnp.zeros((length_y, length_z), F32)
        for tile in range(tiles):
            mixed[tile, pl.ds(per_row + at, length_y, stride=per_row), :] = value[
                :, tile * lanes : (tile + 1) * lanes
            ]

    group = 2 * ROWS

    def build(block, carry):
        start = pl.multiple_of(block * (group * per_row), group * per_row)
        window = jnp.concatenate(
            [mixed[tile, pl.ds(start, group * per_row), :] for tile in range(tiles)], axis=1
        )
        shape = (group, per_row, length_z)
        value = jnp.stack(
            [
                shifted_lanes(window, 1).reshape(shape),
                window.reshape(shape),
                shifted_lanes(window, -1).reshape(shape),
            ],
            axis=1,
        )
        store = pl.multiple_of(block * (group * 3 * per_row), group * 3 * per_row)
        taps[pl.ds(store, group * 3 * per_row), :] = value.reshape(-1, length_z).astype(BF)
        return carry

    skewed = out_rows == length_y and blocks // UNROLL > 2
    per_group = UNROLL * ROWS // group
    early = 2 * per_group + per_group + 1
    if skewed:
        for block in range(early):
            build(block, 0)
    else:
        lax.fori_loop(0, padded // group, build, 0)
    spare = weight1_ref.shape[2] - (ROWS + 2) * 3 * per_row
    ones_row = lax.broadcasted_iota(jnp.int32, (spare, length_z), 0)
    ones = jnp.where(ones_row < 3, 1.0, 0.0).astype(BF)

    def first(block, carry):
        for part in range(UNROLL):
            at = first_block + block * UNROLL + part
            start = pl.multiple_of(at * (ROWS * 3 * per_row), ROWS * 3 * per_row)
            window = jnp.concatenate(
                [taps[pl.ds(start, (ROWS + 2) * 3 * per_row), :], ones], axis=0
            )
            value = dot(weight1_ref[cascade], window)
            store = pl.multiple_of((at * ROWS + 1) * width, width)
            hidden[pl.ds(store, ROWS * width), :] = jnp.maximum(value, 0.0).astype(BF)
        return carry

    if skewed:
        for block in range(2):
            first(block, 0)
    else:
        lax.fori_loop(0, blocks // UNROLL, first, 0)
    block_rows = channels * ROWS
    unroll = min(UNROLL, out_rows // ROWS)
    span = unroll * ROWS

    def second(block, carry):
        results = []
        for part in range(unroll):
            at = out_block + block * unroll + part
            start = pl.multiple_of(at * (ROWS * width), ROWS * width)
            parts = dot(weight2_ref[cascade], hidden[pl.ds(start, (ROWS + 2) * width), :])
            third = parts.shape[0] // 3
            results.append(
                shifted_lanes(parts[:third], 1)
                + parts[third : 2 * third]
                + shifted_lanes(parts[2 * third :], -1)
            )
        rows = pl.ds(pl.multiple_of(block * span, span), span)
        from_rows = pl.ds(pl.multiple_of(out_block * ROWS + block * span, ROWS * 2), span)
        for plane in range(neighbours + 1):
            for channel in range(channels):
                lo = plane * block_rows + channel * ROWS
                value = jnp.concatenate([piece[lo : lo + ROWS] for piece in results], axis=0)
                if plane == 0:
                    base_ref[channel, rows, :] = dc_ref[channel, from_rows, :] + value
                else:
                    send_refs[plane - 1][channel, rows, :] = value.astype(BF)
        return carry

    def both(block, carry):
        second(block - 2, 0)
        first(block, 0)
        for part in range(per_group):
            at = (block + 1) * per_group + 1 + part
            build(jnp.minimum(at, padded // group - 1), 0)
        return carry

    if skewed:
        lax.fori_loop(2, blocks // UNROLL, both, 0)
        for block in range(blocks // UNROLL - 2, blocks // UNROLL):
            second(block, 0)
    else:
        lax.fori_loop(0, out_rows // span, second, 0)


def mask_kernel(bits_ref, columns_ref, order_ref, mask_ref):
    phases, length_y, length_z = mask_ref.shape
    for phase in range(phases):
        bits = bits_ref[phase]
        chosen = jnp.zeros((length_y, length_z), jnp.int32)
        for word in range(bits.shape[1]):
            chosen = jnp.where(columns_ref[0:1] == word, bits[:, word : word + 1], chosen)
        shift = jnp.broadcast_to(columns_ref[1:2], chosen.shape)
        taken = lax.shift_right_logical(chosen, shift) & 1
        mask_ref[phase] = dot(order_ref[...], taken.astype(F32).astype(BF))


def prepare_kernel(
    width, per_row, place_ref, pack_ref, select1_ref, select2_ref, weight1_ref, weight2_ref
):
    variant = place_ref[1] if select1_ref.shape[0] > 1 else 0
    count = select1_ref.shape[1]
    for cascade in range(pack_ref.shape[0]):
        small1 = pack_ref[cascade, :width, :count].astype(BF)
        small2 = pack_ref[cascade, width : 2 * width, :count].astype(BF)
        bias = pack_ref[cascade, 2 * width :, 0:1]
        terms = []
        for _ in range(3):
            terms.append(bias.astype(BF).astype(F32))
            bias = bias - terms[-1]
        base = dot(small1, select1_ref[variant])
        column = lax.broadcasted_iota(jnp.int32, base.shape, 1)
        step = per_row
        for row in range(ROWS):
            value = base if row == 0 else pltpu.roll(base, row * 3 * step, 1)
            for at, term in enumerate(terms):
                value = jnp.where(column == (ROWS + 2) * 3 * step + at, term, value)
            weight1_ref[cascade, row * width : (row + 1) * width, :] = value.astype(BF)
        repeated = jnp.concatenate([small2] * (ROWS + 2), axis=0)
        shape = weight2_ref.shape[1:]
        column = lax.broadcasted_iota(jnp.int32, shape, 1)
        lower = (lax.broadcasted_iota(jnp.int32, shape, 0) & (ROWS - 1)) * width
        value = jnp.zeros(shape, F32)
        for tap in range(3):
            placed = lax.dot_general(
                select2_ref[variant, tap],
                repeated,
                (((1,), (1,)), ((), ())),
                preferred_element_type=F32,
            )
            low = lower + tap * width
            value = jnp.where((column >= low) & (column < low + width), placed, value)
        weight2_ref[cascade] = value.astype(BF)


def assemble_kernel(members, spaces, steps, place_ref, local_ref, *refs):
    block_refs = refs[: len(steps) * members]
    out_refs = refs[len(steps) * members :]
    rows = local_ref.shape[2]

    def put(owner, at, block):
        where = pl.ds(pl.multiple_of(at * rows, rows), rows)
        taken = 0
        for out_ref in out_refs:
            size = out_ref.shape[0] // members
            for index in range(size):
                out_ref[owner * size + index, where, :] = block[taken + index].astype(out_ref.dtype)
            taken += size

    for member in range(members):
        put(member, place_ref[0], local_ref[member])
    for turn, step in enumerate(steps):
        at = lax.rem(place_ref[0] - step + spaces, spaces)
        for offset in range(members):
            owner = lax.rem(place_ref[2] + offset, members)
            put(owner, at, block_refs[turn * members + offset])


def stack_kernel(shared, spaces, steps, offsets, heads, place_ref, *refs):
    head_refs = refs[:heads]
    local_ref = refs[heads]
    block_refs = refs[heads + 1 : -1]
    out_ref = refs[-1]
    share, rows = local_ref.shape[1:3]
    base = 0
    for head_ref in head_refs:
        base = head_ref.shape[0]
        out_ref[:base] = head_ref[...]
    for turn, offset in enumerate(offsets):
        owner = lax.rem(place_ref[2] + offset, shared)
        for nth, step in enumerate((0, *steps)):
            at = lax.rem(place_ref[0] - step + spaces, spaces)
            where = pl.ds(pl.multiple_of(at * rows, rows), rows)
            for index in range(share):
                if nth:
                    block = block_refs[turn * len(steps) + nth - 1][index]
                else:
                    block = local_ref[owner, index]
                out_ref[base + turn * share + index, where, :] = block.astype(out_ref.dtype)


def ring(value, axis, step):
    count = lax.axis_size(axis)
    return lax.ppermute(value, axis, [(i, (i + step) % count) for i in range(count)])


def gathered(value, axis):
    count = lax.axis_size(axis)
    index = lax.axis_index(axis)
    whole = jnp.zeros((count,) + value.shape, value.dtype)
    for step in range(count):
        block = ring(value, axis, step) if step else value
        whole = lax.dynamic_update_index_in_dim(whole, block, (index - step) % count, 0)
    return whole


def per_device(image, sens, adjoint, mask_bits, step_size, conv1_w, conv1_b, conv2_w):
    channels, slab_count, _, row_count, length_z = image.shape
    phases, length_y = mask_bits.shape[:2]
    planes = lax.axis_size("coil")
    coil_local = sens.shape[0]
    width = conv1_w.shape[1]
    groups = lax.axis_size("group")
    members = lax.axis_size("member")
    cascades = groups * members
    group = lax.axis_index("group")
    member = lax.axis_index("member")
    plane = lax.axis_index("coil")
    section = group * members + member
    table_z = half_tables(length_z)
    alternate = np.arange(length_y).reshape(2, -1, ROWS).swapaxes(0, 1).reshape(-1)
    table_y = half_tables(length_y)[alternate]
    tables = tuple(jnp.asarray(value) for value in (table_z, table_z.T, table_y, table_y.T))
    count = conv1_w.shape[2]

    if planes == 1:
        sides, variants = [], [[0]]
    elif planes == 2:
        sides, variants = [None], [[0, 1], [0, -1]]
    else:
        sides, variants = [-1, 1], [[0, -1, 1]]
    neighbours = len(sides)
    involved = neighbours + 1
    per_row = -(-(involved * channels) // 8) * 8
    chosen = [tap_selectors(channels, per_row, offsets) for offsets in variants]
    select1, select2 = (jnp.asarray(np.stack(parts)) for parts in zip(*chosen))

    place = jnp.stack([lax.axis_index("space"), plane, member]).astype(jnp.int32)
    spaces = lax.axis_size("space")
    own_image = lax.dynamic_index_in_dim(image, group, 1, keepdims=False)[:, 0].astype(BF)
    own_adjoint = lax.dynamic_index_in_dim(adjoint, group, 1, keepdims=False)[:, 0].astype(BF)
    coils = coil_local * planes
    shared = members if phases % members == 0 and coils % members == 0 else 1
    steps = sorted(range(1, spaces), key=lambda step: min(step, spaces - step))

    def shares(parts):
        local = jnp.concatenate(
            [part.reshape(shared, -1, row_count, length_z) for part in parts], axis=1
        )
        return local, lax.dynamic_index_in_dim(local, member % shared, 0, keepdims=False)

    def sent_blocks(mine):
        blocks = []
        for step in steps:
            if blocks and 2 * step == spaces:
                mine, blocks[0] = lax.optimization_barrier((mine, blocks[0]))
            block = ring(mine, "space", step)
            blocks.append(block)
        return blocks

    def traded(blocks):
        pairs = []
        for block in blocks:
            pairs.append(block)
            for offset in range(1, shared):
                pairs.append(ring(block, "member", -offset))
        return pairs

    def put_together(local, blocks, sizes, dtypes):
        return pl.pallas_call(
            functools.partial(assemble_kernel, shared, spaces, steps),
            out_shape=tuple(
                jax.ShapeDtypeStruct((size, length_y, length_z), dtype)
                for size, dtype in zip(sizes, dtypes)
            ),
            in_specs=[smem] + [vmem] * (1 + len(blocks)),
            out_specs=(vmem,) * len(sizes),
            compiler_params=params,
        )(place, local, *blocks)

    local1, mine1 = shares([own_image, own_adjoint])
    sens, mine1 = lax.optimization_barrier((sens, mine1))
    blocks1 = [ring(mine1, "space", step) for step in steps]
    if planes == 2:
        sent = lax.dynamic_slice(
            sens, (0, group, 1 - plane, 0, 0), (coil_local, 1, 1) + sens.shape[3:]
        )[:, 0, 0]
        received = ring(sent, "coil", 1)
        own = lax.dynamic_slice(
            sens, (0, group, plane, 0, 0), (coil_local, 1, 1) + sens.shape[3:]
        )[:, 0, 0]
    else:
        slab_sens = lax.dynamic_index_in_dim(sens, group, 1, keepdims=False)
        sent = slab_sens
        received = lax.all_to_all(sent, "coil", split_axis=1, concat_axis=0, tiled=True)[:, 0]
        own = received[:0]
    maps = jnp.concatenate([own, received], axis=0)
    maps = maps.reshape(coils, row_count, 2, length_z).transpose(0, 2, 1, 3)
    local2, mine2 = shares([maps.reshape(2 * coils, row_count, length_z)])
    blocks2 = sent_blocks(mine2)
    conv1_w, conv2_w, conv1_b, step_size, mine2 = lax.optimization_barrier(
        (conv1_w, conv2_w, conv1_b, step_size, mine2)
    )
    extra = jnp.concatenate(
        [conv1_b.T, jnp.broadcast_to(step_size.reshape(1, 1), (width, 1))], axis=1
    )
    packed = jnp.concatenate(
        [
            jnp.pad(part, ((0, 0), (0, -(-count // LANES) * LANES - part.shape[1])))
            for part in (conv1_w[0].astype(F32), conv2_w[0].astype(F32), extra)
        ],
        axis=0,
    )
    packed = gathered(gathered(packed, "member"), "group")
    packed = packed.reshape((cascades,) + packed.shape[2:])

    full = jax.ShapeDtypeStruct((channels, length_y, length_z), F32)
    half = jax.ShapeDtypeStruct((channels, length_y, length_z), BF)
    vmem = pl.BlockSpec(memory_space=pltpu.VMEM)
    smem = pl.BlockSpec(memory_space=pltpu.SMEM)
    params = pltpu.CompilerParams(vmem_limit_bytes=32 * 1024 * 1024)
    base, target = put_together(local1, traded(blocks1), [channels, channels], [BF, BF])

    def stacked(offsets, heads, pieces):
        size = local2.shape[1] * len(offsets) + sum(head.shape[0] for head in heads)
        return pl.pallas_call(
            functools.partial(stack_kernel, shared, spaces, steps, offsets, len(heads)),
            out_shape=jax.ShapeDtypeStruct((size, length_y, length_z), F32),
            in_specs=[smem] + [vmem] * (1 + len(heads) + len(pieces)),
            out_specs=vmem,
            compiler_params=params,
        )(place, *heads, local2, *pieces)

    own_maps = maps = stacked((0,), [], blocks2)
    if shared > 1:
        others = tuple(range(1, shared))
        pieces = [ring(block, "member", -offset) for offset in others for block in blocks2]
        maps = stacked(others, [own_maps], pieces)
    order = np.eye(length_y)[slot_order(length_y)[alternate]].astype(BF)
    column = slot_order(length_z)
    columns = np.stack([column // 30, column % 30]).astype(np.int32)
    sampled = pl.pallas_call(
        mask_kernel,
        out_shape=jax.ShapeDtypeStruct((phases, length_y, length_z), F32),
        in_specs=[vmem] * 3,
        out_specs=vmem,
        compiler_params=params,
    )(mask_bits, jnp.asarray(columns), jnp.asarray(order))
    weight1, weight2 = pl.pallas_call(
        functools.partial(prepare_kernel, width, per_row),
        out_shape=(
            jax.ShapeDtypeStruct((cascades, ROWS * width, select1.shape[2]), BF),
            jax.ShapeDtypeStruct((cascades, select2.shape[2], (ROWS + 2) * width), BF),
        ),
        in_specs=[smem] + [vmem] * 3,
        out_specs=(vmem,) * 2,
        compiler_params=params,
    )(place, packed, select1, select2)
    rows_shape = jax.ShapeDtypeStruct((channels, row_count, length_z), F32)

    margin = 2 * ROWS
    windowed = row_count + 2 * margin
    if row_count % margin or windowed % (UNROLL * ROWS) or windowed >= length_y:
        windowed = length_y

    def consistency(cascade, base, parts, maps, first_coil=0, carried=None, final=True):
        height = windowed if cascade == cascades - 1 else length_y
        shape = (channels, height, length_z)
        operands = [base, *parts] + ([] if carried is None else [carried])
        operands += [maps, sampled, *tables] + ([target, packed] if final else [])
        sums = jax.ShapeDtypeStruct(shape, F32)
        return pl.pallas_call(
            functools.partial(
                consistency_kernel,
                phases,
                width,
                cascade,
                len(parts),
                first_coil,
                carried is not None,
                final,
            ),
            out_shape=(rows_shape, sums, jax.ShapeDtypeStruct(shape, BF)) if final else sums,
            in_specs=[smem] + [vmem] * len(operands),
            out_specs=(vmem,) * 3 if final else vmem,
            scratch_shapes=([pltpu.VMEM(shape, F32)] if final else [])
            + [pltpu.VMEM((channels, length_y, length_z), F32)] * 2
            + [pltpu.VMEM((phases, length_y, 2 * length_z), dtype) for dtype in (BF, F32, BF)]
            + [pltpu.VMEM((phases, 2 * height, length_z), BF)],
            compiler_params=params,
        )(place, *operands)

    def refine(cascade, value, others, updated):
        rows = value.shape[1]
        padded = rows + 2 * ROWS
        shape = (channels, rows if rows == length_y else row_count, length_z)
        return pl.pallas_call(
            functools.partial(refine_kernel, neighbours, width, cascade, length_y),
            out_shape=(jax.ShapeDtypeStruct(shape, F32),)
            + (jax.ShapeDtypeStruct(shape, BF),) * neighbours,
            in_specs=[smem] + [vmem] * (4 + neighbours),
            out_specs=(vmem,) * (1 + neighbours),
            scratch_shapes=[
                pltpu.VMEM((length_z // LANES, padded * per_row, LANES), F32),
                pltpu.VMEM((padded * 3 * per_row, length_z), BF),
                pltpu.VMEM(((rows + 2) * width, length_z), BF),
            ],
            compiler_params=params,
        )(place, value, *others, updated, weight1, weight2)

    def exchanged(values):
        received = []
        for value, side in zip(values, sides):
            if side is None:
                pairs = [(0, 1), (1, 0)]
            else:
                pairs = [(i, i - side) for i in range(planes) if 0 <= i - side < planes]
            received.append(lax.ppermute(value, "coil", pairs))
        return received

    row_start = lax.axis_index("space") * row_count

    def own_rows(value):
        if value.shape[1] == row_count:
            return value
        return lax.dynamic_slice_in_dim(value, row_start, row_count, 1)

    results = []
    parts = []
    for cascade in range(cascades):
        if cascade == 0 and cascades > 1 and shared > 1:
            carried = consistency(0, base, [], own_maps, final=False)
            first_coil = own_maps.shape[0] // 2
            rows, updated, value = consistency(0, base, [], maps, first_coil, carried)
        else:
            rows, updated, value = consistency(cascade, base, parts, maps)
        if cascade:
            results.append(rows)
        others = exchanged([value] * neighbours)
        base, *sends = refine(cascade, value, others, updated)
        turned = sends[::-1] if neighbours == 2 else sends
        parts = exchanged(turned)[::-1] if neighbours == 2 else exchanged(turned)
    last = own_rows(base)
    for part in parts:
        last = last + own_rows(part).astype(F32)
    results.append(last)

    def result_of(wanted):
        chosen = results[0]
        for cascade in range(1, cascades):
            chosen = jnp.where(wanted == cascade, results[cascade], chosen)
        return chosen

    output = jnp.zeros((channels, slab_count, row_count, length_z), F32)
    for step in range(groups):
        if step == 0:
            chosen = result_of(section)
        else:
            target_group = (group - step) % groups
            chosen = result_of(target_group * members + member).astype(BF)
            chosen = lax.ppermute(
                chosen, "group", [(i, (i - step) % groups) for i in range(groups)]
            ).astype(F32)
        output = lax.dynamic_update_slice_in_dim(
            output, chosen[:, None], (group + step) % groups, 1
        )
    return output[None, :, :, None]


def solution(mesh):
    sections, coils, spaces = mesh.devices.shape
    def run(image, *args):
        groups = image.shape[1]
        fine = Mesh(
            mesh.devices.reshape(groups, sections // groups, coils, spaces),
            ("group", "member", "coil", "space"),
        )
        section = ("group", "member")
        in_specs = (
            P(None, None, "coil", "space", None),
            P("coil", None, None, "space", None),
            P(None, None, "coil", "space", None),
            P(),
            P(section),
            P(section, None, None),
            P(section, None),
            P(section, None, None),
        )
        out_specs = P(section, None, None, "coil", "space", None)
        return jax.shard_map(
            per_device, mesh=fine, in_specs=in_specs, out_specs=out_specs, check_vma=False
        )(image, *args)

    return run
```
